256 devices in a mesh: tm: 8 (over y, core), space: 32 (over x, z).
Axes of the slice: x: 4, y: 4, z: 8, core: 2. Of those that a mesh axis runs over, the one named last changes fastest.
Arguments:
- state_guess: float32 [16, 64, 96, 128], P('tm', 'space'), may hold values from -6 to 6
- adjoint_guess: float32 [16, 64, 96, 128], P('tm', 'space'), may hold values from -6 to 6
- target: float32 [16, 64, 96, 128], P('tm', 'space'), may hold values from -6 to 6
- initial_state: float32 [64, 96, 128], P('space'), may hold values from -6 to 6
- diffusivity: float32 [64, 96, 128], P('space'), may hold values from 0.3 to 3
Outputs:
- state_field: float32 [16, 64, 96, 128], P('tm', 'space')
- adjoint_field: float32 [16, 64, 96, 128], P('tm', 'space')
The draws below stay inside these ranges and needn't reach their ends.
All inputs are finite; a program needn't handle non-finite values.
Results may differ from the reference program's by a relative error of at most 0.00025.
Values sent between devices are 32-bit elements; how exact they have to be, the bound alone decides.
No kernel may reach another device: no remote copies, remote signals or barrier semaphores. Data moves between devices by JAX's collectives and lax.ppermute only.
A program may use at most 64 MiB of HBM per device.

```python
import math
import jax
import jax.numpy as jnp

NY = 96
NZ = 128
SWEEPS = 4
OUTER = 2
STEPS = 16
NX = 64


def block_levels(own_key, dims, shards, low, largest):
    gain = 1.0
    for axis_at, blocks in shards:
        heights = jax.random.uniform(jax.random.fold_in(jax.random.fold_in(own_key, 6), axis_at), (blocks,), jnp.float32, low / len(shards), largest / len(shards))
        gain = gain * jnp.repeat(jnp.exp(heights), dims[axis_at] // blocks).reshape((-1,) + (1,) * (len(dims) - 1 - axis_at))
    return gain


def gaussian(stream_key, shape, width, bound, cuts=(), held_as=jnp.bfloat16):
    gain = block_levels(stream_key, shape, cuts, -0.22, 0.18) if cuts else 1.0
    entries = jax.random.normal(stream_key, shape, jnp.float32) * width * gain
    return jnp.minimum(jnp.maximum(entries, -bound), bound).astype(held_as)


def setup_inputs(seed: int = 0) -> dict:
    arg_keys = jax.random.split(jax.random.key(seed), 6)
    return {
        "state_guess": gaussian(arg_keys[0], (STEPS, NX, NY, NZ), 1.0, 6.0, ((0, 8), (1, 32)), jnp.float32),
        "adjoint_guess": gaussian(arg_keys[1], (STEPS, NX, NY, NZ), 1.0, 6.0, ((0, 8), (1, 32)), jnp.float32),
        "target": gaussian(arg_keys[2], (STEPS, NX, NY, NZ), 1.0, 6.0, ((0, 8), (1, 32)), jnp.float32),
        "initial_state": gaussian(arg_keys[3], (NX, NY, NZ), 1.0, 6.0, ((0, 32),), jnp.float32),
        "diffusivity": jnp.clip(jnp.exp(math.log(3.0) - 2.3025851 * jax.random.uniform(arg_keys[4], (NX, NY, NZ), jnp.float32) ** block_levels(arg_keys[4], (NX, NY, NZ), ((0, 32),), -0.2, 0.2)), 0.3, 3.0),
    }


step_size = 0.25
control_cost = 0.05


def rim_slices(padded):
    return [padded[..., 2:, 1:-1, 1:-1], padded[..., :-2, 1:-1, 1:-1],
            padded[..., 1:-1, 2:, 1:-1], padded[..., 1:-1, :-2, 1:-1],
            padded[..., 1:-1, 1:-1, 2:], padded[..., 1:-1, 1:-1, :-2]]


def pad_cells(values):
    widths = [(0, 0)] * (values.ndim - 3) + [(1, 1)] * 3
    return jnp.pad(values, widths)


def face_weights(diffusivity):
    return [0.5 * (diffusivity + beside) for beside in rim_slices(pad_cells(diffusivity))]


def neighbour_sum(values, weights):
    pieces = rim_slices(pad_cells(values))
    summed = weights[0] * pieces[0]
    for weight_one, piece_one in zip(weights[1:], pieces[1:]):
        summed = summed + weight_one * piece_one
    return summed


def apply_block(right_side, shift_real, shift_imag, determinant):
    state_real, state_imag, adjoint_real, adjoint_imag = right_side
    coupling = step_size / control_cost
    new_state_real = (shift_real * state_real + shift_imag * state_imag - coupling * adjoint_real) / determinant
    new_state_imag = (shift_real * state_imag - shift_imag * state_real - coupling * adjoint_imag) / determinant
    new_adjoint_real = (step_size * state_real + shift_real * adjoint_real - shift_imag * adjoint_imag) / determinant
    new_adjoint_imag = (step_size * state_imag + shift_real * adjoint_imag + shift_imag * adjoint_real) / determinant
    return (new_state_real, new_state_imag, new_adjoint_real, new_adjoint_imag)


def reference(state_guess, adjoint_guess, target, initial_state, diffusivity):
    weights = face_weights(diffusivity)
    diagonal = weights[0] + weights[1] + weights[2] + weights[3] + weights[4] + weights[5]
    angles = 2.0 * math.pi * jnp.arange(STEPS, dtype=jnp.float32) / STEPS
    shift_real = (1.0 - jnp.cos(angles))[:, None, None, None] + step_size * diagonal
    shift_imag = jnp.sin(angles)[:, None, None, None]
    determinant = shift_real * shift_real + shift_imag * shift_imag + step_size * step_size / control_cost
    zero_step = jnp.zeros_like(initial_state)[None]
    source = jnp.concatenate([initial_state[None], jnp.zeros_like(state_guess[1:])], 0)
    state_now = state_guess
    adjoint_now = adjoint_guess
    for outer_step in range(OUTER):
        before = jnp.concatenate([zero_step, state_now[:-1]], 0)
        later_adjoint = jnp.concatenate([adjoint_now[1:], zero_step], 0)
        diffuse_state = diagonal * state_now - neighbour_sum(state_now, weights)
        diffuse_adjoint = diagonal * adjoint_now - neighbour_sum(adjoint_now, weights)
        res_state = source - (state_now - before + step_size * diffuse_state + (step_size / control_cost) * adjoint_now)
        res_adjoint = -step_size * target - (adjoint_now - later_adjoint + step_size * diffuse_adjoint - step_size * state_now)
        spec_state = jnp.fft.fft(res_state, axis=0)
        spec_adjoint = jnp.fft.fft(res_adjoint, axis=0)
        right_side = (jnp.real(spec_state), jnp.imag(spec_state), jnp.real(spec_adjoint), jnp.imag(spec_adjoint))
        iterate = apply_block(right_side, shift_real, shift_imag, determinant)
        for sweep_index in range(1, SWEEPS):
            pushed = tuple(side_part + step_size * neighbour_sum(guess_part, weights)
                           for side_part, guess_part in zip(right_side, iterate))
            iterate = apply_block(pushed, shift_real, shift_imag, determinant)
        state_now = state_now + jnp.real(jnp.fft.ifft(iterate[0] + 1j * iterate[1], axis=0))
        adjoint_now = adjoint_now + jnp.real(jnp.fft.ifft(iterate[2] + 1j * iterate[3], axis=0))
    return state_now, adjoint_now
```

```python
import math

import jax
import jax.numpy as jnp
import numpy as np
from jax import lax
from jax.experimental import pallas as pl
from jax.experimental.pallas import tpu as pltpu
from jax.sharding import PartitionSpec as P

TAU = 0.25
COUPLING = 5.0
DET_SHIFT = 1.25
OUTER = 2

OWN = 12
HALO = 4
WIN = OWN + 2 * HALO


def transform_matrices():
    modes = np.arange(8)[:, None]
    steps = np.concatenate([np.arange(0, 16, 2), np.arange(1, 16, 2)])[None, :]
    angle = 2.0 * np.pi * ((modes * steps) % 16) / 16.0
    real, imag = np.cos(angle), -np.sin(angle)
    imag[0] = np.where(steps[0] % 2 == 0, 1.0, -1.0)
    forward = np.concatenate([real, imag], 0)
    back = forward.T.copy() / 8.0
    back[:, 0] /= 2.0
    back[:, 8] /= 2.0
    eye = np.eye(8)
    return np.kron(eye, forward).astype(np.float32), np.kron(eye, back).astype(np.float32)


def mode_constants():
    theta = 2.0 * np.pi * np.arange(8) / 16.0
    shift_a = 1.0 - np.cos(theta)
    shift_b = shift_a.copy()
    shift_b[0] = 2.0
    lag = np.sin(theta)
    out = np.stack([shift_a, shift_b, lag])[:, :, None] * np.ones((1, 1, 128))
    return out.astype(np.float32)


def whole(*shape):
    return jax.ShapeDtypeStruct(shape, jnp.float32)


def call(body, name, outs, n_in, scratch=(), scalars=1):
    vmem = pl.BlockSpec(memory_space=pltpu.VMEM)
    smem = pl.BlockSpec(memory_space=pltpu.SMEM)
    return pl.pallas_call(
        body,
        name=name,
        out_shape=outs,
        in_specs=[smem] * scalars + [vmem] * n_in,
        out_specs=[vmem] * len(outs),
        scratch_shapes=list(scratch),
        compiler_params=pltpu.CompilerParams(vmem_limit_bytes=48 * 1024 * 1024),
    )


def pack_body(pos, state, adjoint, target, *rest):
    outs, stage = rest[:8], rest[8]
    t = pos[0]
    flip = pos[1]
    for f, ref in enumerate((state, adjoint, target)):
        for n in range(2):
            for x in range(2):
                base = ((f * 2 + n) * 2 + x) * WIN
                for d in range(8):
                    low = OWN * d - HALO
                    first, last = max(low, 0), min(low + WIN, 96)
                    stage[d, base + first - low : base + last - low, :] = ref[n, x ^ flip, first:last, :]
                    if first > low:
                        stage[d, base : base + first - low, :] = jnp.zeros((first - low, 128), jnp.float32)
                    if last < low + WIN:
                        stage[d, base + last - low : base + WIN, :] = jnp.zeros((low + WIN - last, 128), jnp.float32)
    for k in range(8):
        outs[k][...] = stage[t ^ k]


def spread_body(pos, *rest):
    pieces, (own, wish, near, far), stage = rest[:8], rest[8:12], rest[12]
    t = pos[0]
    rows = 12 * WIN
    for k in range(8):
        stage[pl.ds(pl.multiple_of((t ^ k) * rows, 8), rows), :] = pieces[k][...]
    for x in range(2):
        for j in range(WIN):
            for f in range(3):
                for n in range(2):
                    v = stage[pl.ds(((f * 2 + n) * 2 + x) * WIN + j, 8, stride=rows), :]
                    if f < 2:
                        c = f * 2 + n
                        own[x, j, c] = v
                        put_field(near, far, x, j, c, v)
                    else:
                        if 1 <= j <= 18:
                            wish[x, j - 1, n] = v
                        if 2 <= j <= 17:
                            out = far if x == 1 else near
                            out[136 + (j - 2) * 2 + n] = v


def put_field(near, far, x, j, c, v):
    first, second = (near, far) if x == 0 else (far, near)
    if 1 <= j <= 18:
        first[(j - 1) * 4 + c] = v
    if 2 <= j <= 17:
        second[72 + (j - 2) * 4 + c] = v


def region(p, j):
    if p == 2 or p == 3:
        return (p - 2) * 18 + j - 1
    return (36 if p == 1 else 52) + j - 2


def spread_sum(v, around, w):
    px, mx, py, my = around
    up = pltpu.roll(v, 127, 1)
    down = pltpu.roll(v, 1, 1)
    return ((w[0] * px + w[1] * mx) + (w[2] * py + w[3] * my)) + (w[4] * up + w[5] * down)


def row_weights(weights, p, j, count):
    tile = weights[(p - 1) * WIN + j]
    return [jnp.broadcast_to(tile[k : k + 1, :], (8, 128)) for k in range(count)]


def solve(right, td, inv, consts):
    ur, ui, pr, pi = right
    shift_a, shift_b, lag = consts
    inv_a, inv_b = inv
    a = shift_a + td
    b = shift_b + td
    return (
        (a * ur + lag * ui - COUPLING * pr) * inv_a,
        (b * ui - lag * ur - COUPLING * pi) * inv_b,
        (TAU * ur + a * pr - lag * pi) * inv_a,
        (TAU * ui + b * pi + lag * pr) * inv_b,
    )


def inverse_body(weights, consts, inv):
    ca, cb, lag = consts[0], consts[1], consts[2]
    base = lag * lag + DET_SHIFT
    for p, lo, hi in ((2, 1, 19), (3, 1, 19), (1, 2, 18), (4, 2, 18)):
        def row(j, carry, p=p):
            tile = weights[(p - 1) * WIN + j]
            td = jnp.broadcast_to(tile[6:7, :], (8, 128))
            a = ca + td
            b = cb + td
            at = region(p, j)
            inv[at, 0] = 1.0 / (a * a + base)
            inv[at, 1] = 1.0 / (b * b + base)
            return carry
        lax.fori_loop(lo, hi, row, 0)


def residual_body(own, wish, near, far, tnear, tfar, weights, consts, inv, forward, rhs, it, out_near, out_far, res, zed):
    def field(p, j, c):
        if p == 2 or p == 3:
            return own[p - 2, j, c]
        side = near if p < 2 else far
        if p == 1 or p == 4:
            return side[(j - 1) * 4 + c]
        return side[72 + (j - 2) * 4 + c]

    def wanted(p, j, n):
        if p == 2 or p == 3:
            return wish[p - 2, j - 1, n]
        return (tnear if p == 1 else tfar)[136 + (j - 2) * 2 + n]

    sub = lax.broadcasted_iota(jnp.int32, (8, 128), 0)
    first = jnp.where(sub == 0, 1.0, 0.0)
    not_first = jnp.where(sub == 0, 0.0, 1.0)
    not_last = jnp.where(sub == 7, 0.0, 1.0)
    for p, lo, hi in ((2, 1, 19), (3, 1, 19), (1, 2, 18), (4, 2, 18)):
        def row(j, carry, p=p):
            w = row_weights(weights, p, j, 8)
            td = w[6]
            v = [field(p, j, c) for c in range(4)]
            n = [
                spread_sum(v[c], (field(p + 1, j, c), field(p - 1, j, c), field(p, j + 1, c), field(p, j - 1, c)), w)
                for c in range(4)
            ]
            at = region(p, j)
            ue, uo, pe, po = v
            before = pltpu.roll(uo, 1, 0) * not_first
            after = pltpu.roll(pe, 7, 0) * not_last
            res[at, 0] = w[7] * first - (ue - before + (td * ue - n[0]) + COUPLING * pe)
            res[at, 1] = -(uo - ue + (td * uo - n[1]) + COUPLING * po)
            res[at, 2] = -TAU * wanted(p, j, 0) - (pe - po + (td * pe - n[2]) - TAU * ue)
            res[at, 3] = -TAU * wanted(p, j, 1) - (po - after + (td * po - n[3]) - TAU * uo)
            return carry
        lax.fori_loop(lo, hi, row, 0)

    def group(g, carry):
        block = res[pl.ds(g * 4, 4)].reshape(128, 128)
        done = jnp.dot(forward[...], block, precision=lax.Precision.HIGHEST, preferred_element_type=jnp.float32)
        rhs[pl.ds(g * 4, 4)] = done.reshape(4, 4, 8, 128)
        return carry
    lax.fori_loop(0, 17, group, 0)

    cs = (consts[0], consts[1], consts[2])
    for p, lo, hi in ((2, 1, 19), (3, 1, 19), (1, 2, 18), (4, 2, 18)):
        def row(j, carry, p=p):
            td = row_weights(weights, p, j, 8)[6]
            at = region(p, j)
            z = solve([rhs[at, c] for c in range(4)], td, (inv[at, 0], inv[at, 1]), cs)
            for c in range(4):
                zed[at, c] = z[c]
            return carry
        lax.fori_loop(lo, hi, row, 0)

    for p in (2, 3):
        def row(j, carry, p=p):
            w = row_weights(weights, p, j, 8)
            at = region(p, j)
            pushed = []
            for c in range(4):
                around = (zed[region(p + 1, j), c], zed[region(p - 1, j), c], zed[at + 1, c], zed[at - 1, c])
                pushed.append(rhs[at, c] + spread_sum(zed[at, c], around, w))
            z = solve(pushed, w[6], (inv[at, 0], inv[at, 1]), cs)
            for c in range(4):
                it[p - 2, j - 2, c] = z[c]
            return carry
        lax.fori_loop(2, 18, row, 0)
    out_near[0:14] = it[0, 1:15]
    out_near[14:26] = it[1, 2:14]
    out_far[0:14] = it[1, 1:15]
    out_far[14:26] = it[0, 2:14]


def sweep_body(it, near, far, rhs, weights, consts, inv, back, zed, fin):
    def guess(p, j, c):
        if p == 2 or p == 3:
            return it[p - 2, j - 2, c]
        side = near if p < 2 else far
        if p == 1 or p == 4:
            return side[j - 3, c]
        return side[14 + j - 4, c]

    def at2(p, j):
        if p == 2 or p == 3:
            return (p - 2) * 14 + j - 3
        return (28 if p == 1 else 40) + j - 4

    cs = (consts[0], consts[1], consts[2])
    for p, lo, hi in ((2, 3, 17), (3, 3, 17), (1, 4, 16), (4, 4, 16)):
        def row(j, carry, p=p):
            w = row_weights(weights, p, j, 8)
            at = region(p, j)
            pushed = []
            for c in range(4):
                around = (guess(p + 1, j, c), guess(p - 1, j, c), guess(p, j + 1, c), guess(p, j - 1, c))
                pushed.append(rhs[at, c] + spread_sum(guess(p, j, c), around, w))
            z = solve(pushed, w[6], (inv[at, 0], inv[at, 1]), cs)
            for c in range(4):
                zed[at2(p, j), c] = z[c]
            return carry
        lax.fori_loop(lo, hi, row, 0)
    for p in (2, 3):
        def row(j, carry, p=p):
            w = row_weights(weights, p, j, 8)
            at = region(p, j)
            here = at2(p, j)
            pushed = []
            for c in range(4):
                around = (zed[at2(p + 1, j), c], zed[at2(p - 1, j), c], zed[here + 1, c], zed[here - 1, c])
                pushed.append(rhs[at, c] + spread_sum(zed[here, c], around, w))
            z = solve(pushed, w[6], (inv[at, 0], inv[at, 1]), cs)
            for c in range(4):
                fin[(p - 2) * OWN + j - 4, c] = z[c]
            return carry
        lax.fori_loop(4, 16, row, 0)

    def group(g, carry):
        block = fin[pl.ds(g * 4, 4)].reshape(128, 128)
        done = jnp.dot(back[...], block, precision=lax.Precision.HIGHEST, preferred_element_type=jnp.float32)
        fin[pl.ds(g * 4, 4)] = done.reshape(4, 4, 8, 128)
        return carry
    lax.fori_loop(0, 6, group, 0)


def middle_body(pos, it, near, far, rhs, weights, consts, inv, back, own, new, send0, send1, zed, fin):
    sweep_body(it, near, far, rhs, weights, consts, inv, back, zed, fin)
    odd = pos[0] & 1
    for x in range(2):
        for j in range(OWN):
            for c in range(4):
                new[x, j, c] = own[x, j + HALO, c] + fin[x * OWN + j, c]
    top = pl.multiple_of(8 * (1 - odd), 4)
    bottom = 8 * odd
    for x in range(2):
        for j in range(HALO):
            send0[x, j] = new[x, top + j]
            send1[x, j] = new[x, bottom + j]


def widen_body(pos, new, got0, got1, own, near, far):
    odd = pos[0] & 1
    for x in range(2):
        own[x, HALO : HALO + OWN] = new[x]
        own[x, pl.ds(16 * (1 - odd), HALO)] = got0[x]
        own[x, pl.ds(16 * odd, HALO)] = got1[x]
    for x in range(2):
        first, second = (near, far) if x == 0 else (far, near)
        first[0:72] = own[x, 1:19].reshape(72, 8, 128)
        second[72:136] = own[x, 2:18].reshape(64, 8, 128)


def last_body(pos, it, near, far, rhs, weights, consts, inv, back, own, *rest):
    outs, (zed, fin, stage) = rest[:8], rest[8:]
    sweep_body(it, near, far, rhs, weights, consts, inv, back, zed, fin)
    t = pos[0]
    for x in range(2):
        for j in range(OWN):
            for c in range(4):
                stage[pl.ds((c * 2 + x) * OWN + j, 8, stride=8 * OWN), :] = own[x, j + HALO, c] + fin[x * OWN + j, c]
    for k in range(8):
        outs[k][...] = stage[pl.ds(pl.multiple_of((t ^ k) * 8 * OWN, 8), 8 * OWN), :]


def unpack_body(pos, *rest):
    pieces, (state, adjoint), stage = rest[:8], rest[8:10], rest[10]
    t = pos[0]
    flip = pos[1]
    for k in range(8):
        stage[t ^ k] = pieces[k][...]
    for f, ref in enumerate((state, adjoint)):
        for n in range(2):
            for x in range(2):
                base = ((f * 2 + n) * 2 + x) * OWN
                for d in range(8):
                    ref[n, x ^ flip, OWN * d : OWN * (d + 1), :] = stage[d, base : base + OWN, :]


def exchange(pieces):
    count = lax.axis_size("tm")
    return [pieces[0]] + [
        lax.ppermute(pieces[k], "tm", [(i, i ^ k) for i in range(count)]) for k in range(1, count)
    ]


def swap(block, axis, start):
    count = lax.axis_size(axis)
    route = []
    for i in range(start, count - 1, 2):
        route += [(i, i + 1), (i + 1, i)]
    return lax.ppermute(block, axis, route)


def face_weights(kappa, first_state, t, s, flip):
    mid = kappa[1:5, 1:-1]
    lane = lax.broadcasted_iota(jnp.int32, mid.shape, 2)
    row = lax.broadcasted_iota(jnp.int32, mid.shape, 1) + OWN * t - HALO
    local = lax.broadcasted_iota(jnp.int32, mid.shape, 0)
    plane = jnp.where(flip == 1, 2 * s + 2 - local, 2 * s - 1 + local)
    ahead = jnp.where(flip == 1, -1, 1)
    half = 0.5 * TAU
    xp = half * (mid + kappa[2:6, 1:-1])
    xm = half * (mid + kappa[0:4, 1:-1])
    yp = half * (mid + kappa[1:5, 2:])
    ym = half * (mid + kappa[1:5, :-2])
    zp = half * (mid + jnp.pad(mid[..., 1:], ((0, 0), (0, 0), (0, 1))))
    zm = half * (mid + jnp.pad(mid[..., :-1], ((0, 0), (0, 0), (1, 0))))
    td = xp + xm + yp + ym + zp + zm
    inside = lambda q, n: (q >= 0) & (q < n)
    here = inside(plane, 64) & inside(row, 96)
    keep = lambda w, ok: jnp.where(here & ok, w, 0.0)
    kinds = [
        keep(xp, inside(plane + ahead, 64)),
        keep(xm, inside(plane - ahead, 64)),
        keep(yp, row + 1 < 96),
        keep(ym, row > 0),
        keep(zp, lane < 127),
        keep(zm, lane > 0),
        td,
        first_state,
    ]
    return jnp.stack(kinds, 2).reshape(4 * WIN, 8, 128)


def on_device(state_guess, adjoint_guess, target, initial_state, diffusivity):
    t = lax.axis_index("tm").astype(jnp.int32)
    s = lax.axis_index("space").astype(jnp.int32)
    flip = s & 1
    pos = jnp.stack([t, flip])
    forward, back = (jnp.asarray(m) for m in transform_matrices())
    consts = jnp.asarray(mode_constants())

    pieces = call(
        pack_body, "pack", [whole(12 * WIN, 128)] * 8, 3, [pltpu.VMEM((8, 12 * WIN, 128), jnp.float32)]
    )(pos, state_guess, adjoint_guess, target)

    both = jnp.concatenate([diffusivity, initial_state], 0)
    both = jnp.where(flip == 1, both[jnp.array([1, 0, 3, 2])], both)
    both = jnp.pad(both, ((0, 0), (HALO + 2, HALO + 2), (0, 0)))
    both = lax.dynamic_slice_in_dim(both, OWN * t, 24, 1)
    far_c = swap(jnp.stack([both[1], both[0], both[3]]), "space", 0)
    near_c = swap(jnp.stack([both[0], both[1], both[2]]), "space", 1)

    got = exchange(pieces)

    kappa = jnp.stack([near_c[1], near_c[0], both[0], both[1], far_c[0], far_c[1]])[:, 1:23]
    begin = jnp.stack([near_c[2], both[2], both[3], far_c[2]])[:, 2:22]
    weights = face_weights(kappa, begin, t, s, flip)
    inv = call(inverse_body, "inverse", [whole(68, 2, 8, 128)], 2, scalars=0)(weights, consts)[0]

    own, wish, near, far = call(
        spread_body,
        "spread",
        [whole(2, WIN, 4, 8, 128), whole(2, 18, 2, 8, 128), whole(168, 8, 128), whole(168, 8, 128)],
        8,
        [pltpu.VMEM((8 * 12 * WIN, 128), jnp.float32)],
    )(pos, *got)

    sweep_scratch = [pltpu.VMEM((52, 4, 8, 128), jnp.float32), pltpu.VMEM((24, 4, 8, 128), jnp.float32)]
    for outer in range(OUTER):
        far_f = swap(far, "space", 0)
        near_f = swap(near, "space", 1)
        if outer == 0:
            wish_near, wish_far = near_f, far_f
        rhs, it, near_z, far_z = call(
            residual_body,
            "residual",
            [whole(68, 4, 8, 128), whole(2, 16, 4, 8, 128), whole(26, 4, 8, 128), whole(26, 4, 8, 128)],
            10,
            [pltpu.VMEM((68, 4, 8, 128), jnp.float32)] * 2,
            scalars=0,
        )(own, wish, near_f, far_f, wish_near, wish_far, weights, consts, inv, forward)
        far_z = swap(far_z, "space", 0)
        near_z = swap(near_z, "space", 1)
        if outer < OUTER - 1:
            new, send0, send1 = call(
                middle_body,
                "middle",
                [whole(2, OWN, 4, 8, 128), whole(2, HALO, 4, 8, 128), whole(2, HALO, 4, 8, 128)],
                9,
                sweep_scratch,
            )(pos, it, near_z, far_z, rhs, weights, consts, inv, back, own)
            got0 = swap(send0, "tm", 0)
            got1 = swap(send1, "tm", 1)
            own, near, far = call(
                widen_body, "widen", [whole(2, WIN, 4, 8, 128), whole(136, 8, 128), whole(136, 8, 128)], 3
            )(pos, new, got0, got1)
    pieces = call(
        last_body,
        "last",
        [whole(8 * OWN, 128)] * 8,
        9,
        sweep_scratch + [pltpu.VMEM((64 * OWN, 128), jnp.float32)],
    )(pos, it, near_z, far_z, rhs, weights, consts, inv, back, own)
    got = exchange(pieces)
    return tuple(
        call(
            unpack_body,
            "unpack",
            [whole(2, 2, 96, 128)] * 2,
            8,
            [pltpu.VMEM((8, 8 * OWN, 128), jnp.float32)],
        )(pos, *got)
    )


def solution(mesh):
    in_specs = (
        P("tm", "space", None, None),
        P("tm", "space", None, None),
        P("tm", "space", None, None),
        P("space", None, None),
        P("space", None, None),
    )
    out_specs = (P("tm", "space", None, None), P("tm", "space", None, None))
    return jax.shard_map(
        on_device, mesh=mesh, in_specs=in_specs, out_specs=out_specs, check_vma=False
    )
```

```python
import math

import jax
import jax.numpy as jnp
import numpy as np
from jax import lax
from jax.experimental import pallas as pl
from jax.experimental.pallas import tpu as pltpu
from jax.sharding import PartitionSpec as P

TAU = 0.25
COUPLING = 5.0
DET_SHIFT = 1.25
OUTER = 2

OWN = 12
HALO = 4
WIN = OWN + 2 * HALO
TALL = 24


def transform_matrices():
    modes = np.arange(8)[:, None]
    steps = np.concatenate([np.arange(0, 16, 2), np.arange(1, 16, 2)])[None, :]
    angle = 2.0 * np.pi * ((modes * steps) % 16) / 16.0
    real, imag = np.cos(angle), -np.sin(angle)
    imag[0] = np.where(steps[0] % 2 == 0, 1.0, -1.0)
    forward = np.concatenate([real, imag], 0)
    back = forward.T.copy() / 8.0
    back[:, 0] /= 2.0
    back[:, 8] /= 2.0
    eye = np.eye(8)
    return np.kron(eye, forward).astype(np.float32), np.kron(eye, back).astype(np.float32)


def mode_constants():
    theta = 2.0 * np.pi * np.arange(8) / 16.0
    shift_a = 1.0 - np.cos(theta)
    shift_b = shift_a.copy()
    shift_b[0] = 2.0
    lag = np.sin(theta)
    out = np.stack([shift_a, shift_b, lag])[:, :, None] * np.ones((1, 1, 128))
    return out.astype(np.float32)


def whole(*shape):
    return jax.ShapeDtypeStruct(shape, jnp.float32)


def call(body, name, outs, n_in, scratch=(), scalars=1):
    vmem = pl.BlockSpec(memory_space=pltpu.VMEM)
    smem = pl.BlockSpec(memory_space=pltpu.SMEM)
    return pl.pallas_call(
        body,
        name=name,
        out_shape=outs,
        in_specs=[smem] * scalars + [vmem] * n_in,
        out_specs=[vmem] * len(outs),
        scratch_shapes=list(scratch),
        compiler_params=pltpu.CompilerParams(vmem_limit_bytes=16 * 1024 * 1024),
    )


def rows(lo, hi, body):
    lax.fori_loop(lo, hi, body, 0, unroll=True)


def pack_body(pos, state, adjoint, target, kappa, begin, *rest):
    outs, (near, far, here, stage) = rest[:8], rest[8:]
    t = pos[0]
    flip = pos[1]
    for f, ref in enumerate((state, adjoint, target)):
        for n in range(2):
            for x in range(2):
                base = ((f * 2 + n) * 2 + x) * WIN
                for d in range(8):
                    low = OWN * d - HALO
                    first, last = max(low, 0), min(low + WIN, 96)
                    stage[d, base + first - low : base + last - low, :] = ref[n, x ^ flip, first:last, :]
                    if first > low:
                        stage[d, base : base + first - low, :] = jnp.zeros((first - low, 128), jnp.float32)
                    if last < low + WIN:
                        stage[d, base + last - low : base + WIN, :] = jnp.zeros((low + WIN - last, 128), jnp.float32)
    for k in range(8):
        outs[k][...] = stage[t ^ k]
    for d in range(8):
        @pl.when(t == d)
        def window(d=d):
            low = OWN * d - HALO
            first, last = max(low, 0), min(low + TALL, 96)
            parts = []
            for ref, x in ((kappa, 0), (kappa, 1), (begin, 0), (begin, 1)):
                v = ref[x ^ flip, first:last, :]
                if first > low:
                    v = jnp.concatenate([jnp.zeros((first - low, 128), jnp.float32), v], 0)
                if last < low + TALL:
                    v = jnp.concatenate([v, jnp.zeros((low + TALL - last, 128), jnp.float32)], 0)
                parts.append(v)
            for i, v in enumerate(parts):
                here[i] = v
            for i, q in enumerate((0, 1, 2)):
                near[i] = parts[q]
            for i, q in enumerate((1, 0, 3)):
                far[i] = parts[q]


def coefficient_body(pos, here, near, far, consts, weights, inv):
    t, flip, s = pos[0], pos[1], pos[2]
    kappa = [near[1], near[0], here[0], here[1], far[0], far[1]]
    begin = [near[2], here[2], here[3], far[2]]
    lane = lax.broadcasted_iota(jnp.int32, (TALL, 128), 1)
    row = lax.broadcasted_iota(jnp.int32, (TALL, 128), 0) + (OWN * t - HALO)
    half = 0.5 * TAU
    for p in range(1, 5):
        plane = jnp.where(flip == 1, 2 * s + 3 - p, 2 * s - 2 + p)
        ahead = jnp.where(flip == 1, plane - 1, plane + 1)
        behind = jnp.where(flip == 1, plane + 1, plane - 1)
        real = jnp.where((plane >= 0) & (plane < 64), half, 0.0)
        to_ahead = jnp.where((ahead >= 0) & (ahead < 64), real, 0.0)
        to_behind = jnp.where((behind >= 0) & (behind < 64), real, 0.0)
        k = kappa[p]
        row_ok = (row >= 0) & (row < 96)
        xp = k + kappa[p + 1]
        xm = k + kappa[p - 1]
        yp = k + pltpu.roll(k, TALL - 1, 0)
        ym = k + pltpu.roll(k, 1, 0)
        zp = k + jnp.where(lane < 127, pltpu.roll(k, 127, 1), 0.0)
        zm = k + jnp.where(lane > 0, pltpu.roll(k, 1, 1), 0.0)
        kinds = [
            jnp.where(row_ok, xp * to_ahead, 0.0),
            jnp.where(row_ok, xm * to_behind, 0.0),
            jnp.where(row_ok & (row < 95), yp * real, 0.0),
            jnp.where(row_ok & (row > 0), ym * real, 0.0),
            jnp.where(row_ok & (lane < 127), zp * real, 0.0),
            jnp.where(row_ok & (lane > 0), zm * real, 0.0),
            half * (((xp + xm) + (yp + ym)) + (zp + zm)),
            begin[p - 1],
        ]
        for i, v in enumerate(kinds):
            weights[pl.ds((p - 1) * TALL * 8 + i, TALL, stride=8), :] = v
    ca, cb, lag = consts[0], consts[1], consts[2]
    base = lag * lag + DET_SHIFT
    for p, lo, hi in ((2, 1, 19), (3, 1, 19), (1, 2, 18), (4, 2, 18)):
        for j in range(lo, hi):
            td = jnp.broadcast_to(weights[pl.ds(((p - 1) * TALL + j) * 8 + 6, 1), :], (8, 128))
            a = ca + td
            b = cb + td
            at = region(p, j)
            inv[at, 0] = 1.0 / (a * a + base)
            inv[at, 1] = 1.0 / (b * b + base)


def spread_body(pos, *rest):
    pieces, (own, wish, near, far), stage = rest[:8], rest[8:12], rest[12]
    t = pos[0]
    rows = 12 * WIN
    for k in range(8):
        stage[pl.ds(pl.multiple_of((t ^ k) * rows, 8), rows), :] = pieces[k][...]
    for x in range(2):
        for j in range(WIN):
            for f in range(3):
                for n in range(2):
                    v = stage[pl.ds(((f * 2 + n) * 2 + x) * WIN + j, 8, stride=rows), :]
                    if f < 2:
                        c = f * 2 + n
                        own[x, j, c] = v
                        put_field(near, far, x, j, c, v)
                    else:
                        if 1 <= j <= 18:
                            wish[x, j - 1, n] = v
                        if 2 <= j <= 17:
                            out = far if x == 1 else near
                            out[136 + (j - 2) * 2 + n] = v


def put_field(near, far, x, j, c, v):
    first, second = (near, far) if x == 0 else (far, near)
    if 1 <= j <= 18:
        first[(j - 1) * 4 + c] = v
    if 2 <= j <= 17:
        second[72 + (j - 2) * 4 + c] = v


def region(p, j):
    if p == 2 or p == 3:
        return (p - 2) * 18 + j - 1
    return (36 if p == 1 else 52) + j - 2


def spread_sum(v, around, w):
    px, mx, py, my = around
    up = pltpu.roll(v, 127, 1)
    down = pltpu.roll(v, 1, 1)
    return ((w[0] * px + w[1] * mx) + (w[2] * py + w[3] * my)) + (w[4] * up + w[5] * down)


def row_weights(weights, p, j, count):
    tile = weights[(p - 1) * TALL + j]
    return [jnp.broadcast_to(tile[k : k + 1, :], (8, 128)) for k in range(count)]


def solve(right, td, inv, consts):
    ur, ui, pr, pi = right
    shift_a, shift_b, lag = consts
    inv_a, inv_b = inv
    a = shift_a + td
    b = shift_b + td
    return (
        (a * ur + lag * ui - COUPLING * pr) * inv_a,
        (b * ui - lag * ur - COUPLING * pi) * inv_b,
        (TAU * ur + a * pr - lag * pi) * inv_a,
        (TAU * ui + b * pi + lag * pr) * inv_b,
    )


def residual_body(own, wish, near, far, tnear, tfar, weights, consts, inv, forward, rhs, it, out_near, out_far, res, zed):
    def field(p, j, c):
        if p == 2 or p == 3:
            return own[p - 2, j, c]
        side = near if p < 2 else far
        if p == 1 or p == 4:
            return side[(j - 1) * 4 + c]
        return side[72 + (j - 2) * 4 + c]

    def wanted(p, j, n):
        if p == 2 or p == 3:
            return wish[p - 2, j - 1, n]
        return (tnear if p == 1 else tfar)[136 + (j - 2) * 2 + n]

    sub = lax.broadcasted_iota(jnp.int32, (8, 128), 0)
    first = jnp.where(sub == 0, 1.0, 0.0)
    not_first = jnp.where(sub == 0, 0.0, 1.0)
    not_last = jnp.where(sub == 7, 0.0, 1.0)
    for p, lo, hi in ((2, 1, 19), (3, 1, 19), (1, 2, 18), (4, 2, 18)):
        def row(j, carry, p=p):
            w = row_weights(weights, p, j, 8)
            td = w[6]
            v = [field(p, j, c) for c in range(4)]
            n = [
                spread_sum(v[c], (field(p + 1, j, c), field(p - 1, j, c), field(p, j + 1, c), field(p, j - 1, c)), w)
                for c in range(4)
            ]
            at = region(p, j)
            ue, uo, pe, po = v
            before = pltpu.roll(uo, 1, 0) * not_first
            after = pltpu.roll(pe, 7, 0) * not_last
            res[at, 0] = w[7] * first - (ue - before + (td * ue - n[0]) + COUPLING * pe)
            res[at, 1] = -(uo - ue + (td * uo - n[1]) + COUPLING * po)
            res[at, 2] = -TAU * wanted(p, j, 0) - (pe - po + (td * pe - n[2]) - TAU * ue)
            res[at, 3] = -TAU * wanted(p, j, 1) - (po - after + (td * po - n[3]) - TAU * uo)
            return carry
        rows(lo, hi, row)

    def group(g, carry):
        block = res[pl.ds(g * 4, 4)].reshape(128, 128)
        done = jnp.dot(forward[...], block, precision=lax.Precision.HIGHEST, preferred_element_type=jnp.float32)
        rhs[pl.ds(g * 4, 4)] = done.reshape(4, 4, 8, 128)
        return carry
    rows(0, 17, group)

    cs = (consts[0], consts[1], consts[2])
    for p, lo, hi in ((2, 1, 19), (3, 1, 19), (1, 2, 18), (4, 2, 18)):
        def row(j, carry, p=p):
            td = row_weights(weights, p, j, 8)[6]
            at = region(p, j)
            z = solve([rhs[at, c] for c in range(4)], td, (inv[at, 0], inv[at, 1]), cs)
            for c in range(4):
                zed[at, c] = z[c]
            return carry
        rows(lo, hi, row)

    for p in (2, 3):
        def row(j, carry, p=p):
            w = row_weights(weights, p, j, 8)
            at = region(p, j)
            pushed = []
            for c in range(4):
                around = (zed[region(p + 1, j), c], zed[region(p - 1, j), c], zed[at + 1, c], zed[at - 1, c])
                pushed.append(rhs[at, c] + spread_sum(zed[at, c], around, w))
            z = solve(pushed, w[6], (inv[at, 0], inv[at, 1]), cs)
            for c in range(4):
                it[p - 2, j - 2, c] = z[c]
            return carry
        rows(2, 18, row)
    out_near[0:14] = it[0, 1:15]
    out_near[14:26] = it[1, 2:14]
    out_far[0:14] = it[1, 1:15]
    out_far[14:26] = it[0, 2:14]


def sweep_body(it, near, far, rhs, weights, consts, inv, back, zed, fin):
    def guess(p, j, c):
        if p == 2 or p == 3:
            return it[p - 2, j - 2, c]
        side = near if p < 2 else far
        if p == 1 or p == 4:
            return side[j - 3, c]
        return side[14 + j - 4, c]

    def at2(p, j):
        if p == 2 or p == 3:
            return (p - 2) * 14 + j - 3
        return (28 if p == 1 else 40) + j - 4

    cs = (consts[0], consts[1], consts[2])
    for p, lo, hi in ((2, 3, 17), (3, 3, 17), (1, 4, 16), (4, 4, 16)):
        def row(j, carry, p=p):
            w = row_weights(weights, p, j, 8)
            at = region(p, j)
            pushed = []
            for c in range(4):
                around = (guess(p + 1, j, c), guess(p - 1, j, c), guess(p, j + 1, c), guess(p, j - 1, c))
                pushed.append(rhs[at, c] + spread_sum(guess(p, j, c), around, w))
            z = solve(pushed, w[6], (inv[at, 0], inv[at, 1]), cs)
            for c in range(4):
                zed[at2(p, j), c] = z[c]
            return carry
        rows(lo, hi, row)
    for p in (2, 3):
        def row(j, carry, p=p):
            w = row_weights(weights, p, j, 8)
            at = region(p, j)
            here = at2(p, j)
            pushed = []
            for c in range(4):
                around = (zed[at2(p + 1, j), c], zed[at2(p - 1, j), c], zed[here + 1, c], zed[here - 1, c])
                pushed.append(rhs[at, c] + spread_sum(zed[here, c], around, w))
            z = solve(pushed, w[6], (inv[at, 0], inv[at, 1]), cs)
            for c in range(4):
                fin[(p - 2) * OWN + j - 4, c] = z[c]
            return carry
        rows(4, 16, row)

    def group(g, carry):
        block = fin[pl.ds(g * 4, 4)].reshape(128, 128)
        done = jnp.dot(back[...], block, precision=lax.Precision.HIGHEST, preferred_element_type=jnp.float32)
        fin[pl.ds(g * 4, 4)] = done.reshape(4, 4, 8, 128)
        return carry
    rows(0, 6, group)


def middle_body(pos, it, near, far, rhs, weights, consts, inv, back, own, new, send0, send1, zed, fin):
    sweep_body(it, near, far, rhs, weights, consts, inv, back, zed, fin)
    odd = pos[0] & 1
    for x in range(2):
        for j in range(OWN):
            for c in range(4):
                new[x, j, c] = own[x, j + HALO, c] + fin[x * OWN + j, c]
    top = pl.multiple_of(8 * (1 - odd), 4)
    bottom = 8 * odd
    for x in range(2):
        for j in range(HALO):
            send0[x, j] = new[x, top + j]
            send1[x, j] = new[x, bottom + j]


def widen_body(pos, new, got0, got1, own, near, far):
    odd = pos[0] & 1
    for x in range(2):
        own[x, HALO : HALO + OWN] = new[x]
        own[x, pl.ds(16 * (1 - odd), HALO)] = got0[x]
        own[x, pl.ds(16 * odd, HALO)] = got1[x]
    for x in range(2):
        first, second = (near, far) if x == 0 else (far, near)
        first[0:72] = own[x, 1:19].reshape(72, 8, 128)
        second[72:136] = own[x, 2:18].reshape(64, 8, 128)


def last_body(pos, it, near, far, rhs, weights, consts, inv, back, own, *rest):
    outs, (zed, fin, stage) = rest[:8], rest[8:]
    sweep_body(it, near, far, rhs, weights, consts, inv, back, zed, fin)
    t = pos[0]
    for x in range(2):
        for j in range(OWN):
            for c in range(4):
                stage[pl.ds((c * 2 + x) * OWN + j, 8, stride=8 * OWN), :] = own[x, j + HALO, c] + fin[x * OWN + j, c]
    for k in range(8):
        outs[k][...] = stage[pl.ds(pl.multiple_of((t ^ k) * 8 * OWN, 8), 8 * OWN), :]


def unpack_body(pos, *rest):
    pieces, (state, adjoint), stage = rest[:8], rest[8:10], rest[10]
    t = pos[0]
    flip = pos[1]
    for k in range(8):
        stage[t ^ k] = pieces[k][...]
    for f, ref in enumerate((state, adjoint)):
        for n in range(2):
            for x in range(2):
                base = ((f * 2 + n) * 2 + x) * OWN
                for d in range(8):
                    ref[n, x ^ flip, OWN * d : OWN * (d + 1), :] = stage[d, base : base + OWN, :]


def exchange(pieces):
    count = lax.axis_size("tm")
    return [pieces[0]] + [
        lax.ppermute(pieces[k], "tm", [(i, i ^ k) for i in range(count)]) for k in range(1, count)
    ]


def swap(block, axis, start):
    count = lax.axis_size(axis)
    route = []
    for i in range(start, count - 1, 2):
        route += [(i, i + 1), (i + 1, i)]
    return lax.ppermute(block, axis, route)


def on_device(state_guess, adjoint_guess, target, initial_state, diffusivity):
    t = lax.axis_index("tm").astype(jnp.int32)
    s = lax.axis_index("space").astype(jnp.int32)
    flip = s & 1
    pos = jnp.stack([t, flip, s])
    forward, back = (jnp.asarray(m) for m in transform_matrices())
    consts = jnp.asarray(mode_constants())

    *pieces, near_c, far_c, here_c = call(
        pack_body,
        "pack",
        [whole(12 * WIN, 128)] * 8 + [whole(3, TALL, 128)] * 2 + [whole(4, TALL, 128)],
        5,
        [pltpu.VMEM((8, 12 * WIN, 128), jnp.float32)],
    )(pos, state_guess, adjoint_guess, target, diffusivity, initial_state)
    far_c = swap(far_c, "space", 0)
    near_c = swap(near_c, "space", 1)
    got = exchange(pieces)
    weights, inv = call(
        coefficient_body, "coefficients", [whole(4 * TALL * 8, 128), whole(68, 2, 8, 128)], 4
    )(pos, here_c, near_c, far_c, consts)
    weights = weights.reshape(4 * TALL, 8, 128)

    own, wish, near, far = call(
        spread_body,
        "spread",
        [whole(2, WIN, 4, 8, 128), whole(2, 18, 2, 8, 128), whole(168, 8, 128), whole(168, 8, 128)],
        8,
        [pltpu.VMEM((8 * 12 * WIN, 128), jnp.float32)],
    )(pos, *got)

    sweep_scratch = [pltpu.VMEM((52, 4, 8, 128), jnp.float32), pltpu.VMEM((24, 4, 8, 128), jnp.float32)]
    for outer in range(OUTER):
        far_f = swap(far, "space", 0)
        near_f = swap(near, "space", 1)
        if outer == 0:
            wish_near, wish_far = near_f, far_f
        rhs, it, near_z, far_z = call(
            residual_body,
            "residual",
            [whole(68, 4, 8, 128), whole(2, 16, 4, 8, 128), whole(26, 4, 8, 128), whole(26, 4, 8, 128)],
            10,
            [pltpu.VMEM((68, 4, 8, 128), jnp.float32)] * 2,
            scalars=0,
        )(own, wish, near_f, far_f, wish_near, wish_far, weights, consts, inv, forward)
        far_z = swap(far_z, "space", 0)
        near_z = swap(near_z, "space", 1)
        if outer < OUTER - 1:
            new, send0, send1 = call(
                middle_body,
                "middle",
                [whole(2, OWN, 4, 8, 128), whole(2, HALO, 4, 8, 128), whole(2, HALO, 4, 8, 128)],
                9,
                sweep_scratch,
            )(pos, it, near_z, far_z, rhs, weights, consts, inv, back, own)
            got0 = swap(send0, "tm", 0)
            got1 = swap(send1, "tm", 1)
            own, near, far = call(
                widen_body, "widen", [whole(2, WIN, 4, 8, 128), whole(136, 8, 128), whole(136, 8, 128)], 3
            )(pos, new, got0, got1)
    pieces = call(
        last_body,
        "last",
        [whole(8 * OWN, 128)] * 8,
        9,
        sweep_scratch + [pltpu.VMEM((64 * OWN, 128), jnp.float32)],
    )(pos, it, near_z, far_z, rhs, weights, consts, inv, back, own)
    got = exchange(pieces)
    return tuple(
        call(
            unpack_body,
            "unpack",
            [whole(2, 2, 96, 128)] * 2,
            8,
            [pltpu.VMEM((8, 8 * OWN, 128), jnp.float32)],
        )(pos, *got)
    )


def solution(mesh):
    in_specs = (
        P("tm", "space", None, None),
        P("tm", "space", None, None),
        P("tm", "space", None, None),
        P("space", None, None),
        P("space", None, None),
    )
    out_specs = (P("tm", "space", None, None), P("tm", "space", None, None))
    return jax.shard_map(
        on_device, mesh=mesh, in_specs=in_specs, out_specs=out_specs, check_vma=False
    )
```

```python
import math

import jax
import jax.numpy as jnp
import numpy as np
from jax import lax
from jax.experimental import pallas as pl
from jax.experimental.pallas import tpu as pltpu
from jax.sharding import PartitionSpec as P

TAU = 0.25
COUPLING = 5.0
DET_SHIFT = 1.25
OUTER = 2

OWN = 12
HALO = 4
WIN = OWN + 2 * HALO
ORDER = (4, 2, 6, 5, 3, 7, 1)
TALL = 24


def transform_matrices():
    modes = np.arange(8)[:, None]
    steps = np.concatenate([np.arange(0, 16, 2), np.arange(1, 16, 2)])[None, :]
    angle = 2.0 * np.pi * ((modes * steps) % 16) / 16.0
    real, imag = np.cos(angle), -np.sin(angle)
    imag[0] = np.where(steps[0] % 2 == 0, 1.0, -1.0)
    forward = np.concatenate([real, imag], 0)
    back = forward.T.copy() / 8.0
    back[:, 0] /= 2.0
    back[:, 8] /= 2.0
    eye = np.eye(8)
    return np.kron(eye, forward).astype(np.float32), np.kron(eye, back).astype(np.float32)


def mode_constants():
    theta = 2.0 * np.pi * np.arange(8) / 16.0
    shift_a = 1.0 - np.cos(theta)
    shift_b = shift_a.copy()
    shift_b[0] = 2.0
    lag = np.sin(theta)
    out = np.stack([shift_a, shift_b, lag])[:, :, None] * np.ones((1, 1, 128))
    return out.astype(np.float32)


def whole(*shape):
    return jax.ShapeDtypeStruct(shape, jnp.float32)


def call(body, name, outs, n_in, scratch=(), scalars=1, far_inputs=0):
    vmem = pl.BlockSpec(memory_space=pltpu.VMEM)
    anywhere = pl.BlockSpec(memory_space=pltpu.HBM)
    smem = pl.BlockSpec(memory_space=pltpu.SMEM)
    return pl.pallas_call(
        body,
        name=name,
        out_shape=outs,
        in_specs=[smem] * scalars + [anywhere] * far_inputs + [vmem] * n_in,
        out_specs=[vmem] * len(outs),
        scratch_shapes=list(scratch),
        compiler_params=pltpu.CompilerParams(vmem_limit_bytes=16 * 1024 * 1024),
    )


def rows(lo, hi, body):
    lax.fori_loop(lo, hi, body, 0, unroll=True)


def pack_body(pos, *rest):
    sources, outs, (near, far, here, stage), held, sems = rest[:5], rest[5:13], rest[13:17], rest[17:22], rest[22]
    copies = [pltpu.make_async_copy(sources[i], held[i], sems.at[i]) for i in range(5)]
    for copy in copies:
        copy.start()
    state, adjoint, target, kappa, begin = held
    t = pos[0]
    flip = pos[1]
    for f, ref in enumerate((state, adjoint, target)):
        copies[f].wait()
        for n in range(2):
            for x in range(2):
                base = ((f * 2 + n) * 2 + x) * WIN
                for d in range(8):
                    low = OWN * d - HALO
                    first, last = max(low, 0), min(low + WIN, 96)
                    stage[d, base + first - low : base + last - low, :] = ref[n, x ^ flip, first:last, :]
                    if first > low:
                        stage[d, base : base + first - low, :] = jnp.zeros((first - low, 128), jnp.float32)
                    if last < low + WIN:
                        stage[d, base + last - low : base + WIN, :] = jnp.zeros((low + WIN - last, 128), jnp.float32)
    for k in range(8):
        outs[k][...] = stage[t ^ k]
    copies[3].wait()
    copies[4].wait()
    for d in range(8):
        @pl.when(t == d)
        def window(d=d):
            low = OWN * d - HALO
            first, last = max(low, 0), min(low + TALL, 96)
            parts = []
            for ref, x in ((kappa, 0), (kappa, 1), (begin, 0), (begin, 1)):
                v = ref[x ^ flip, first:last, :]
                if first > low:
                    v = jnp.concatenate([jnp.zeros((first - low, 128), jnp.float32), v], 0)
                if last < low + TALL:
                    v = jnp.concatenate([v, jnp.zeros((low + TALL - last, 128), jnp.float32)], 0)
                parts.append(v)
            for i, v in enumerate(parts):
                here[i] = v
            for i, q in enumerate((0, 1, 2)):
                near[i] = parts[q]
            for i, q in enumerate((1, 0, 3)):
                far[i] = parts[q]


def coefficient_body(pos, here, near, far, consts, weights, inv):
    t, flip, s = pos[0], pos[1], pos[2]
    near, far = ([side[168 + 3 * i : 171 + 3 * i].reshape(TALL, 128) for i in range(3)] for side in (near, far))
    kappa = [near[1], near[0], here[0], here[1], far[0], far[1]]
    begin = [near[2], here[2], here[3], far[2]]
    lane = lax.broadcasted_iota(jnp.int32, (TALL, 128), 1)
    row = lax.broadcasted_iota(jnp.int32, (TALL, 128), 0) + (OWN * t - HALO)
    half = 0.5 * TAU
    for p in range(1, 5):
        plane = jnp.where(flip == 1, 2 * s + 3 - p, 2 * s - 2 + p)
        ahead = jnp.where(flip == 1, plane - 1, plane + 1)
        behind = jnp.where(flip == 1, plane + 1, plane - 1)
        real = jnp.where((plane >= 0) & (plane < 64), half, 0.0)
        to_ahead = jnp.where((ahead >= 0) & (ahead < 64), real, 0.0)
        to_behind = jnp.where((behind >= 0) & (behind < 64), real, 0.0)
        k = kappa[p]
        row_ok = (row >= 0) & (row < 96)
        xp = k + kappa[p + 1]
        xm = k + kappa[p - 1]
        yp = k + pltpu.roll(k, TALL - 1, 0)
        ym = k + pltpu.roll(k, 1, 0)
        zp = k + jnp.where(lane < 127, pltpu.roll(k, 127, 1), 0.0)
        zm = k + jnp.where(lane > 0, pltpu.roll(k, 1, 1), 0.0)
        kinds = [
            jnp.where(row_ok, xp * to_ahead, 0.0),
            jnp.where(row_ok, xm * to_behind, 0.0),
            jnp.where(row_ok & (row < 95), yp * real, 0.0),
            jnp.where(row_ok & (row > 0), ym * real, 0.0),
            jnp.where(row_ok & (lane < 127), zp * real, 0.0),
            jnp.where(row_ok & (lane > 0), zm * real, 0.0),
            half * (((xp + xm) + (yp + ym)) + (zp + zm)),
            begin[p - 1],
        ]
        for i, v in enumerate(kinds):
            weights[pl.ds((p - 1) * TALL * 8 + i, TALL, stride=8), :] = v
    ca, cb, lag = consts[0], consts[1], consts[2]
    base = lag * lag + DET_SHIFT
    for p, lo, hi in ((2, 1, 19), (3, 1, 19), (1, 2, 18), (4, 2, 18)):
        for j in range(lo, hi):
            td = jnp.broadcast_to(weights[pl.ds(((p - 1) * TALL + j) * 8 + 6, 1), :], (8, 128))
            a = ca + td
            b = cb + td
            at = region(p, j)
            inv[at, 0] = 1.0 / (a * a + base)
            inv[at, 1] = 1.0 / (b * b + base)


def spread_body(pos, *rest):
    pieces, (near_c, far_c), (own, wish, near, far), stage = rest[:8], rest[8:10], rest[10:14], rest[14]
    for i in range(3):
        near[168 + 3 * i : 171 + 3 * i] = near_c[i].reshape(3, 8, 128)
        far[168 + 3 * i : 171 + 3 * i] = far_c[i].reshape(3, 8, 128)
    t = pos[0]
    rows = 12 * WIN
    for k, piece in zip(ORDER + (0,), pieces):
        stage[pl.ds(pl.multiple_of((t ^ k) * rows, 8), rows), :] = piece[...]
    for x in range(2):
        for j in range(WIN):
            for f in range(3):
                for n in range(2):
                    v = stage[pl.ds(((f * 2 + n) * 2 + x) * WIN + j, 8, stride=rows), :]
                    if f < 2:
                        c = f * 2 + n
                        own[x, j, c] = v
                        put_field(near, far, x, j, c, v)
                    else:
                        if 1 <= j <= 18:
                            wish[x, j - 1, n] = v
                        if 2 <= j <= 17:
                            out = far if x == 1 else near
                            out[136 + (j - 2) * 2 + n] = v


def put_field(near, far, x, j, c, v):
    first, second = (near, far) if x == 0 else (far, near)
    if 1 <= j <= 18:
        first[(j - 1) * 4 + c] = v
    if 2 <= j <= 17:
        second[72 + (j - 2) * 4 + c] = v


def region(p, j):
    if p == 2 or p == 3:
        return (p - 2) * 18 + j - 1
    return (36 if p == 1 else 52) + j - 2


def spread_sum(v, around, w):
    px, mx, py, my = around
    up = pltpu.roll(v, 127, 1)
    down = pltpu.roll(v, 1, 1)
    return ((w[0] * px + w[1] * mx) + (w[2] * py + w[3] * my)) + (w[4] * up + w[5] * down)


def row_weights(weights, p, j, count):
    tile = weights[(p - 1) * TALL + j]
    return [jnp.broadcast_to(tile[k : k + 1, :], (8, 128)) for k in range(count)]


def solve(right, td, inv, consts):
    ur, ui, pr, pi = right
    shift_a, shift_b, lag = consts
    inv_a, inv_b = inv
    a = shift_a + td
    b = shift_b + td
    return (
        (a * ur + lag * ui - COUPLING * pr) * inv_a,
        (b * ui - lag * ur - COUPLING * pi) * inv_b,
        (TAU * ur + a * pr - lag * pi) * inv_a,
        (TAU * ui + b * pi + lag * pr) * inv_b,
    )


def residual_body(own, wish, near, far, tnear, tfar, weights, consts, inv, forward, rhs, it, out_near, out_far, res, zed):
    def field(p, j, c):
        if p == 2 or p == 3:
            return own[p - 2, j, c]
        side = near if p < 2 else far
        if p == 1 or p == 4:
            return side[(j - 1) * 4 + c]
        return side[72 + (j - 2) * 4 + c]

    def wanted(p, j, n):
        if p == 2 or p == 3:
            return wish[p - 2, j - 1, n]
        return (tnear if p == 1 else tfar)[136 + (j - 2) * 2 + n]

    sub = lax.broadcasted_iota(jnp.int32, (8, 128), 0)
    first = jnp.where(sub == 0, 1.0, 0.0)
    not_first = jnp.where(sub == 0, 0.0, 1.0)
    not_last = jnp.where(sub == 7, 0.0, 1.0)
    for p, lo, hi in ((2, 1, 19), (3, 1, 19), (1, 2, 18), (4, 2, 18)):
        def row(j, carry, p=p):
            w = row_weights(weights, p, j, 8)
            td = w[6]
            v = [field(p, j, c) for c in range(4)]
            n = [
                spread_sum(v[c], (field(p + 1, j, c), field(p - 1, j, c), field(p, j + 1, c), field(p, j - 1, c)), w)
                for c in range(4)
            ]
            at = region(p, j)
            ue, uo, pe, po = v
            before = pltpu.roll(uo, 1, 0) * not_first
            after = pltpu.roll(pe, 7, 0) * not_last
            res[at, 0] = w[7] * first - (ue - before + (td * ue - n[0]) + COUPLING * pe)
            res[at, 1] = -(uo - ue + (td * uo - n[1]) + COUPLING * po)
            res[at, 2] = -TAU * wanted(p, j, 0) - (pe - po + (td * pe - n[2]) - TAU * ue)
            res[at, 3] = -TAU * wanted(p, j, 1) - (po - after + (td * po - n[3]) - TAU * uo)
            return carry
        rows(lo, hi, row)

    def group(g, carry):
        block = res[pl.ds(g * 4, 4)].reshape(128, 128)
        done = jnp.dot(forward[...], block, precision=lax.Precision.HIGHEST, preferred_element_type=jnp.float32)
        rhs[pl.ds(g * 4, 4)] = done.reshape(4, 4, 8, 128)
        return carry
    rows(0, 17, group)

    cs = (consts[0], consts[1], consts[2])
    for p, lo, hi in ((2, 1, 19), (3, 1, 19), (1, 2, 18), (4, 2, 18)):
        def row(j, carry, p=p):
            td = row_weights(weights, p, j, 8)[6]
            at = region(p, j)
            z = solve([rhs[at, c] for c in range(4)], td, (inv[at, 0], inv[at, 1]), cs)
            for c in range(4):
                zed[at, c] = z[c]
            return carry
        rows(lo, hi, row)

    for p in (2, 3):
        def row(j, carry, p=p):
            w = row_weights(weights, p, j, 8)
            at = region(p, j)
            pushed = []
            for c in range(4):
                around = (zed[region(p + 1, j), c], zed[region(p - 1, j), c], zed[at + 1, c], zed[at - 1, c])
                pushed.append(rhs[at, c] + spread_sum(zed[at, c], around, w))
            z = solve(pushed, w[6], (inv[at, 0], inv[at, 1]), cs)
            for c in range(4):
                it[p - 2, j - 2, c] = z[c]
            return carry
        rows(2, 18, row)
    out_near[0:14] = it[0, 1:15]
    out_near[14:26] = it[1, 2:14]
    out_far[0:14] = it[1, 1:15]
    out_far[14:26] = it[0, 2:14]


def sweep_body(it, near, far, rhs, weights, consts, inv, back, zed, fin):
    def guess(p, j, c):
        if p == 2 or p == 3:
            return it[p - 2, j - 2, c]
        side = near if p < 2 else far
        if p == 1 or p == 4:
            return side[j - 3, c]
        return side[14 + j - 4, c]

    def at2(p, j):
        if p == 2 or p == 3:
            return (p - 2) * 14 + j - 3
        return (28 if p == 1 else 40) + j - 4

    cs = (consts[0], consts[1], consts[2])
    for p, lo, hi in ((2, 3, 17), (3, 3, 17), (1, 4, 16), (4, 4, 16)):
        def row(j, carry, p=p):
            w = row_weights(weights, p, j, 8)
            at = region(p, j)
            pushed = []
            for c in range(4):
                around = (guess(p + 1, j, c), guess(p - 1, j, c), guess(p, j + 1, c), guess(p, j - 1, c))
                pushed.append(rhs[at, c] + spread_sum(guess(p, j, c), around, w))
            z = solve(pushed, w[6], (inv[at, 0], inv[at, 1]), cs)
            for c in range(4):
                zed[at2(p, j), c] = z[c]
            return carry
        rows(lo, hi, row)
    for p in (2, 3):
        def row(j, carry, p=p):
            w = row_weights(weights, p, j, 8)
            at = region(p, j)
            here = at2(p, j)
            pushed = []
            for c in range(4):
                around = (zed[at2(p + 1, j), c], zed[at2(p - 1, j), c], zed[here + 1, c], zed[here - 1, c])
                pushed.append(rhs[at, c] + spread_sum(zed[here, c], around, w))
            z = solve(pushed, w[6], (inv[at, 0], inv[at, 1]), cs)
            for c in range(4):
                fin[(p - 2) * OWN + j - 4, c] = z[c]
            return carry
        rows(4, 16, row)

    def group(g, carry):
        block = fin[pl.ds(g * 4, 4)].reshape(128, 128)
        done = jnp.dot(back[...], block, precision=lax.Precision.HIGHEST, preferred_element_type=jnp.float32)
        fin[pl.ds(g * 4, 4)] = done.reshape(4, 4, 8, 128)
        return carry
    rows(0, 6, group)


def middle_body(it, near, far, rhs, weights, consts, inv, back, own, new, out_near, out_far, zed, fin):
    sweep_body(it, near, far, rhs, weights, consts, inv, back, zed, fin)
    for x in range(2):
        first, second = (out_near, out_far) if x == 0 else (out_far, out_near)
        for j in range(OWN):
            for c in range(4):
                v = own[x, j + HALO, c] + fin[x * OWN + j, c]
                new[x, j, c] = v
                first[j, c] = v
                second[OWN + j, c] = v


EDGE = ((0, 4), (4, 4), (8, 3), (11, 3), (14, 2), (16, 2))


def edges_body(pos, new, near, far, send0, send1):
    odd = pos[0] & 1
    planes = (
        lambda j, n: new[0, pl.ds(j, n)],
        lambda j, n: new[1, pl.ds(j, n)],
        lambda j, n: near[pl.ds(j, n)],
        lambda j, n: far[pl.ds(j, n)],
        lambda j, n: near[pl.ds(OWN + j, n)],
        lambda j, n: far[pl.ds(OWN + j, n)],
    )
    for take, (at, n) in zip(planes, EDGE):
        send0[at : at + n] = take((OWN - n) * (1 - odd), n)
        send1[at : at + n] = take((OWN - n) * odd, n)


def widen_body(pos, got1, got0, new, near_x, far_x, own, near, far):
    odd = pos[0] & 1
    for x in range(2):
        own[x, HALO : HALO + OWN] = new[x]
    for out, got in ((near, near_x), (far, far_x)):
        out[3 : 3 + OWN] = got[0:OWN]
        out[20 : 20 + OWN] = got[OWN : 2 * OWN]
    for got, high in ((got0, 1 - odd), (got1, odd)):
        own[0, pl.ds(16 * high, 4)] = got[0:4]
        own[1, pl.ds(16 * high, 4)] = got[4:8]
        near[pl.ds(15 * high, 3)] = got[8:11]
        far[pl.ds(15 * high, 3)] = got[11:14]
        near[pl.ds(18 + 14 * high, 2)] = got[14:16]
        far[pl.ds(18 + 14 * high, 2)] = got[16:18]


def last_body(pos, it, near, far, rhs, weights, consts, inv, back, own, *rest):
    outs, (zed, fin, stage) = rest[:8], rest[8:]
    sweep_body(it, near, far, rhs, weights, consts, inv, back, zed, fin)
    t = pos[0]
    for x in range(2):
        for j in range(OWN):
            for c in range(4):
                stage[pl.ds((c * 2 + x) * OWN + j, 8, stride=8 * OWN), :] = own[x, j + HALO, c] + fin[x * OWN + j, c]
    for k in range(8):
        outs[k][...] = stage[pl.ds(pl.multiple_of((t ^ k) * 8 * OWN, 8), 8 * OWN), :]


def unpack_body(pos, *rest):
    pieces, (state, adjoint), stage = rest[:8], rest[8:10], rest[10]
    t = pos[0]
    flip = pos[1]
    for k, piece in zip(ORDER + (0,), pieces):
        stage[t ^ k] = piece[...]
    for f, ref in enumerate((state, adjoint)):
        for n in range(2):
            for x in range(2):
                base = ((f * 2 + n) * 2 + x) * OWN
                for d in range(8):
                    ref[n, x ^ flip, OWN * d : OWN * (d + 1), :] = stage[d, base : base + OWN, :]


def exchange(pieces):
    count = lax.axis_size("tm")
    return [lax.ppermute(pieces[k], "tm", [(i, i ^ k) for i in range(count)]) for k in ORDER] + [pieces[0]]


def swap(block, axis, start):
    count = lax.axis_size(axis)
    route = []
    for i in range(start, count - 1, 2):
        route += [(i, i + 1), (i + 1, i)]
    return lax.ppermute(block, axis, route)


def on_device(state_guess, adjoint_guess, target, initial_state, diffusivity):
    t = lax.axis_index("tm").astype(jnp.int32)
    s = lax.axis_index("space").astype(jnp.int32)
    flip = s & 1
    pos = jnp.stack([t, flip, s])
    forward, back = (jnp.asarray(m) for m in transform_matrices())
    consts = jnp.asarray(mode_constants())

    *pieces, near_c, far_c, here_c = call(
        pack_body,
        "pack",
        [whole(12 * WIN, 128)] * 8 + [whole(3, TALL, 128)] * 2 + [whole(4, TALL, 128)],
        0,
        [pltpu.VMEM((8, 12 * WIN, 128), jnp.float32)]
        + [pltpu.VMEM((2, 2, 96, 128), jnp.float32)] * 3
        + [pltpu.VMEM((2, 96, 128), jnp.float32)] * 2
        + [pltpu.SemaphoreType.DMA((5,))],
        far_inputs=5,
    )(pos, *(pltpu.with_memory_space_constraint(a, pltpu.HBM) for a in (state_guess, adjoint_guess, target, diffusivity, initial_state)))
    got = exchange(pieces)
    own, wish, near, far = call(
        spread_body,
        "spread",
        [whole(2, WIN, 4, 8, 128), whole(2, 18, 2, 8, 128), whole(177, 8, 128), whole(177, 8, 128)],
        10,
        [pltpu.VMEM((8 * 12 * WIN, 128), jnp.float32)],
    )(pos, *got, near_c, far_c)
    far = far_first = swap(far, "space", 0)
    near = near_first = swap(near, "space", 1)
    weights, inv = call(
        coefficient_body, "coefficients", [whole(4 * TALL * 8, 128), whole(68, 2, 8, 128)], 4
    )(pos, here_c, near, far, consts)
    weights = weights.reshape(4 * TALL, 8, 128)

    sweep_scratch = [pltpu.VMEM((52, 4, 8, 128), jnp.float32), pltpu.VMEM((24, 4, 8, 128), jnp.float32)]
    for outer in range(OUTER):
        rhs, it, near_z, far_z = call(
            residual_body,
            "residual",
            [whole(68, 4, 8, 128), whole(2, 16, 4, 8, 128), whole(26, 4, 8, 128), whole(26, 4, 8, 128)],
            10,
            [pltpu.VMEM((68, 4, 8, 128), jnp.float32)] * 2,
            scalars=0,
        )(own, wish, near, far, near_first, far_first, weights, consts, inv, forward)
        far_z = swap(far_z, "space", 0)
        near_z = swap(near_z, "space", 1)
        if outer < OUTER - 1:
            new, near, far = call(
                middle_body,
                "middle",
                [whole(2, OWN, 4, 8, 128), whole(2 * OWN, 4, 8, 128), whole(2 * OWN, 4, 8, 128)],
                9,
                sweep_scratch,
                scalars=0,
            )(it, near_z, far_z, rhs, weights, consts, inv, back, own)
            far = swap(far, "space", 0)
            near = swap(near, "space", 1)
            send0, send1 = call(edges_body, "edges", [whole(18, 4, 8, 128)] * 2, 3)(pos, new, near, far)
            got1 = swap(send1, "tm", 1)
            got0 = swap(send0, "tm", 0)
            own, near, far = call(
                widen_body, "widen", [whole(2, WIN, 4, 8, 128), whole(34, 4, 8, 128), whole(34, 4, 8, 128)], 5
            )(pos, got1, got0, new, near, far)
            near = near.reshape(136, 8, 128)
            far = far.reshape(136, 8, 128)
    pieces = call(
        last_body,
        "last",
        [whole(8 * OWN, 128)] * 8,
        9,
        sweep_scratch + [pltpu.VMEM((64 * OWN, 128), jnp.float32)],
    )(pos, it, near_z, far_z, rhs, weights, consts, inv, back, own)
    got = exchange(pieces)
    return tuple(
        call(
            unpack_body,
            "unpack",
            [whole(2, 2, 96, 128)] * 2,
            8,
            [pltpu.VMEM((8, 8 * OWN, 128), jnp.float32)],
        )(pos, *got)
    )


def solution(mesh):
    in_specs = (
        P("tm", "space", None, None),
        P("tm", "space", None, None),
        P("tm", "space", None, None),
        P("space", None, None),
        P("space", None, None),
    )
    out_specs = (P("tm", "space", None, None), P("tm", "space", None, None))
    return jax.shard_map(
        on_device, mesh=mesh, in_specs=in_specs, out_specs=out_specs, check_vma=False
    )
```

```python
import math

import jax
import jax.numpy as jnp
import numpy as np
from jax import lax
from jax.experimental import pallas as pl
from jax.experimental.pallas import tpu as pltpu
from jax.sharding import PartitionSpec as P

TAU = 0.25
COUPLING = 5.0
DET_SHIFT = 1.25
OUTER = 2

OWN = 12
HALO = 4
WIN = OWN + 2 * HALO
ORDER = (4, 2, 6, 5, 3, 7, 1)
TALL = 24


def transform_matrices():
    modes = np.arange(8)[:, None]
    steps = np.concatenate([np.arange(0, 16, 2), np.arange(1, 16, 2)])[None, :]
    angle = 2.0 * np.pi * ((modes * steps) % 16) / 16.0
    real, imag = np.cos(angle), -np.sin(angle)
    imag[0] = np.where(steps[0] % 2 == 0, 1.0, -1.0)
    forward = np.concatenate([real, imag], 0)
    back = forward.T.copy() / 8.0
    back[:, 0] /= 2.0
    back[:, 8] /= 2.0
    eye = np.eye(8)
    return np.kron(eye, forward).astype(np.float32), np.kron(eye, back).astype(np.float32)


def mode_constants():
    theta = 2.0 * np.pi * np.arange(8) / 16.0
    shift_a = 1.0 - np.cos(theta)
    shift_b = shift_a.copy()
    shift_b[0] = 2.0
    lag = np.sin(theta)
    phase_a, phase_b = np.cos(theta), np.sin(theta)
    phase_b[0] = -1.0
    share = np.where(np.arange(8) == 0, 1.0, 2.0) / 16.0
    last_a, last_b = share * np.cos(15.0 * theta), -share * np.sin(15.0 * theta)
    last_b[0] = -1.0 / 16.0
    first_a, first_b = share, np.where(np.arange(8) == 0, 1.0, 0.0) / 16.0
    slot = np.where(np.arange(8) == 0, 1.0, 0.0)
    kinds = [shift_a, shift_b, lag, phase_a, phase_b, last_a, last_b, first_a, first_b, slot]
    return (np.stack(kinds)[:, :, None] * np.ones((1, 1, 128))).astype(np.float32)


def whole(*shape):
    return jax.ShapeDtypeStruct(shape, jnp.float32)


def call(body, name, outs, n_in, scratch=(), scalars=1, far_inputs=0):
    vmem = pl.BlockSpec(memory_space=pltpu.VMEM)
    anywhere = pl.BlockSpec(memory_space=pltpu.HBM)
    smem = pl.BlockSpec(memory_space=pltpu.SMEM)
    return pl.pallas_call(
        body,
        name=name,
        out_shape=outs,
        in_specs=[smem] * scalars + [anywhere] * far_inputs + [vmem] * n_in,
        out_specs=[vmem] * len(outs),
        scratch_shapes=list(scratch),
        compiler_params=pltpu.CompilerParams(vmem_limit_bytes=16 * 1024 * 1024),
    )


def rows(lo, hi, body):
    lax.fori_loop(lo, hi, body, 0, unroll=True)


def pack_body(pos, *rest):
    sources, outs, (near, far, here), tables = rest[:8], rest[8:16], rest[16:19], rest[19:22]
    stage, held, sems = rest[22], rest[23:28], rest[28]
    copies = [pltpu.make_async_copy(sources[i], ref, sems.at[i]) for i, ref in enumerate(held + tables)]
    for copy in copies:
        copy.start()
    state, adjoint, target, kappa, begin = held
    t = pos[0]
    flip = pos[1]
    for f, ref in enumerate((state, adjoint, target)):
        copies[f].wait()
        for n in range(2):
            for x in range(2):
                base = ((f * 2 + n) * 2 + x) * WIN
                for d in range(8):
                    low = OWN * d - HALO
                    first, last = max(low, 0), min(low + WIN, 96)
                    stage[d, base + first - low : base + last - low, :] = ref[n, x ^ flip, first:last, :]
                    if first > low:
                        stage[d, base : base + first - low, :] = jnp.zeros((first - low, 128), jnp.float32)
                    if last < low + WIN:
                        stage[d, base + last - low : base + WIN, :] = jnp.zeros((low + WIN - last, 128), jnp.float32)
    for k in range(8):
        outs[k][...] = stage[t ^ k]
    for copy in copies[3:]:
        copy.wait()
    for d in range(8):
        @pl.when(t == d)
        def window(d=d):
            low = OWN * d - HALO
            first, last = max(low, 0), min(low + TALL, 96)
            parts = []
            for ref, x in ((kappa, 0), (kappa, 1), (begin, 0), (begin, 1)):
                v = ref[x ^ flip, first:last, :]
                if first > low:
                    v = jnp.concatenate([jnp.zeros((first - low, 128), jnp.float32), v], 0)
                if last < low + TALL:
                    v = jnp.concatenate([v, jnp.zeros((low + TALL - last, 128), jnp.float32)], 0)
                parts.append(v)
            for i, v in enumerate(parts):
                here[i] = v
            for i, q in enumerate((0, 1, 2)):
                near[i] = parts[q]
            for i, q in enumerate((1, 0, 3)):
                far[i] = parts[q]


def coefficient_body(pos, here, near, far, consts, weights, inv):
    t, flip, s = pos[0], pos[1], pos[2]
    near, far = ([side[168 + 3 * i : 171 + 3 * i].reshape(TALL, 128) for i in range(3)] for side in (near, far))
    kappa = [near[1], near[0], here[0], here[1], far[0], far[1]]
    begin = [near[2], here[2], here[3], far[2]]
    lane = lax.broadcasted_iota(jnp.int32, (TALL, 128), 1)
    row = lax.broadcasted_iota(jnp.int32, (TALL, 128), 0) + (OWN * t - HALO)
    half = 0.5 * TAU
    for p in range(1, 5):
        plane = jnp.where(flip == 1, 2 * s + 3 - p, 2 * s - 2 + p)
        ahead = jnp.where(flip == 1, plane - 1, plane + 1)
        behind = jnp.where(flip == 1, plane + 1, plane - 1)
        real = jnp.where((plane >= 0) & (plane < 64), half, 0.0)
        to_ahead = jnp.where((ahead >= 0) & (ahead < 64), real, 0.0)
        to_behind = jnp.where((behind >= 0) & (behind < 64), real, 0.0)
        k = kappa[p]
        row_ok = (row >= 0) & (row < 96)
        xp = k + kappa[p + 1]
        xm = k + kappa[p - 1]
        yp = k + pltpu.roll(k, TALL - 1, 0)
        ym = k + pltpu.roll(k, 1, 0)
        zp = k + jnp.where(lane < 127, pltpu.roll(k, 127, 1), 0.0)
        zm = k + jnp.where(lane > 0, pltpu.roll(k, 1, 1), 0.0)
        kinds = [
            jnp.where(row_ok, xp * to_ahead, 0.0),
            jnp.where(row_ok, xm * to_behind, 0.0),
            jnp.where(row_ok & (row < 95), yp * real, 0.0),
            jnp.where(row_ok & (row > 0), ym * real, 0.0),
            jnp.where(row_ok & (lane < 127), zp * real, 0.0),
            jnp.where(row_ok & (lane > 0), zm * real, 0.0),
            half * (((xp + xm) + (yp + ym)) + (zp + zm)),
            begin[p - 1],
        ]
        for i, v in enumerate(kinds):
            weights[pl.ds((p - 1) * TALL * 8 + i, TALL, stride=8), :] = v
    ca, cb, lag = consts[0], consts[1], consts[2]
    base = lag * lag + DET_SHIFT
    for p, lo, hi in ((2, 1, 19), (3, 1, 19), (1, 2, 18), (4, 2, 18)):
        for j in range(lo, hi):
            td = jnp.broadcast_to(weights[pl.ds(((p - 1) * TALL + j) * 8 + 6, 1), :], (8, 128))
            a = ca + td
            b = cb + td
            at = region(p, j)
            inv[at, 0] = 1.0 / (a * a + base)
            inv[at, 1] = 1.0 / (b * b + base)


def spread_body(pos, *rest):
    pieces, (near_c, far_c, forward), (own, wish, near, far), stage = rest[:8], rest[8:11], rest[11:15], rest[15]
    for i in range(3):
        near[168 + 3 * i : 171 + 3 * i] = near_c[i].reshape(3, 8, 128)
        far[168 + 3 * i : 171 + 3 * i] = far_c[i].reshape(3, 8, 128)
    t = pos[0]
    rows = 12 * WIN
    for k, piece in zip(ORDER + (0,), pieces):
        stage[pl.ds(pl.multiple_of((t ^ k) * rows, 8), rows), :] = piece[...]

    def steps(f, n, x, j):
        return stage[pl.ds(((f * 2 + n) * 2 + x) * WIN + j, 8, stride=rows), :]

    matrix = forward[...]
    for x in range(2):
        for low in range(0, WIN, 4):
            block = [steps(f, n, x, low + i) for i in range(4) for f in range(2) for n in range(2)]
            done = transform(matrix, jnp.concatenate(block, 0))
            for i in range(4):
                for c in range(4):
                    v = done[(i * 4 + c) * 8 : (i * 4 + c + 1) * 8]
                    own[x, low + i, c] = v
                    put_field(near, far, x, low + i, c, v)
    cells = [(x, j) for x in range(2) for j in range(WIN)]
    for low in range(0, len(cells), 8):
        block = [steps(2, n, x, j) for x, j in cells[low : low + 8] for n in range(2)]
        done = transform(matrix, jnp.concatenate(block, 0))
        for i, (x, j) in enumerate(cells[low : low + 8]):
            for n in range(2):
                v = done[(i * 2 + n) * 8 : (i * 2 + n + 1) * 8]
                if 1 <= j <= 18:
                    wish[x, j - 1, n] = v
                if 2 <= j <= 17:
                    out = far if x == 1 else near
                    out[136 + (j - 2) * 2 + n] = v


def transform(matrix, block):
    return jnp.dot(matrix, block, precision=lax.Precision.HIGHEST, preferred_element_type=jnp.float32)


def put_field(near, far, x, j, c, v):
    first, second = (near, far) if x == 0 else (far, near)
    if 1 <= j <= 18:
        first[(j - 1) * 4 + c] = v
    if 2 <= j <= 17:
        second[72 + (j - 2) * 4 + c] = v


def region(p, j):
    if p == 2 or p == 3:
        return (p - 2) * 18 + j - 1
    return (36 if p == 1 else 52) + j - 2


def spread_sum(v, around, w):
    px, mx, py, my = around
    up = pltpu.roll(v, 127, 1)
    down = pltpu.roll(v, 1, 1)
    return ((w[0] * px + w[1] * mx) + (w[2] * py + w[3] * my)) + (w[4] * up + w[5] * down)


def row_weights(weights, p, j, count):
    tile = weights[(p - 1) * TALL + j]
    return [jnp.broadcast_to(tile[k : k + 1, :], (8, 128)) for k in range(count)]


def solve(right, td, inv, consts):
    ur, ui, pr, pi = right
    shift_a, shift_b, lag = consts
    inv_a, inv_b = inv
    a = shift_a + td
    b = shift_b + td
    return (
        (a * ur + lag * ui - COUPLING * pr) * inv_a,
        (b * ui - lag * ur - COUPLING * pi) * inv_b,
        (TAU * ur + a * pr - lag * pi) * inv_a,
        (TAU * ui + b * pi + lag * pr) * inv_b,
    )


def over_sublanes(v):
    v = v + pltpu.roll(v, 4, 0)
    v = v + pltpu.roll(v, 2, 0)
    return v + pltpu.roll(v, 1, 0)


def front_body(own, wish, near, far, tnear, tfar, weights, consts, inv, fixed, it, out_near, out_far, zed):
    def field(p, j, c):
        if p == 2 or p == 3:
            return own[p - 2, j, c]
        side = near if p < 2 else far
        if p == 1 or p == 4:
            return side[(j - 1) * 4 + c]
        return side[72 + (j - 2) * 4 + c]

    def wanted(p, j, n):
        if p == 2 or p == 3:
            return wish[p - 2, j - 1, n]
        return (tnear if p == 1 else tfar)[136 + (j - 2) * 2 + n]

    cs = (consts[0], consts[1], consts[2])
    phase_a, phase_b, last_a, last_b, first_a, first_b, slot = (consts[i] for i in range(3, 10))
    for p, lo, hi in ((2, 1, 19), (3, 1, 19), (1, 2, 18), (4, 2, 18)):
        def row(j, carry, p=p):
            w = row_weights(weights, p, j, 8)
            v = [field(p, j, c) for c in range(4)]
            last = over_sublanes(last_a * v[0] + last_b * v[1])
            first = over_sublanes(first_a * v[2] + first_b * v[3])
            begin = w[7] - last
            kept = (
                begin,
                slot * begin,
                -TAU * wanted(p, j, 0) - phase_a * first,
                -TAU * wanted(p, j, 1) - phase_b * first,
            )
            at = region(p, j)
            pushed = []
            for c in range(4):
                fixed[at, c] = kept[c]
                around = (field(p + 1, j, c), field(p - 1, j, c), field(p, j + 1, c), field(p, j - 1, c))
                pushed.append(kept[c] + spread_sum(v[c], around, w))
            z = solve(pushed, w[6], (inv[at, 0], inv[at, 1]), cs)
            for c in range(4):
                zed[at, c] = z[c]
            return carry
        rows(lo, hi, row)

    for p in (2, 3):
        def row(j, carry, p=p):
            w = row_weights(weights, p, j, 8)
            at = region(p, j)
            pushed = []
            for c in range(4):
                around = (zed[region(p + 1, j), c], zed[region(p - 1, j), c], zed[at + 1, c], zed[at - 1, c])
                pushed.append(fixed[at, c] + spread_sum(zed[at, c], around, w))
            z = solve(pushed, w[6], (inv[at, 0], inv[at, 1]), cs)
            for c in range(4):
                it[p - 2, j - 2, c] = z[c]
            return carry
        rows(2, 18, row)
    out_near[0:14] = it[0, 1:15]
    out_near[14:26] = it[1, 2:14]
    out_far[0:14] = it[1, 1:15]
    out_far[14:26] = it[0, 2:14]


def sweep_body(it, near, far, fixed, weights, consts, inv, zed, put):
    def guess(p, j, c):
        if p == 2 or p == 3:
            return it[p - 2, j - 2, c]
        side = near if p < 2 else far
        if p == 1 or p == 4:
            return side[j - 3, c]
        return side[14 + j - 4, c]

    def at2(p, j):
        if p == 2 or p == 3:
            return (p - 2) * 14 + j - 3
        return (28 if p == 1 else 40) + j - 4

    cs = (consts[0], consts[1], consts[2])
    for p, lo, hi in ((2, 3, 17), (3, 3, 17), (1, 4, 16), (4, 4, 16)):
        def row(j, carry, p=p):
            w = row_weights(weights, p, j, 8)
            at = region(p, j)
            pushed = []
            for c in range(4):
                around = (guess(p + 1, j, c), guess(p - 1, j, c), guess(p, j + 1, c), guess(p, j - 1, c))
                pushed.append(fixed[at, c] + spread_sum(guess(p, j, c), around, w))
            z = solve(pushed, w[6], (inv[at, 0], inv[at, 1]), cs)
            for c in range(4):
                zed[at2(p, j), c] = z[c]
            return carry
        rows(lo, hi, row)
    for p in (2, 3):
        def row(j, carry, p=p):
            w = row_weights(weights, p, j, 8)
            at = region(p, j)
            here = at2(p, j)
            pushed = []
            for c in range(4):
                around = (zed[at2(p + 1, j), c], zed[at2(p - 1, j), c], zed[here + 1, c], zed[here - 1, c])
                pushed.append(fixed[at, c] + spread_sum(zed[here, c], around, w))
            z = solve(pushed, w[6], (inv[at, 0], inv[at, 1]), cs)
            for c in range(4):
                put(p - 2, j - 4, c, z[c])
            return carry
        rows(4, 16, row)


def middle_body(it, near, far, fixed, weights, consts, inv, new, out_near, out_far, zed):
    def put(x, j, c, v):
        new[x, j, c] = v
        first, second = (out_near, out_far) if x == 0 else (out_far, out_near)
        first[j, c] = v
        second[OWN + j, c] = v
    sweep_body(it, near, far, fixed, weights, consts, inv, zed, put)


EDGE = ((0, 4), (4, 4), (8, 3), (11, 3), (14, 2), (16, 2))


def edges_body(pos, new, near, far, send0, send1):
    odd = pos[0] & 1
    planes = (
        lambda j, n: new[0, pl.ds(j, n)],
        lambda j, n: new[1, pl.ds(j, n)],
        lambda j, n: near[pl.ds(j, n)],
        lambda j, n: far[pl.ds(j, n)],
        lambda j, n: near[pl.ds(OWN + j, n)],
        lambda j, n: far[pl.ds(OWN + j, n)],
    )
    for take, (at, n) in zip(planes, EDGE):
        send0[at : at + n] = take((OWN - n) * (1 - odd), n)
        send1[at : at + n] = take((OWN - n) * odd, n)


def widen_body(pos, got1, got0, new, near_x, far_x, own, near, far):
    odd = pos[0] & 1
    for x in range(2):
        own[x, HALO : HALO + OWN] = new[x]
    for out, got in ((near, near_x), (far, far_x)):
        out[3 : 3 + OWN] = got[0:OWN]
        out[20 : 20 + OWN] = got[OWN : 2 * OWN]
    for got, high in ((got0, 1 - odd), (got1, odd)):
        own[0, pl.ds(16 * high, 4)] = got[0:4]
        own[1, pl.ds(16 * high, 4)] = got[4:8]
        near[pl.ds(15 * high, 3)] = got[8:11]
        far[pl.ds(15 * high, 3)] = got[11:14]
        near[pl.ds(18 + 14 * high, 2)] = got[14:16]
        far[pl.ds(18 + 14 * high, 2)] = got[16:18]


def last_body(pos, it, near, far, fixed, weights, consts, inv, back, *rest):
    outs, (zed, fin, stage) = rest[:8], rest[8:]
    def put(x, j, c, v):
        fin[x * OWN + j, c] = v
    sweep_body(it, near, far, fixed, weights, consts, inv, zed, put)
    t = pos[0]
    matrix = back[...]
    for low in range(0, 2 * OWN, 4):
        done = transform(matrix, fin[low : low + 4].reshape(128, 128))
        for i in range(4):
            x, j = divmod(low + i, OWN)
            for c in range(4):
                stage[pl.ds((c * 2 + x) * OWN + j, 8, stride=8 * OWN), :] = done[(i * 4 + c) * 8 : (i * 4 + c + 1) * 8]
    for k in range(8):
        outs[k][...] = stage[pl.ds(pl.multiple_of((t ^ k) * 8 * OWN, 8), 8 * OWN), :]


def unpack_body(pos, *rest):
    pieces, (state, adjoint), stage = rest[:8], rest[8:10], rest[10]
    t = pos[0]
    flip = pos[1]
    for k, piece in zip(ORDER + (0,), pieces):
        stage[t ^ k] = piece[...]
    for f, ref in enumerate((state, adjoint)):
        for n in range(2):
            for x in range(2):
                base = ((f * 2 + n) * 2 + x) * OWN
                for d in range(8):
                    ref[n, x ^ flip, OWN * d : OWN * (d + 1), :] = stage[d, base : base + OWN, :]


def exchange(pieces):
    count = lax.axis_size("tm")
    return [lax.ppermute(pieces[k], "tm", [(i, i ^ k) for i in range(count)]) for k in ORDER] + [pieces[0]]


def swap(block, axis, start):
    count = lax.axis_size(axis)
    route = []
    for i in range(start, count - 1, 2):
        route += [(i, i + 1), (i + 1, i)]
    return lax.ppermute(block, axis, route)


def on_device(state_guess, adjoint_guess, target, initial_state, diffusivity):
    t = lax.axis_index("tm").astype(jnp.int32)
    s = lax.axis_index("space").astype(jnp.int32)
    flip = s & 1
    pos = jnp.stack([t, flip, s])
    forward, back = (jnp.asarray(m) for m in transform_matrices())
    consts = jnp.asarray(mode_constants())

    arguments = (state_guess, adjoint_guess, target, diffusivity, initial_state, forward, back, consts)
    *pieces, near_c, far_c, here_c, forward, back, consts = call(
        pack_body,
        "pack",
        [whole(12 * WIN, 128)] * 8 + [whole(3, TALL, 128)] * 2 + [whole(4, TALL, 128)]
        + [whole(128, 128)] * 2 + [whole(10, 8, 128)],
        0,
        [pltpu.VMEM((8, 12 * WIN, 128), jnp.float32)]
        + [pltpu.VMEM((2, 2, 96, 128), jnp.float32)] * 3
        + [pltpu.VMEM((2, 96, 128), jnp.float32)] * 2
        + [pltpu.SemaphoreType.DMA((8,))],
        far_inputs=8,
    )(pos, *(pltpu.with_memory_space_constraint(a, pltpu.HBM) for a in arguments))
    got = exchange(pieces)
    own, wish, near, far = call(
        spread_body,
        "spread",
        [whole(2, WIN, 4, 8, 128), whole(2, 18, 2, 8, 128), whole(177, 8, 128), whole(177, 8, 128)],
        11,
        [pltpu.VMEM((8 * 12 * WIN, 128), jnp.float32)],
    )(pos, *got, near_c, far_c, forward)
    far = far_first = swap(far, "space", 0)
    near = near_first = swap(near, "space", 1)
    weights, inv = call(
        coefficient_body, "coefficients", [whole(4 * TALL * 8, 128), whole(68, 2, 8, 128)], 4
    )(pos, here_c, near, far, consts)
    weights = weights.reshape(4 * TALL, 8, 128)

    sweep_scratch = [pltpu.VMEM((52, 4, 8, 128), jnp.float32)]
    for outer in range(OUTER):
        fixed, it, near_z, far_z = call(
            front_body,
            "front",
            [whole(68, 4, 8, 128), whole(2, 16, 4, 8, 128), whole(26, 4, 8, 128), whole(26, 4, 8, 128)],
            9,
            [pltpu.VMEM((68, 4, 8, 128), jnp.float32)],
            scalars=0,
        )(own, wish, near, far, near_first, far_first, weights, consts, inv)
        far_z = swap(far_z, "space", 0)
        near_z = swap(near_z, "space", 1)
        if outer < OUTER - 1:
            new, near, far = call(
                middle_body,
                "middle",
                [whole(2, OWN, 4, 8, 128), whole(2 * OWN, 4, 8, 128), whole(2 * OWN, 4, 8, 128)],
                7,
                sweep_scratch,
                scalars=0,
            )(it, near_z, far_z, fixed, weights, consts, inv)
            far = swap(far, "space", 0)
            near = swap(near, "space", 1)
            send0, send1 = call(edges_body, "edges", [whole(18, 4, 8, 128)] * 2, 3)(pos, new, near, far)
            got1 = swap(send1, "tm", 1)
            got0 = swap(send0, "tm", 0)
            own, near, far = call(
                widen_body, "widen", [whole(2, WIN, 4, 8, 128), whole(34, 4, 8, 128), whole(34, 4, 8, 128)], 5
            )(pos, got1, got0, new, near, far)
            near = near.reshape(136, 8, 128)
            far = far.reshape(136, 8, 128)
    pieces = call(
        last_body,
        "last",
        [whole(8 * OWN, 128)] * 8,
        8,
        sweep_scratch + [pltpu.VMEM((2 * OWN, 4, 8, 128), jnp.float32), pltpu.VMEM((64 * OWN, 128), jnp.float32)],
    )(pos, it, near_z, far_z, fixed, weights, consts, inv, back)
    got = exchange(pieces)
    return tuple(
        call(
            unpack_body,
            "unpack",
            [whole(2, 2, 96, 128)] * 2,
            8,
            [pltpu.VMEM((8, 8 * OWN, 128), jnp.float32)],
        )(pos, *got)
    )


def solution(mesh):
    in_specs = (
        P("tm", "space", None, None),
        P("tm", "space", None, None),
        P("tm", "space", None, None),
        P("space", None, None),
        P("space", None, None),
    )
    out_specs = (P("tm", "space", None, None), P("tm", "space", None, None))
    return jax.shard_map(
        on_device, mesh=mesh, in_specs=in_specs, out_specs=out_specs, check_vma=False
    )
```

```python
import math

import jax
import jax.numpy as jnp
import numpy as np
from jax import lax
from jax.experimental import pallas as pl
from jax.experimental.pallas import tpu as pltpu
from jax.sharding import PartitionSpec as P

TAU = 0.25
COUPLING = 5.0
DET_SHIFT = 1.25
OUTER = 2

OWN = 12
HALO = 4
WIN = OWN + 2 * HALO
ORDER = (4, 2, 6, 5, 3, 7, 1)
CHIPS = (2, 1, 3)
TALL = 24


def transform_matrices():
    modes = np.arange(8)[:, None]
    steps = np.concatenate([np.arange(0, 16, 2), np.arange(1, 16, 2)])[None, :]
    angle = 2.0 * np.pi * ((modes * steps) % 16) / 16.0
    real, imag = np.cos(angle), -np.sin(angle)
    imag[0] = np.where(steps[0] % 2 == 0, 1.0, -1.0)
    forward = np.concatenate([real, imag], 0)
    back = forward.T.copy() / 8.0
    back[:, 0] /= 2.0
    back[:, 8] /= 2.0
    eye = np.eye(8)
    return np.kron(eye, forward).astype(np.float32), np.kron(eye, back).astype(np.float32)


def mode_constants():
    theta = 2.0 * np.pi * np.arange(8) / 16.0
    shift_a = 1.0 - np.cos(theta)
    shift_b = shift_a.copy()
    shift_b[0] = 2.0
    lag = np.sin(theta)
    phase_a, phase_b = np.cos(theta), np.sin(theta)
    phase_b[0] = -1.0
    share = np.where(np.arange(8) == 0, 1.0, 2.0) / 16.0
    last_a, last_b = share * np.cos(15.0 * theta), -share * np.sin(15.0 * theta)
    last_b[0] = -1.0 / 16.0
    first_a, first_b = share, np.where(np.arange(8) == 0, 1.0, 0.0) / 16.0
    slot = np.where(np.arange(8) == 0, 1.0, 0.0)
    kinds = [shift_a, shift_b, lag, phase_a, phase_b, last_a, last_b, first_a, first_b, slot]
    return (np.stack(kinds)[:, :, None] * np.ones((1, 1, 128))).astype(np.float32)


def whole(*shape):
    return jax.ShapeDtypeStruct(shape, jnp.float32)


def call(body, name, outs, n_in, scratch=(), scalars=1, far_inputs=0):
    vmem = pl.BlockSpec(memory_space=pltpu.VMEM)
    anywhere = pl.BlockSpec(memory_space=pltpu.HBM)
    smem = pl.BlockSpec(memory_space=pltpu.SMEM)
    return pl.pallas_call(
        body,
        name=name,
        out_shape=outs,
        in_specs=[smem] * scalars + [anywhere] * far_inputs + [vmem] * n_in,
        out_specs=[vmem] * len(outs),
        scratch_shapes=list(scratch),
        compiler_params=pltpu.CompilerParams(vmem_limit_bytes=16 * 1024 * 1024),
    )


def rows(lo, hi, body):
    lax.fori_loop(lo, hi, body, 0, unroll=True)


def pack_body(pos, *rest):
    sources, outs, (near, far, here), tables = rest[:8], rest[8:16], rest[16:19], rest[19:22]
    stage, held, sems = rest[22], rest[23:28], rest[28]
    copies = [pltpu.make_async_copy(sources[i], ref, sems.at[i]) for i, ref in enumerate(held + tables)]
    for copy in copies:
        copy.start()
    state, adjoint, target, kappa, begin = held
    t = pos[0]
    flip = pos[1]
    for f, ref in enumerate((state, adjoint, target)):
        copies[f].wait()
        for n in range(2):
            for x in range(2):
                base = ((f * 2 + n) * 2 + x) * WIN
                for d in range(8):
                    low = OWN * d - HALO
                    first, last = max(low, 0), min(low + WIN, 96)
                    stage[d, base + first - low : base + last - low, :] = ref[n, x ^ flip, first:last, :]
                    if first > low:
                        stage[d, base : base + first - low, :] = jnp.zeros((first - low, 128), jnp.float32)
                    if last < low + WIN:
                        stage[d, base + last - low : base + WIN, :] = jnp.zeros((low + WIN - last, 128), jnp.float32)
    for k in range(8):
        outs[k][...] = stage[t ^ k]
    for copy in copies[3:]:
        copy.wait()
    for d in range(8):
        @pl.when(t == d)
        def window(d=d):
            low = OWN * d - HALO
            first, last = max(low, 0), min(low + TALL, 96)
            parts = []
            for ref, x in ((kappa, 0), (kappa, 1), (begin, 0), (begin, 1)):
                v = ref[x ^ flip, first:last, :]
                if first > low:
                    v = jnp.concatenate([jnp.zeros((first - low, 128), jnp.float32), v], 0)
                if last < low + TALL:
                    v = jnp.concatenate([v, jnp.zeros((low + TALL - last, 128), jnp.float32)], 0)
                parts.append(v)
            for i, v in enumerate(parts):
                here[i] = v
            for i, q in enumerate((0, 1, 2)):
                near[i] = parts[q]
            for i, q in enumerate((1, 0, 3)):
                far[i] = parts[q]


def coefficient_body(pos, far, near, here, consts, weights, inv):
    t, flip, s = pos[0], pos[1], pos[2]
    near, far = ([side[168 + 3 * i : 171 + 3 * i].reshape(TALL, 128) for i in range(3)] for side in (near, far))
    kappa = [near[1], near[0], here[0], here[1], far[0], far[1]]
    for p in range(6):
        plane = jnp.where(flip == 1, 2 * s + 3 - p, 2 * s - 2 + p)
        kappa[p] = kappa[p] * jnp.where((plane >= 0) & (plane < 64), 1.0, 0.0)
    begin = [near[2], here[2], here[3], far[2]]
    lane = lax.broadcasted_iota(jnp.int32, (TALL, 128), 1)
    row = lax.broadcasted_iota(jnp.int32, (TALL, 128), 0) + (OWN * t - HALO)
    half = 0.5 * TAU
    for p in range(1, 5):
        plane = jnp.where(flip == 1, 2 * s + 3 - p, 2 * s - 2 + p)
        ahead = jnp.where(flip == 1, plane - 1, plane + 1)
        behind = jnp.where(flip == 1, plane + 1, plane - 1)
        real = jnp.where((plane >= 0) & (plane < 64), half, 0.0)
        to_ahead = jnp.where((ahead >= 0) & (ahead < 64), real, 0.0)
        to_behind = jnp.where((behind >= 0) & (behind < 64), real, 0.0)
        k = kappa[p]
        row_ok = (row >= 0) & (row < 96)
        xp = k + kappa[p + 1]
        xm = k + kappa[p - 1]
        yp = k + pltpu.roll(k, TALL - 1, 0)
        ym = k + pltpu.roll(k, 1, 0)
        zp = k + jnp.where(lane < 127, pltpu.roll(k, 127, 1), 0.0)
        zm = k + jnp.where(lane > 0, pltpu.roll(k, 1, 1), 0.0)
        kinds = [
            jnp.where(row_ok, xp * to_ahead, 0.0),
            jnp.where(row_ok, xm * to_behind, 0.0),
            jnp.where(row_ok & (row < 95), yp * real, 0.0),
            jnp.where(row_ok & (row > 0), ym * real, 0.0),
            jnp.where(row_ok & (lane < 127), zp * real, 0.0),
            jnp.where(row_ok & (lane > 0), zm * real, 0.0),
            half * (((xp + xm) + (yp + ym)) + (zp + zm)),
            begin[p - 1],
        ]
        for i, v in enumerate(kinds):
            weights[pl.ds((p - 1) * TALL * 8 + i, TALL, stride=8), :] = v
    ca, cb, lag = consts[0], consts[1], consts[2]
    base = lag * lag + DET_SHIFT
    for p, lo, hi in ((2, 1, 19), (3, 1, 19), (1, 2, 18), (4, 2, 18)):
        for j in range(lo, hi):
            td = jnp.broadcast_to(weights[pl.ds(((p - 1) * TALL + j) * 8 + 6, 1), :], (8, 128))
            a = ca + td
            b = cb + td
            at = region(p, j)
            inv[at, 0] = 1.0 / (a * a + base)
            inv[at, 1] = 1.0 / (b * b + base)


def spread_body(pos, *rest):
    pieces, (near_c, far_c, forward), (own, wish, near, far), stage = rest[:8], rest[8:11], rest[11:15], rest[15]
    for i in range(3):
        near[168 + 3 * i : 171 + 3 * i] = near_c[i].reshape(3, 8, 128)
        far[168 + 3 * i : 171 + 3 * i] = far_c[i].reshape(3, 8, 128)
    t = pos[0]
    rows = 12 * WIN
    for k, piece in zip(ORDER + (0,), pieces):
        stage[pl.ds(pl.multiple_of((t ^ k) * rows, 8), rows), :] = piece[...]

    def steps(f, n, x, j):
        return stage[pl.ds(((f * 2 + n) * 2 + x) * WIN + j, 8, stride=rows), :]

    matrix = forward[...]
    for x in range(2):
        for low in range(0, WIN, 4):
            block = [steps(f, n, x, low + i) for i in range(4) for f in range(2) for n in range(2)]
            done = transform(matrix, jnp.concatenate(block, 0))
            for i in range(4):
                for c in range(4):
                    v = done[(i * 4 + c) * 8 : (i * 4 + c + 1) * 8]
                    own[x, low + i, c] = v
                    put_field(near, far, x, low + i, c, v)
    cells = [(x, j) for x in range(2) for j in range(WIN)]
    for low in range(0, len(cells), 8):
        block = [steps(2, n, x, j) for x, j in cells[low : low + 8] for n in range(2)]
        done = transform(matrix, jnp.concatenate(block, 0))
        for i, (x, j) in enumerate(cells[low : low + 8]):
            for n in range(2):
                v = done[(i * 2 + n) * 8 : (i * 2 + n + 1) * 8]
                if 1 <= j <= 18:
                    wish[x, j - 1, n] = v
                if 2 <= j <= 17:
                    out = far if x == 1 else near
                    out[136 + (j - 2) * 2 + n] = v


def transform(matrix, block):
    return jnp.dot(matrix, block, precision=lax.Precision.HIGHEST, preferred_element_type=jnp.float32)


def put_field(near, far, x, j, c, v):
    first, second = (near, far) if x == 0 else (far, near)
    if 1 <= j <= 18:
        first[(j - 1) * 4 + c] = v
    if 2 <= j <= 17:
        second[72 + (j - 2) * 4 + c] = v


def region(p, j):
    if p == 2 or p == 3:
        return (p - 2) * 18 + j - 1
    return (36 if p == 1 else 52) + j - 2


def spread_sum(v, around, w):
    px, mx, py, my = around
    up = pltpu.roll(v, 127, 1)
    down = pltpu.roll(v, 1, 1)
    return ((w[0] * px + w[1] * mx) + (w[2] * py + w[3] * my)) + (w[4] * up + w[5] * down)


def row_weights(weights, p, j, count):
    tile = weights[(p - 1) * TALL + j]
    return [jnp.broadcast_to(tile[k : k + 1, :], (8, 128)) for k in range(count)]


def solve(right, td, inv, consts):
    ur, ui, pr, pi = right
    shift_a, shift_b, lag = consts
    inv_a, inv_b = inv
    a = shift_a + td
    b = shift_b + td
    return (
        (a * ur + lag * ui - COUPLING * pr) * inv_a,
        (b * ui - lag * ur - COUPLING * pi) * inv_b,
        (TAU * ur + a * pr - lag * pi) * inv_a,
        (TAU * ui + b * pi + lag * pr) * inv_b,
    )


def over_sublanes(v):
    v = v + pltpu.roll(v, 4, 0)
    v = v + pltpu.roll(v, 2, 0)
    return v + pltpu.roll(v, 1, 0)


def front_body(far, near, own, wish, tnear, tfar, weights, consts, inv, fixed, it, out_near, out_far, zed):
    def field(p, j, c):
        if p == 2 or p == 3:
            return own[p - 2, j, c]
        side = near if p < 2 else far
        if p == 1 or p == 4:
            return side[(j - 1) * 4 + c]
        return side[72 + (j - 2) * 4 + c]

    def wanted(p, j, n):
        if p == 2 or p == 3:
            return wish[p - 2, j - 1, n]
        return (tnear if p == 1 else tfar)[136 + (j - 2) * 2 + n]

    cs = (consts[0], consts[1], consts[2])
    phase_a, phase_b, last_a, last_b, first_a, first_b, slot = (consts[i] for i in range(3, 10))
    for p, lo, hi in ((2, 1, 19), (3, 1, 19), (1, 2, 18), (4, 2, 18)):
        def row(j, carry, p=p):
            w = row_weights(weights, p, j, 8)
            v = [field(p, j, c) for c in range(4)]
            last = over_sublanes(last_a * v[0] + last_b * v[1])
            first = over_sublanes(first_a * v[2] + first_b * v[3])
            begin = w[7] - last
            kept = (
                begin,
                slot * begin,
                -TAU * wanted(p, j, 0) - phase_a * first,
                -TAU * wanted(p, j, 1) - phase_b * first,
            )
            at = region(p, j)
            pushed = []
            for c in range(4):
                fixed[at, c] = kept[c]
                around = (field(p + 1, j, c), field(p - 1, j, c), field(p, j + 1, c), field(p, j - 1, c))
                pushed.append(kept[c] + spread_sum(v[c], around, w))
            z = solve(pushed, w[6], (inv[at, 0], inv[at, 1]), cs)
            for c in range(4):
                zed[at, c] = z[c]
            return carry
        rows(lo, hi, row)

    for p in (2, 3):
        def row(j, carry, p=p):
            w = row_weights(weights, p, j, 8)
            at = region(p, j)
            pushed = []
            for c in range(4):
                around = (zed[region(p + 1, j), c], zed[region(p - 1, j), c], zed[at + 1, c], zed[at - 1, c])
                pushed.append(fixed[at, c] + spread_sum(zed[at, c], around, w))
            z = solve(pushed, w[6], (inv[at, 0], inv[at, 1]), cs)
            for c in range(4):
                it[p - 2, j - 2, c] = z[c]
            return carry
        rows(2, 18, row)
    out_near[0:14] = it[0, 1:15]
    out_near[14:26] = it[1, 2:14]
    out_far[0:14] = it[1, 1:15]
    out_far[14:26] = it[0, 2:14]


def sweep_body(it, near, far, fixed, weights, consts, inv, zed, put):
    def guess(p, j, c):
        if p == 2 or p == 3:
            return it[p - 2, j - 2, c]
        side = near if p < 2 else far
        if p == 1 or p == 4:
            return side[j - 3, c]
        return side[14 + j - 4, c]

    def at2(p, j):
        if p == 2 or p == 3:
            return (p - 2) * 14 + j - 3
        return (28 if p == 1 else 40) + j - 4

    cs = (consts[0], consts[1], consts[2])
    for p, lo, hi in ((2, 3, 17), (3, 3, 17), (1, 4, 16), (4, 4, 16)):
        def row(j, carry, p=p):
            w = row_weights(weights, p, j, 8)
            at = region(p, j)
            pushed = []
            for c in range(4):
                around = (guess(p + 1, j, c), guess(p - 1, j, c), guess(p, j + 1, c), guess(p, j - 1, c))
                pushed.append(fixed[at, c] + spread_sum(guess(p, j, c), around, w))
            z = solve(pushed, w[6], (inv[at, 0], inv[at, 1]), cs)
            for c in range(4):
                zed[at2(p, j), c] = z[c]
            return carry
        rows(lo, hi, row)
    for p in (2, 3):
        def row(j, carry, p=p):
            w = row_weights(weights, p, j, 8)
            at = region(p, j)
            here = at2(p, j)
            pushed = []
            for c in range(4):
                around = (zed[at2(p + 1, j), c], zed[at2(p - 1, j), c], zed[here + 1, c], zed[here - 1, c])
                pushed.append(fixed[at, c] + spread_sum(zed[here, c], around, w))
            z = solve(pushed, w[6], (inv[at, 0], inv[at, 1]), cs)
            for c in range(4):
                put(p - 2, j - 4, c, z[c])
            return carry
        rows(4, 16, row)


def middle_body(far, near, it, fixed, weights, consts, inv, new, out_near, out_far, zed):
    def put(x, j, c, v):
        new[x, j, c] = v
        first, second = (out_near, out_far) if x == 0 else (out_far, out_near)
        first[j, c] = v
        second[OWN + j, c] = v
    sweep_body(it, near, far, fixed, weights, consts, inv, zed, put)


EDGE = ((0, 4), (4, 4), (8, 3), (11, 3), (14, 2), (16, 2))


def edges_body(pos, far, near, new, send0, send1):
    odd = pos[0] & 1
    planes = (
        lambda j, n: new[0, pl.ds(j, n)],
        lambda j, n: new[1, pl.ds(j, n)],
        lambda j, n: near[pl.ds(j, n)],
        lambda j, n: far[pl.ds(j, n)],
        lambda j, n: near[pl.ds(OWN + j, n)],
        lambda j, n: far[pl.ds(OWN + j, n)],
    )
    for take, (at, n) in zip(planes, EDGE):
        send0[at : at + n] = take((OWN - n) * (1 - odd), n)
        send1[at : at + n] = take((OWN - n) * odd, n)


def widen_body(pos, got1, got0, new, near_x, far_x, own, near, far):
    odd = pos[0] & 1
    for x in range(2):
        own[x, HALO : HALO + OWN] = new[x]
    for out, got in ((near, near_x), (far, far_x)):
        out[3 : 3 + OWN] = got[0:OWN]
        out[20 : 20 + OWN] = got[OWN : 2 * OWN]
    for got, high in ((got0, 1 - odd), (got1, odd)):
        own[0, pl.ds(16 * high, 4)] = got[0:4]
        own[1, pl.ds(16 * high, 4)] = got[4:8]
        near[pl.ds(15 * high, 3)] = got[8:11]
        far[pl.ds(15 * high, 3)] = got[11:14]
        near[pl.ds(18 + 14 * high, 2)] = got[14:16]
        far[pl.ds(18 + 14 * high, 2)] = got[16:18]


def last_body(pos, far, near, it, fixed, weights, consts, inv, back, *rest):
    outs, (zed, fin, stage) = rest[:2], rest[2:]
    def put(x, j, c, v):
        fin[x * OWN + j, c] = v
    sweep_body(it, near, far, fixed, weights, consts, inv, zed, put)
    t = pos[0]
    matrix = back[...]
    for low in range(0, 2 * OWN, 4):
        done = transform(matrix, fin[low : low + 4].reshape(128, 128))
        for i in range(4):
            x, j = divmod(low + i, OWN)
            for c in range(4):
                stage[pl.ds((c * 2 + x) * OWN + j, 8, stride=8 * OWN), :] = done[(i * 4 + c) * 8 : (i * 4 + c + 1) * 8]
    for k in range(8):
        outs[k & 1][k >> 1] = stage[pl.ds(pl.multiple_of((t ^ k) * 8 * OWN, 8), 8 * OWN), :]


def merge_body(other, mine, *outs):
    for out, k in zip(outs, CHIPS):
        out[0] = mine[k]
        out[1] = other[k]


def unpack_body(pos, a, b, c, other, mine, state, adjoint, stage):
    t = pos[0]
    flip = pos[1]
    for ref, k in zip((a, b, c), CHIPS):
        stage[t ^ (2 * k)] = ref[0]
        stage[t ^ (2 * k + 1)] = ref[1]
    stage[t] = mine[0]
    stage[t ^ 1] = other[0]
    for f, ref in enumerate((state, adjoint)):
        for n in range(2):
            for x in range(2):
                base = ((f * 2 + n) * 2 + x) * OWN
                for d in range(8):
                    ref[n, x ^ flip, OWN * d : OWN * (d + 1), :] = stage[d, base : base + OWN, :]


def exchange(pieces):
    count = lax.axis_size("tm")
    return [lax.ppermute(pieces[k], "tm", [(i, i ^ k) for i in range(count)]) for k in ORDER] + [pieces[0]]


def swap(block, axis, start):
    count = lax.axis_size(axis)
    route = []
    for i in range(start, start + count, 2):
        low, high = i % count, (i + 1) % count
        route += [(low, high), (high, low)]
    return lax.ppermute(block, axis, route)


def on_device(state_guess, adjoint_guess, target, initial_state, diffusivity):
    t = lax.axis_index("tm").astype(jnp.int32)
    s = lax.axis_index("space").astype(jnp.int32)
    flip = s & 1
    pos = jnp.stack([t, flip, s])
    forward, back = (jnp.asarray(m) for m in transform_matrices())
    consts = jnp.asarray(mode_constants())

    arguments = (state_guess, adjoint_guess, target, diffusivity, initial_state, forward, back, consts)
    *pieces, near_c, far_c, here_c, forward, back, consts = call(
        pack_body,
        "pack",
        [whole(12 * WIN, 128)] * 8 + [whole(3, TALL, 128)] * 2 + [whole(4, TALL, 128)]
        + [whole(128, 128)] * 2 + [whole(10, 8, 128)],
        0,
        [pltpu.VMEM((8, 12 * WIN, 128), jnp.float32)]
        + [pltpu.VMEM((2, 2, 96, 128), jnp.float32)] * 3
        + [pltpu.VMEM((2, 96, 128), jnp.float32)] * 2
        + [pltpu.SemaphoreType.DMA((8,))],
        far_inputs=8,
    )(pos, *(pltpu.with_memory_space_constraint(a, pltpu.HBM) for a in arguments))
    got = exchange(pieces)
    own, wish, near, far = call(
        spread_body,
        "spread",
        [whole(2, WIN, 4, 8, 128), whole(2, 18, 2, 8, 128), whole(177, 8, 128), whole(177, 8, 128)],
        11,
        [pltpu.VMEM((8 * 12 * WIN, 128), jnp.float32)],
    )(pos, *got, near_c, far_c, forward)
    far = far_first = swap(far, "space", 0)
    near = near_first = swap(near, "space", 1)
    weights, inv = call(
        coefficient_body, "coefficients", [whole(4 * TALL * 8, 128), whole(68, 2, 8, 128)], 4
    )(pos, far, near, here_c, consts)
    weights = weights.reshape(4 * TALL, 8, 128)

    sweep_scratch = [pltpu.VMEM((52, 4, 8, 128), jnp.float32)]
    for outer in range(OUTER):
        fixed, it, near_z, far_z = call(
            front_body,
            "front",
            [whole(68, 4, 8, 128), whole(2, 16, 4, 8, 128), whole(26, 4, 8, 128), whole(26, 4, 8, 128)],
            9,
            [pltpu.VMEM((68, 4, 8, 128), jnp.float32)],
            scalars=0,
        )(far, near, own, wish, near_first, far_first, weights, consts, inv)
        far_z = swap(far_z, "space", 0)
        near_z = swap(near_z, "space", 1)
        if outer < OUTER - 1:
            new, near, far = call(
                middle_body,
                "middle",
                [whole(2, OWN, 4, 8, 128), whole(2 * OWN, 4, 8, 128), whole(2 * OWN, 4, 8, 128)],
                7,
                sweep_scratch,
                scalars=0,
            )(far_z, near_z, it, fixed, weights, consts, inv)
            far = swap(far, "space", 0)
            near = swap(near, "space", 1)
            send0, send1 = call(edges_body, "edges", [whole(18, 4, 8, 128)] * 2, 3)(pos, far, near, new)
            got1 = swap(send1, "tm", 1)
            got0 = swap(send0, "tm", 0)
            own, near, far = call(
                widen_body, "widen", [whole(2, WIN, 4, 8, 128), whole(34, 4, 8, 128), whole(34, 4, 8, 128)], 5
            )(pos, got1, got0, new, near, far)
            near = near.reshape(136, 8, 128)
            far = far.reshape(136, 8, 128)
    mine, other = call(
        last_body,
        "last",
        [whole(4, 8 * OWN, 128)] * 2,
        8,
        sweep_scratch + [pltpu.VMEM((2 * OWN, 4, 8, 128), jnp.float32), pltpu.VMEM((64 * OWN, 128), jnp.float32)],
    )(pos, far_z, near_z, it, fixed, weights, consts, inv, back)
    other = swap(other, "tm", 0)
    pairs = call(merge_body, "merge", [whole(2, 8 * OWN, 128)] * 3, 2, scalars=0)(other, mine)
    count = lax.axis_size("tm")
    got = [
        lax.ppermute(pair, "tm", [(i, i ^ (2 * k)) for i in range(count)]) for pair, k in zip(pairs, CHIPS)
    ]
    return tuple(
        call(
            unpack_body,
            "unpack",
            [whole(2, 2, 96, 128)] * 2,
            5,
            [pltpu.VMEM((8, 8 * OWN, 128), jnp.float32)],
        )(pos, *got, other, mine)
    )


def solution(mesh):
    in_specs = (
        P("tm", "space", None, None),
        P("tm", "space", None, None),
        P("tm", "space", None, None),
        P("space", None, None),
        P("space", None, None),
    )
    out_specs = (P("tm", "space", None, None), P("tm", "space", None, None))
    return jax.shard_map(
        on_device, mesh=mesh, in_specs=in_specs, out_specs=out_specs, check_vma=False
    )
```

```python
import math

import jax
import jax.numpy as jnp
import numpy as np
from jax import lax
from jax.experimental import pallas as pl
from jax.experimental.pallas import tpu as pltpu
from jax.sharding import PartitionSpec as P

TAU = 0.25
COUPLING = 5.0
DET_SHIFT = 1.25
OUTER = 2

OWN = 12
HALO = 4
WIN = OWN + 2 * HALO
ORDER = (4, 2, 6, 5, 3, 7, 1)
CHIPS = (2, 1, 3)
TALL = 24


def transform_matrices():
    modes = np.arange(8)[:, None]
    steps = np.concatenate([np.arange(0, 16, 2), np.arange(1, 16, 2)])[None, :]
    angle = 2.0 * np.pi * ((modes * steps) % 16) / 16.0
    real, imag = np.cos(angle), -np.sin(angle)
    imag[0] = np.where(steps[0] % 2 == 0, 1.0, -1.0)
    forward = np.concatenate([real, imag], 0)
    back = forward.T.copy() / 8.0
    back[:, 0] /= 2.0
    back[:, 8] /= 2.0
    eye = np.eye(8)
    return np.kron(eye, forward).astype(np.float32), np.kron(eye, back).astype(np.float32)


def mode_constants():
    theta = 2.0 * np.pi * np.arange(8) / 16.0
    shift_a = 1.0 - np.cos(theta)
    shift_b = shift_a.copy()
    shift_b[0] = 2.0
    lag = np.sin(theta)
    phase_a, phase_b = np.cos(theta), np.sin(theta)
    phase_b[0] = -1.0
    share = np.where(np.arange(8) == 0, 1.0, 2.0) / 16.0
    last_a, last_b = share * np.cos(15.0 * theta), -share * np.sin(15.0 * theta)
    last_b[0] = -1.0 / 16.0
    first_a, first_b = share, np.where(np.arange(8) == 0, 1.0, 0.0) / 16.0
    slot = np.where(np.arange(8) == 0, 1.0, 0.0)
    kinds = [shift_a, shift_b, lag, phase_a, phase_b, last_a, last_b, first_a, first_b, slot]
    return (np.stack(kinds)[:, :, None] * np.ones((1, 1, 128))).astype(np.float32)


def whole(*shape):
    return jax.ShapeDtypeStruct(shape, jnp.float32)


def call(body, name, outs, n_in, scratch=(), scalars=1, far_inputs=0, far_outputs=False):
    vmem = pl.BlockSpec(memory_space=pltpu.VMEM)
    anywhere = pl.BlockSpec(memory_space=pltpu.HBM)
    smem = pl.BlockSpec(memory_space=pltpu.SMEM)
    return pl.pallas_call(
        body,
        name=name,
        out_shape=outs,
        in_specs=[smem] * scalars + [anywhere] * far_inputs + [vmem] * n_in,
        out_specs=[anywhere if far_outputs else vmem] * len(outs),
        scratch_shapes=list(scratch),
        compiler_params=pltpu.CompilerParams(vmem_limit_bytes=16 * 1024 * 1024),
    )


def rows(lo, hi, body):
    lax.fori_loop(lo, hi, body, 0, unroll=True)


def pack_body(pos, *rest):
    sources, outs, (near, far, here), tables = rest[:8], rest[8:16], rest[16:19], rest[19:22]
    stage, held, sems = rest[22], rest[23:28], rest[28]
    slabs = [
        pltpu.make_async_copy(sources[f].at[n], held[f].at[n], sems.at[2 * f + n]) for f in range(3) for n in range(2)
    ]
    copies = [pltpu.make_async_copy(sources[3 + i], ref, sems.at[6 + i]) for i, ref in enumerate(held[3:] + tables)]
    for copy in slabs + copies:
        copy.start()
    state, adjoint, target, kappa, begin = held
    t = pos[0]
    flip = pos[1]
    for f, ref in enumerate((state, adjoint, target)):
        for n in range(2):
            slabs[2 * f + n].wait()
            for x in range(2):
                base = ((f * 2 + n) * 2 + x) * WIN
                for d in range(8):
                    low = OWN * d - HALO
                    first, last = max(low, 0), min(low + WIN, 96)
                    stage[d, base + first - low : base + last - low, :] = ref[n, x ^ flip, first:last, :]
                    if first > low:
                        stage[d, base : base + first - low, :] = jnp.zeros((first - low, 128), jnp.float32)
                    if last < low + WIN:
                        stage[d, base + last - low : base + WIN, :] = jnp.zeros((low + WIN - last, 128), jnp.float32)
    for k in range(8):
        outs[k][...] = stage[t ^ k]
    for copy in copies:
        copy.wait()
    for d in range(8):
        @pl.when(t == d)
        def window(d=d):
            low = OWN * d - HALO
            first, last = max(low, 0), min(low + TALL, 96)
            parts = []
            for ref, x in ((kappa, 0), (kappa, 1), (begin, 0), (begin, 1)):
                v = ref[x ^ flip, first:last, :]
                if first > low:
                    v = jnp.concatenate([jnp.zeros((first - low, 128), jnp.float32), v], 0)
                if last < low + TALL:
                    v = jnp.concatenate([v, jnp.zeros((low + TALL - last, 128), jnp.float32)], 0)
                parts.append(v)
            for i, v in enumerate(parts):
                here[i] = v
            for i, q in enumerate((0, 1, 2)):
                near[i] = parts[q]
            for i, q in enumerate((1, 0, 3)):
                far[i] = parts[q]


def coefficient_body(pos, far, near, here, consts, weights, inv):
    t, flip, s = pos[0], pos[1], pos[2]
    near, far = ([side[168 + 3 * i : 171 + 3 * i].reshape(TALL, 128) for i in range(3)] for side in (near, far))
    kappa = [near[1], near[0], here[0], here[1], far[0], far[1]]
    for p in range(6):
        plane = jnp.where(flip == 1, 2 * s + 3 - p, 2 * s - 2 + p)
        kappa[p] = kappa[p] * jnp.where((plane >= 0) & (plane < 64), 1.0, 0.0)
    begin = [near[2], here[2], here[3], far[2]]
    lane = lax.broadcasted_iota(jnp.int32, (TALL, 128), 1)
    row = lax.broadcasted_iota(jnp.int32, (TALL, 128), 0) + (OWN * t - HALO)
    half = 0.5 * TAU
    for p in range(1, 5):
        plane = jnp.where(flip == 1, 2 * s + 3 - p, 2 * s - 2 + p)
        ahead = jnp.where(flip == 1, plane - 1, plane + 1)
        behind = jnp.where(flip == 1, plane + 1, plane - 1)
        real = jnp.where((plane >= 0) & (plane < 64), half, 0.0)
        to_ahead = jnp.where((ahead >= 0) & (ahead < 64), real, 0.0)
        to_behind = jnp.where((behind >= 0) & (behind < 64), real, 0.0)
        k = kappa[p]
        row_ok = (row >= 0) & (row < 96)
        xp = k + kappa[p + 1]
        xm = k + kappa[p - 1]
        yp = k + pltpu.roll(k, TALL - 1, 0)
        ym = k + pltpu.roll(k, 1, 0)
        zp = k + jnp.where(lane < 127, pltpu.roll(k, 127, 1), 0.0)
        zm = k + jnp.where(lane > 0, pltpu.roll(k, 1, 1), 0.0)
        kinds = [
            jnp.where(row_ok, xp * to_ahead, 0.0),
            jnp.where(row_ok, xm * to_behind, 0.0),
            jnp.where(row_ok & (row < 95), yp * real, 0.0),
            jnp.where(row_ok & (row > 0), ym * real, 0.0),
            jnp.where(row_ok & (lane < 127), zp * real, 0.0),
            jnp.where(row_ok & (lane > 0), zm * real, 0.0),
            half * (((xp + xm) + (yp + ym)) + (zp + zm)),
            begin[p - 1],
        ]
        for i, v in enumerate(kinds):
            weights[pl.ds((p - 1) * TALL * 8 + i, TALL, stride=8), :] = v
    ca, cb, lag = consts[0], consts[1], consts[2]
    base = lag * lag + DET_SHIFT
    for p, lo, hi in ((2, 1, 19), (3, 1, 19), (1, 2, 18), (4, 2, 18)):
        for j in range(lo, hi):
            td = jnp.broadcast_to(weights[pl.ds(((p - 1) * TALL + j) * 8 + 6, 1), :], (8, 128))
            a = ca + td
            b = cb + td
            at = region(p, j)
            inv[at, 0] = 1.0 / (a * a + base)
            inv[at, 1] = 1.0 / (b * b + base)


def spread_body(pos, *rest):
    pieces, (near_c, far_c, forward), (own, wish, near, far), stage = rest[:8], rest[8:11], rest[11:15], rest[15]
    for i in range(3):
        near[168 + 3 * i : 171 + 3 * i] = near_c[i].reshape(3, 8, 128)
        far[168 + 3 * i : 171 + 3 * i] = far_c[i].reshape(3, 8, 128)
    t = pos[0]
    rows = 12 * WIN
    for k, piece in zip(ORDER + (0,), pieces):
        stage[pl.ds(pl.multiple_of((t ^ k) * rows, 8), rows), :] = piece[...]

    def steps(f, n, x, j):
        return stage[pl.ds(((f * 2 + n) * 2 + x) * WIN + j, 8, stride=rows), :]

    matrix = forward[...]
    for x in range(2):
        for low in range(0, WIN, 4):
            block = [steps(f, n, x, low + i) for i in range(4) for f in range(2) for n in range(2)]
            done = transform(matrix, jnp.concatenate(block, 0))
            for i in range(4):
                for c in range(4):
                    v = done[(i * 4 + c) * 8 : (i * 4 + c + 1) * 8]
                    own[x, low + i, c] = v
                    put_field(near, far, x, low + i, c, v)
    cells = [(x, j) for x in range(2) for j in range(WIN)]
    for low in range(0, len(cells), 8):
        block = [steps(2, n, x, j) for x, j in cells[low : low + 8] for n in range(2)]
        done = transform(matrix, jnp.concatenate(block, 0))
        for i, (x, j) in enumerate(cells[low : low + 8]):
            for n in range(2):
                v = done[(i * 2 + n) * 8 : (i * 2 + n + 1) * 8]
                if 1 <= j <= 18:
                    wish[x, j - 1, n] = v
                if 2 <= j <= 17:
                    out = far if x == 1 else near
                    out[136 + (j - 2) * 2 + n] = v


def transform(matrix, block):
    return jnp.dot(matrix, block, precision=lax.Precision.HIGHEST, preferred_element_type=jnp.float32)


def put_field(near, far, x, j, c, v):
    first, second = (near, far) if x == 0 else (far, near)
    if 1 <= j <= 18:
        first[(j - 1) * 4 + c] = v
    if 2 <= j <= 17:
        second[72 + (j - 2) * 4 + c] = v


def region(p, j):
    if p == 2 or p == 3:
        return (p - 2) * 18 + j - 1
    return (36 if p == 1 else 52) + j - 2


def spread_sum(v, around, w):
    px, mx, py, my = around
    up = pltpu.roll(v, 127, 1)
    down = pltpu.roll(v, 1, 1)
    return ((w[0] * px + w[1] * mx) + (w[2] * py + w[3] * my)) + (w[4] * up + w[5] * down)


def row_weights(weights, p, j, count):
    tile = weights[(p - 1) * TALL + j]
    return [jnp.broadcast_to(tile[k : k + 1, :], (8, 128)) for k in range(count)]


def solve(right, td, inv, consts):
    ur, ui, pr, pi = right
    shift_a, shift_b, lag = consts
    inv_a, inv_b = inv
    a = shift_a + td
    b = shift_b + td
    return (
        (a * ur + lag * ui - COUPLING * pr) * inv_a,
        (b * ui - lag * ur - COUPLING * pi) * inv_b,
        (TAU * ur + a * pr - lag * pi) * inv_a,
        (TAU * ui + b * pi + lag * pr) * inv_b,
    )


def over_sublanes(v):
    v = v + pltpu.roll(v, 4, 0)
    v = v + pltpu.roll(v, 2, 0)
    return v + pltpu.roll(v, 1, 0)


def front_body(far, near, own, wish, tnear, tfar, weights, consts, inv, fixed, it, out_near, out_far, zed):
    def field(p, j, c):
        if p == 2 or p == 3:
            return own[p - 2, j, c]
        side = near if p < 2 else far
        if p == 1 or p == 4:
            return side[(j - 1) * 4 + c]
        return side[72 + (j - 2) * 4 + c]

    def wanted(p, j, n):
        if p == 2 or p == 3:
            return wish[p - 2, j - 1, n]
        return (tnear if p == 1 else tfar)[136 + (j - 2) * 2 + n]

    cs = (consts[0], consts[1], consts[2])
    phase_a, phase_b, last_a, last_b, first_a, first_b, slot = (consts[i] for i in range(3, 10))
    for p, lo, hi in ((2, 1, 19), (3, 1, 19), (1, 2, 18), (4, 2, 18)):
        def row(j, carry, p=p):
            w = row_weights(weights, p, j, 8)
            v = [field(p, j, c) for c in range(4)]
            last = over_sublanes(last_a * v[0] + last_b * v[1])
            first = over_sublanes(first_a * v[2] + first_b * v[3])
            begin = w[7] - last
            kept = (
                begin,
                slot * begin,
                -TAU * wanted(p, j, 0) - phase_a * first,
                -TAU * wanted(p, j, 1) - phase_b * first,
            )
            at = region(p, j)
            pushed = []
            for c in range(4):
                fixed[at, c] = kept[c]
                around = (field(p + 1, j, c), field(p - 1, j, c), field(p, j + 1, c), field(p, j - 1, c))
                pushed.append(kept[c] + spread_sum(v[c], around, w))
            z = solve(pushed, w[6], (inv[at, 0], inv[at, 1]), cs)
            for c in range(4):
                zed[at, c] = z[c]
            return carry
        rows(lo, hi, row)

    for p in (2, 3):
        def row(j, carry, p=p):
            w = row_weights(weights, p, j, 8)
            at = region(p, j)
            pushed = []
            for c in range(4):
                around = (zed[region(p + 1, j), c], zed[region(p - 1, j), c], zed[at + 1, c], zed[at - 1, c])
                pushed.append(fixed[at, c] + spread_sum(zed[at, c], around, w))
            z = solve(pushed, w[6], (inv[at, 0], inv[at, 1]), cs)
            for c in range(4):
                it[p - 2, j - 2, c] = z[c]
            return carry
        rows(2, 18, row)
    out_near[0:14] = it[0, 1:15]
    out_near[14:26] = it[1, 2:14]
    out_far[0:14] = it[1, 1:15]
    out_far[14:26] = it[0, 2:14]


def sweep_body(it, near, far, fixed, weights, consts, inv, zed, put):
    def guess(p, j, c):
        if p == 2 or p == 3:
            return it[p - 2, j - 2, c]
        side = near if p < 2 else far
        if p == 1 or p == 4:
            return side[j - 3, c]
        return side[14 + j - 4, c]

    def at2(p, j):
        if p == 2 or p == 3:
            return (p - 2) * 14 + j - 3
        return (28 if p == 1 else 40) + j - 4

    cs = (consts[0], consts[1], consts[2])
    for p, lo, hi in ((2, 3, 17), (3, 3, 17), (1, 4, 16), (4, 4, 16)):
        def row(j, carry, p=p):
            w = row_weights(weights, p, j, 8)
            at = region(p, j)
            pushed = []
            for c in range(4):
                around = (guess(p + 1, j, c), guess(p - 1, j, c), guess(p, j + 1, c), guess(p, j - 1, c))
                pushed.append(fixed[at, c] + spread_sum(guess(p, j, c), around, w))
            z = solve(pushed, w[6], (inv[at, 0], inv[at, 1]), cs)
            for c in range(4):
                zed[at2(p, j), c] = z[c]
            return carry
        rows(lo, hi, row)
    for p in (2, 3):
        def row(j, carry, p=p):
            w = row_weights(weights, p, j, 8)
            at = region(p, j)
            here = at2(p, j)
            pushed = []
            for c in range(4):
                around = (zed[at2(p + 1, j), c], zed[at2(p - 1, j), c], zed[here + 1, c], zed[here - 1, c])
                pushed.append(fixed[at, c] + spread_sum(zed[here, c], around, w))
            z = solve(pushed, w[6], (inv[at, 0], inv[at, 1]), cs)
            for c in range(4):
                put(p - 2, j - 4, c, z[c])
            return carry
        rows(4, 16, row)


def middle_body(far, near, it, fixed, weights, consts, inv, new, out_near, out_far, zed):
    def put(x, j, c, v):
        new[x, j, c] = v
        first, second = (out_near, out_far) if x == 0 else (out_far, out_near)
        first[j, c] = v
        second[OWN + j, c] = v
    sweep_body(it, near, far, fixed, weights, consts, inv, zed, put)


EDGE = ((0, 4), (4, 4), (8, 3), (11, 3), (14, 2), (16, 2))


def edges_body(pos, far, near, new, send0, send1):
    odd = pos[0] & 1
    planes = (
        lambda j, n: new[0, pl.ds(j, n)],
        lambda j, n: new[1, pl.ds(j, n)],
        lambda j, n: near[pl.ds(j, n)],
        lambda j, n: far[pl.ds(j, n)],
        lambda j, n: near[pl.ds(OWN + j, n)],
        lambda j, n: far[pl.ds(OWN + j, n)],
    )
    for take, (at, n) in zip(planes, EDGE):
        send0[at : at + n] = take((OWN - n) * (1 - odd), n)
        send1[at : at + n] = take((OWN - n) * odd, n)


def widen_body(pos, got1, got0, new, near_x, far_x, own, near, far):
    odd = pos[0] & 1
    for x in range(2):
        own[x, HALO : HALO + OWN] = new[x]
    for out, got in ((near, near_x), (far, far_x)):
        out[3 : 3 + OWN] = got[0:OWN]
        out[20 : 20 + OWN] = got[OWN : 2 * OWN]
    for got, high in ((got0, 1 - odd), (got1, odd)):
        own[0, pl.ds(16 * high, 4)] = got[0:4]
        own[1, pl.ds(16 * high, 4)] = got[4:8]
        near[pl.ds(15 * high, 3)] = got[8:11]
        far[pl.ds(15 * high, 3)] = got[11:14]
        near[pl.ds(18 + 14 * high, 2)] = got[14:16]
        far[pl.ds(18 + 14 * high, 2)] = got[16:18]


def last_body(pos, far, near, it, fixed, weights, consts, inv, back, *rest):
    outs, (zed, fin, stage) = rest[:2], rest[2:]
    def put(x, j, c, v):
        fin[x * OWN + j, c] = v
    sweep_body(it, near, far, fixed, weights, consts, inv, zed, put)
    t = pos[0]
    matrix = back[...]
    for low in range(0, 2 * OWN, 4):
        done = transform(matrix, fin[low : low + 4].reshape(128, 128))
        for i in range(4):
            x, j = divmod(low + i, OWN)
            for c in range(4):
                stage[pl.ds((c * 2 + x) * OWN + j, 8, stride=8 * OWN), :] = done[(i * 4 + c) * 8 : (i * 4 + c + 1) * 8]
    for k in range(8):
        outs[k & 1][k >> 1] = stage[pl.ds(pl.multiple_of((t ^ k) * 8 * OWN, 8), 8 * OWN), :]


def merge_body(other, mine, *outs):
    for out, k in zip(outs, CHIPS):
        out[0] = mine[k]
        out[1] = other[k]


def unpack_body(pos, a, b, c, other, mine, state, adjoint, stage, held, sems):
    t = pos[0]
    flip = pos[1]
    for ref, k in zip((a, b, c), CHIPS):
        stage[t ^ (2 * k)] = ref[0]
        stage[t ^ (2 * k + 1)] = ref[1]
    stage[t] = mine[0]
    stage[t ^ 1] = other[0]
    copies = []
    for f, ref in enumerate((state, adjoint)):
        for n in range(2):
            for x in range(2):
                base = ((f * 2 + n) * 2 + x) * OWN
                for d in range(8):
                    held[f, n, x, OWN * d : OWN * (d + 1), :] = stage[d, base : base + OWN, :]
                copies.append(
                    pltpu.make_async_copy(held.at[f, n, x], ref.at[n, x ^ flip], sems.at[(f * 2 + n) * 2 + x])
                )
                copies[-1].start()
    for copy in copies:
        copy.wait()


def exchange(pieces):
    count = lax.axis_size("tm")
    return [lax.ppermute(pieces[k], "tm", [(i, i ^ k) for i in range(count)]) for k in ORDER] + [pieces[0]]


def swap(block, axis, start):
    count = lax.axis_size(axis)
    route = [(i, i) for i in range(start)]
    for i in range(start, count - 1, 2):
        route += [(i, i + 1), (i + 1, i)]
    route += [(i, i) for i in range(len(route), count)]
    return lax.ppermute(block, axis, route)


def on_device(state_guess, adjoint_guess, target, initial_state, diffusivity):
    t = lax.axis_index("tm").astype(jnp.int32)
    s = lax.axis_index("space").astype(jnp.int32)
    flip = s & 1
    pos = jnp.stack([t, flip, s])
    forward, back = (jnp.asarray(m) for m in transform_matrices())
    consts = jnp.asarray(mode_constants())

    arguments = (state_guess, adjoint_guess, target, diffusivity, initial_state, forward, back, consts)
    *pieces, near_c, far_c, here_c, forward, back, consts = call(
        pack_body,
        "pack",
        [whole(12 * WIN, 128)] * 8 + [whole(3, TALL, 128)] * 2 + [whole(4, TALL, 128)]
        + [whole(128, 128)] * 2 + [whole(10, 8, 128)],
        0,
        [pltpu.VMEM((8, 12 * WIN, 128), jnp.float32)]
        + [pltpu.VMEM((2, 2, 96, 128), jnp.float32)] * 3
        + [pltpu.VMEM((2, 96, 128), jnp.float32)] * 2
        + [pltpu.SemaphoreType.DMA((11,))],
        far_inputs=8,
    )(pos, *(pltpu.with_memory_space_constraint(a, pltpu.HBM) for a in arguments))
    got = exchange(pieces)
    own, wish, near, far = call(
        spread_body,
        "spread",
        [whole(2, WIN, 4, 8, 128), whole(2, 18, 2, 8, 128), whole(177, 8, 128), whole(177, 8, 128)],
        11,
        [pltpu.VMEM((8 * 12 * WIN, 128), jnp.float32)],
    )(pos, *got, near_c, far_c, forward)
    far = far_first = swap(far, "space", 0)
    near = near_first = swap(near, "space", 1)
    weights, inv = call(
        coefficient_body, "coefficients", [whole(4 * TALL * 8, 128), whole(68, 2, 8, 128)], 4
    )(pos, far, near, here_c, consts)
    weights = weights.reshape(4 * TALL, 8, 128)

    sweep_scratch = [pltpu.VMEM((52, 4, 8, 128), jnp.float32)]
    for outer in range(OUTER):
        fixed, it, near_z, far_z = call(
            front_body,
            "front",
            [whole(68, 4, 8, 128), whole(2, 16, 4, 8, 128), whole(26, 4, 8, 128), whole(26, 4, 8, 128)],
            9,
            [pltpu.VMEM((68, 4, 8, 128), jnp.float32)],
            scalars=0,
        )(far, near, own, wish, near_first, far_first, weights, consts, inv)
        far_z = swap(far_z, "space", 0)
        near_z = swap(near_z, "space", 1)
        if outer < OUTER - 1:
            new, near, far = call(
                middle_body,
                "middle",
                [whole(2, OWN, 4, 8, 128), whole(2 * OWN, 4, 8, 128), whole(2 * OWN, 4, 8, 128)],
                7,
                sweep_scratch,
                scalars=0,
            )(far_z, near_z, it, fixed, weights, consts, inv)
            far = swap(far, "space", 0)
            near = swap(near, "space", 1)
            send0, send1 = call(edges_body, "edges", [whole(18, 4, 8, 128)] * 2, 3)(pos, far, near, new)
            got1 = swap(send1, "tm", 1)
            got0 = swap(send0, "tm", 0)
            own, near, far = call(
                widen_body, "widen", [whole(2, WIN, 4, 8, 128), whole(34, 4, 8, 128), whole(34, 4, 8, 128)], 5
            )(pos, got1, got0, new, near, far)
            near = near.reshape(136, 8, 128)
            far = far.reshape(136, 8, 128)
    mine, other = call(
        last_body,
        "last",
        [whole(4, 8 * OWN, 128)] * 2,
        8,
        sweep_scratch + [pltpu.VMEM((2 * OWN, 4, 8, 128), jnp.float32), pltpu.VMEM((64 * OWN, 128), jnp.float32)],
    )(pos, far_z, near_z, it, fixed, weights, consts, inv, back)
    other = swap(other, "tm", 0)
    pairs = call(merge_body, "merge", [whole(2, 8 * OWN, 128)] * 3, 2, scalars=0)(other, mine)
    count = lax.axis_size("tm")
    got = [
        lax.ppermute(pair, "tm", [(i, i ^ (2 * k)) for i in range(count)]) for pair, k in zip(pairs, CHIPS)
    ]
    return tuple(
        call(
            unpack_body,
            "unpack",
            [whole(2, 2, 96, 128)] * 2,
            5,
            [
                pltpu.VMEM((8, 8 * OWN, 128), jnp.float32),
                pltpu.VMEM((2, 2, 2, 96, 128), jnp.float32),
                pltpu.SemaphoreType.DMA((8,)),
            ],
            far_outputs=True,
        )(pos, *got, other, mine)
    )


def solution(mesh):
    in_specs = (
        P("tm", "space", None, None),
        P("tm", "space", None, None),
        P("tm", "space", None, None),
        P("space", None, None),
        P("space", None, None),
    )
    out_specs = (P("tm", "space", None, None), P("tm", "space", None, None))
    return jax.shard_map(
        on_device, mesh=mesh, in_specs=in_specs, out_specs=out_specs, check_vma=False
    )
```

```python
import math

import jax
import jax.numpy as jnp
import numpy as np
from jax import lax
from jax.experimental import pallas as pl
from jax.experimental.pallas import tpu as pltpu
from jax.sharding import PartitionSpec as P

TAU = 0.25
COUPLING = 5.0
DET_SHIFT = 1.25
OUTER = 2

OWN = 12
HALO = 4
WIN = OWN + 2 * HALO
ORDER = (4, 2, 6, 5, 3, 7, 1)
CHIPS = (2, 1, 3)
TALL = 24


def transform_matrices():
    modes = np.arange(8)[:, None]
    steps = np.concatenate([np.arange(0, 16, 2), np.arange(1, 16, 2)])[None, :]
    angle = 2.0 * np.pi * ((modes * steps) % 16) / 16.0
    real, imag = np.cos(angle), -np.sin(angle)
    imag[0] = np.where(steps[0] % 2 == 0, 1.0, -1.0)
    forward = np.concatenate([real, imag], 0)
    back = forward.T.copy() / 8.0
    back[:, 0] /= 2.0
    back[:, 8] /= 2.0
    eye = np.eye(8)
    return np.kron(eye, forward).astype(np.float32), np.kron(eye, back).astype(np.float32)


def mode_constants():
    theta = 2.0 * np.pi * np.arange(8) / 16.0
    shift_a = 1.0 - np.cos(theta)
    shift_b = shift_a.copy()
    shift_b[0] = 2.0
    lag = np.sin(theta)
    phase_a, phase_b = np.cos(theta), np.sin(theta)
    phase_b[0] = -1.0
    share = np.where(np.arange(8) == 0, 1.0, 2.0) / 16.0
    last_a, last_b = share * np.cos(15.0 * theta), -share * np.sin(15.0 * theta)
    last_b[0] = -1.0 / 16.0
    first_a, first_b = share, np.where(np.arange(8) == 0, 1.0, 0.0) / 16.0
    slot = np.where(np.arange(8) == 0, 1.0, 0.0)
    kinds = [shift_a, shift_b, lag, phase_a, phase_b, last_a, last_b, first_a, first_b, slot]
    return (np.stack(kinds)[:, :, None] * np.ones((1, 1, 128))).astype(np.float32)


def whole(*shape):
    return jax.ShapeDtypeStruct(shape, jnp.float32)


def call(body, name, outs, n_in, scratch=(), scalars=1, far_inputs=0, far_outputs=False):
    vmem = pl.BlockSpec(memory_space=pltpu.VMEM)
    anywhere = pl.BlockSpec(memory_space=pltpu.HBM)
    smem = pl.BlockSpec(memory_space=pltpu.SMEM)
    return pl.pallas_call(
        body,
        name=name,
        out_shape=outs,
        in_specs=[smem] * scalars + [anywhere] * far_inputs + [vmem] * n_in,
        out_specs=[anywhere if far_outputs else vmem] * len(outs),
        scratch_shapes=list(scratch),
        compiler_params=pltpu.CompilerParams(vmem_limit_bytes=16 * 1024 * 1024),
    )


def rows(lo, hi, body):
    lax.fori_loop(lo, hi, body, 0, unroll=True)


def pack_body(pos, *rest):
    sources, outs, (near, far, here), tables = rest[:8], rest[8:16], rest[16:19], rest[19:22]
    stage, held, sems = rest[22], rest[23:28], rest[28]
    slabs = [
        pltpu.make_async_copy(sources[f].at[n], held[f].at[n], sems.at[2 * f + n]) for f in range(3) for n in range(2)
    ]
    copies = [pltpu.make_async_copy(sources[3 + i], ref, sems.at[6 + i]) for i, ref in enumerate(held[3:] + tables)]
    for copy in slabs + copies:
        copy.start()
    state, adjoint, target, kappa, begin = held
    t = pos[0]
    flip = pos[1]
    for f, ref in enumerate((state, adjoint, target)):
        for n in range(2):
            slabs[2 * f + n].wait()
            for x in range(2):
                base = ((f * 2 + n) * 2 + x) * WIN
                for d in range(8):
                    low = OWN * d - HALO
                    first, last = max(low, 0), min(low + WIN, 96)
                    stage[d, base + first - low : base + last - low, :] = ref[n, x ^ flip, first:last, :]
                    if first > low:
                        stage[d, base : base + first - low, :] = jnp.zeros((first - low, 128), jnp.float32)
                    if last < low + WIN:
                        stage[d, base + last - low : base + WIN, :] = jnp.zeros((low + WIN - last, 128), jnp.float32)
    for k in range(8):
        outs[k][...] = stage[t ^ k]
    for copy in copies:
        copy.wait()
    for d in range(8):
        @pl.when(t == d)
        def window(d=d):
            low = OWN * d - HALO
            first, last = max(low, 0), min(low + TALL, 96)
            parts = []
            for ref, x in ((kappa, 0), (kappa, 1), (begin, 0), (begin, 1)):
                v = ref[x ^ flip, first:last, :]
                if first > low:
                    v = jnp.concatenate([jnp.zeros((first - low, 128), jnp.float32), v], 0)
                if last < low + TALL:
                    v = jnp.concatenate([v, jnp.zeros((low + TALL - last, 128), jnp.float32)], 0)
                parts.append(v)
            for i, v in enumerate(parts):
                here[i] = v
            for i, q in enumerate((0, 1, 2)):
                near[i] = parts[q]
            for i, q in enumerate((1, 0, 3)):
                far[i] = parts[q]


def coefficient_body(pos, far, near, here, consts, weights, inv):
    t, flip, s = pos[0], pos[1], pos[2]
    near, far = ([side[168 + 3 * i : 171 + 3 * i].reshape(TALL, 128) for i in range(3)] for side in (near, far))
    kappa = [near[1], near[0], here[0], here[1], far[0], far[1]]
    for p in range(6):
        plane = jnp.where(flip == 1, 2 * s + 3 - p, 2 * s - 2 + p)
        kappa[p] = kappa[p] * jnp.where((plane >= 0) & (plane < 64), 1.0, 0.0)
    begin = [near[2], here[2], here[3], far[2]]
    lane = lax.broadcasted_iota(jnp.int32, (TALL, 128), 1)
    row = lax.broadcasted_iota(jnp.int32, (TALL, 128), 0) + (OWN * t - HALO)
    half = 0.5 * TAU
    for p in range(1, 5):
        plane = jnp.where(flip == 1, 2 * s + 3 - p, 2 * s - 2 + p)
        ahead = jnp.where(flip == 1, plane - 1, plane + 1)
        behind = jnp.where(flip == 1, plane + 1, plane - 1)
        real = jnp.where((plane >= 0) & (plane < 64), half, 0.0)
        to_ahead = jnp.where((ahead >= 0) & (ahead < 64), real, 0.0)
        to_behind = jnp.where((behind >= 0) & (behind < 64), real, 0.0)
        k = kappa[p]
        row_ok = (row >= 0) & (row < 96)
        xp = k + kappa[p + 1]
        xm = k + kappa[p - 1]
        yp = k + pltpu.roll(k, TALL - 1, 0)
        ym = k + pltpu.roll(k, 1, 0)
        zp = k + jnp.where(lane < 127, pltpu.roll(k, 127, 1), 0.0)
        zm = k + jnp.where(lane > 0, pltpu.roll(k, 1, 1), 0.0)
        kinds = [
            jnp.where(row_ok, xp * to_ahead, 0.0),
            jnp.where(row_ok, xm * to_behind, 0.0),
            jnp.where(row_ok & (row < 95), yp * real, 0.0),
            jnp.where(row_ok & (row > 0), ym * real, 0.0),
            jnp.where(row_ok & (lane < 127), zp * real, 0.0),
            jnp.where(row_ok & (lane > 0), zm * real, 0.0),
            half * (((xp + xm) + (yp + ym)) + (zp + zm)),
            begin[p - 1],
        ]
        for i, v in enumerate(kinds):
            weights[pl.ds((p - 1) * TALL * 8 + i, TALL, stride=8), :] = v
    ca, cb, lag = consts[0], consts[1], consts[2]
    base = lag * lag + DET_SHIFT
    for p, lo, hi in ((2, 1, 19), (3, 1, 19), (1, 2, 18), (4, 2, 18)):
        for j in range(lo, hi):
            td = jnp.broadcast_to(weights[pl.ds(((p - 1) * TALL + j) * 8 + 6, 1), :], (8, 128))
            a = ca + td
            b = cb + td
            at = region(p, j)
            inv[at, 0] = 1.0 / (a * a + base)
            inv[at, 1] = 1.0 / (b * b + base)


def spread_body(pos, *rest):
    pieces, (near_c, far_c, forward), (own, wish, near, far), stage = rest[:8], rest[8:11], rest[11:15], rest[15]
    for i in range(3):
        near[168 + 3 * i : 171 + 3 * i] = near_c[i].reshape(3, 8, 128)
        far[168 + 3 * i : 171 + 3 * i] = far_c[i].reshape(3, 8, 128)
    t = pos[0]
    rows = 12 * WIN
    for k, piece in zip(ORDER + (0,), pieces):
        stage[pl.ds(pl.multiple_of((t ^ k) * rows, 8), rows), :] = piece[...]

    def steps(f, n, x, j):
        return stage[pl.ds(((f * 2 + n) * 2 + x) * WIN + j, 8, stride=rows), :]

    matrix = forward[...]
    for x in range(2):
        for low in range(0, WIN, 4):
            block = [steps(f, n, x, low + i) for i in range(4) for f in range(2) for n in range(2)]
            done = transform(matrix, jnp.concatenate(block, 0))
            for i in range(4):
                for c in range(4):
                    v = done[(i * 4 + c) * 8 : (i * 4 + c + 1) * 8]
                    own[x, low + i, c] = v
                    put_field(near, far, x, low + i, c, v)
    cells = [(x, j) for x in range(2) for j in range(WIN)]
    for low in range(0, len(cells), 8):
        block = [steps(2, n, x, j) for x, j in cells[low : low + 8] for n in range(2)]
        done = transform(matrix, jnp.concatenate(block, 0))
        for i, (x, j) in enumerate(cells[low : low + 8]):
            for n in range(2):
                v = done[(i * 2 + n) * 8 : (i * 2 + n + 1) * 8]
                if 1 <= j <= 18:
                    wish[x, j - 1, n] = v
                if 2 <= j <= 17:
                    out = far if x == 1 else near
                    out[136 + (j - 2) * 2 + n] = v


def transform(matrix, block):
    return jnp.dot(matrix, block, precision=lax.Precision.HIGHEST, preferred_element_type=jnp.float32)


def put_field(near, far, x, j, c, v):
    first, second = (near, far) if x == 0 else (far, near)
    if 1 <= j <= 18:
        first[(j - 1) * 4 + c] = v
    if 2 <= j <= 17:
        second[72 + (j - 2) * 4 + c] = v


def region(p, j):
    if p == 2 or p == 3:
        return (p - 2) * 18 + j - 1
    return (36 if p == 1 else 52) + j - 2


def spread_sum(v, around, w):
    px, mx, py, my = around
    up = pltpu.roll(v, 127, 1)
    down = pltpu.roll(v, 1, 1)
    return ((w[0] * px + w[1] * mx) + (w[2] * py + w[3] * my)) + (w[4] * up + w[5] * down)


def row_weights(weights, p, j, count):
    tile = weights[(p - 1) * TALL + j]
    return [jnp.broadcast_to(tile[k : k + 1, :], (8, 128)) for k in range(count)]


def solve(right, td, inv, consts):
    ur, ui, pr, pi = right
    shift_a, shift_b, lag = consts
    inv_a, inv_b = inv
    a = shift_a + td
    b = shift_b + td
    return (
        (a * ur + lag * ui - COUPLING * pr) * inv_a,
        (b * ui - lag * ur - COUPLING * pi) * inv_b,
        (TAU * ur + a * pr - lag * pi) * inv_a,
        (TAU * ui + b * pi + lag * pr) * inv_b,
    )


def over_sublanes(v):
    v = v + pltpu.roll(v, 4, 0)
    v = v + pltpu.roll(v, 2, 0)
    return v + pltpu.roll(v, 1, 0)


def front_body(far, near, own, wish, tnear, tfar, weights, consts, inv, fixed, it, out_near, out_far, zed):
    def field(p, j, c):
        if p == 2 or p == 3:
            return own[p - 2, j, c]
        side = near if p < 2 else far
        if p == 1 or p == 4:
            return side[(j - 1) * 4 + c]
        return side[72 + (j - 2) * 4 + c]

    def wanted(p, j, n):
        if p == 2 or p == 3:
            return wish[p - 2, j - 1, n]
        return (tnear if p == 1 else tfar)[136 + (j - 2) * 2 + n]

    cs = (consts[0], consts[1], consts[2])
    phase_a, phase_b, last_a, last_b, first_a, first_b, slot = (consts[i] for i in range(3, 10))
    for p, lo, hi in ((2, 1, 19), (3, 1, 19), (1, 2, 18), (4, 2, 18)):
        def row(j, carry, p=p):
            w = row_weights(weights, p, j, 8)
            v = [field(p, j, c) for c in range(4)]
            last = over_sublanes(last_a * v[0] + last_b * v[1])
            first = over_sublanes(first_a * v[2] + first_b * v[3])
            begin = w[7] - last
            kept = (
                begin,
                slot * begin,
                -TAU * wanted(p, j, 0) - phase_a * first,
                -TAU * wanted(p, j, 1) - phase_b * first,
            )
            at = region(p, j)
            pushed = []
            for c in range(4):
                fixed[at, c] = kept[c]
                around = (field(p + 1, j, c), field(p - 1, j, c), field(p, j + 1, c), field(p, j - 1, c))
                pushed.append(kept[c] + spread_sum(v[c], around, w))
            z = solve(pushed, w[6], (inv[at, 0], inv[at, 1]), cs)
            for c in range(4):
                zed[at, c] = z[c]
            return carry
        rows(lo, hi, row)

    for p in (2, 3):
        def row(j, carry, p=p):
            w = row_weights(weights, p, j, 8)
            at = region(p, j)
            pushed = []
            for c in range(4):
                around = (zed[region(p + 1, j), c], zed[region(p - 1, j), c], zed[at + 1, c], zed[at - 1, c])
                pushed.append(fixed[at, c] + spread_sum(zed[at, c], around, w))
            z = solve(pushed, w[6], (inv[at, 0], inv[at, 1]), cs)
            for c in range(4):
                it[p - 2, j - 2, c] = z[c]
            return carry
        rows(2, 18, row)
    out_near[0:14] = it[0, 1:15]
    out_near[14:26] = it[1, 2:14]
    out_far[0:14] = it[1, 1:15]
    out_far[14:26] = it[0, 2:14]


def sweep_body(it, near, far, fixed, weights, consts, inv, zed, put):
    def guess(p, j, c):
        if p == 2 or p == 3:
            return it[p - 2, j - 2, c]
        side = near if p < 2 else far
        if p == 1 or p == 4:
            return side[j - 3, c]
        return side[14 + j - 4, c]

    def at2(p, j):
        if p == 2 or p == 3:
            return (p - 2) * 14 + j - 3
        return (28 if p == 1 else 40) + j - 4

    cs = (consts[0], consts[1], consts[2])
    for p, lo, hi in ((2, 3, 17), (3, 3, 17), (1, 4, 16), (4, 4, 16)):
        def row(j, carry, p=p):
            w = row_weights(weights, p, j, 8)
            at = region(p, j)
            pushed = []
            for c in range(4):
                around = (guess(p + 1, j, c), guess(p - 1, j, c), guess(p, j + 1, c), guess(p, j - 1, c))
                pushed.append(fixed[at, c] + spread_sum(guess(p, j, c), around, w))
            z = solve(pushed, w[6], (inv[at, 0], inv[at, 1]), cs)
            for c in range(4):
                zed[at2(p, j), c] = z[c]
            return carry
        rows(lo, hi, row)
    for p in (2, 3):
        def row(j, carry, p=p):
            w = row_weights(weights, p, j, 8)
            at = region(p, j)
            here = at2(p, j)
            pushed = []
            for c in range(4):
                around = (zed[at2(p + 1, j), c], zed[at2(p - 1, j), c], zed[here + 1, c], zed[here - 1, c])
                pushed.append(fixed[at, c] + spread_sum(zed[here, c], around, w))
            z = solve(pushed, w[6], (inv[at, 0], inv[at, 1]), cs)
            for c in range(4):
                put(p - 2, j - 4, c, z[c])
            return carry
        rows(4, 16, row)


def middle_body(far, near, it, fixed, weights, consts, inv, new, out_near, out_far, zed):
    def put(x, j, c, v):
        new[x, j, c] = v
        first, second = (out_near, out_far) if x == 0 else (out_far, out_near)
        first[j, c] = v
        second[OWN + j, c] = v
    sweep_body(it, near, far, fixed, weights, consts, inv, zed, put)


EDGE = ((0, 4), (4, 4), (8, 3), (11, 3), (14, 2), (16, 2))


def edges_body(pos, far, near, new, send0, send1):
    odd = pos[0] & 1
    planes = (
        lambda j, n: new[0, pl.ds(j, n)],
        lambda j, n: new[1, pl.ds(j, n)],
        lambda j, n: near[pl.ds(j, n)],
        lambda j, n: far[pl.ds(j, n)],
        lambda j, n: near[pl.ds(OWN + j, n)],
        lambda j, n: far[pl.ds(OWN + j, n)],
    )
    for take, (at, n) in zip(planes, EDGE):
        send0[at : at + n] = take((OWN - n) * (1 - odd), n)
        send1[at : at + n] = take((OWN - n) * odd, n)


def widen_body(pos, got1, got0, new, near_x, far_x, own, near, far):
    odd = pos[0] & 1
    for x in range(2):
        own[x, HALO : HALO + OWN] = new[x]
    for out, got in ((near, near_x), (far, far_x)):
        out[3 : 3 + OWN] = got[0:OWN]
        out[20 : 20 + OWN] = got[OWN : 2 * OWN]
    for got, high in ((got0, 1 - odd), (got1, odd)):
        own[0, pl.ds(16 * high, 4)] = got[0:4]
        own[1, pl.ds(16 * high, 4)] = got[4:8]
        near[pl.ds(15 * high, 3)] = got[8:11]
        far[pl.ds(15 * high, 3)] = got[11:14]
        near[pl.ds(18 + 14 * high, 2)] = got[14:16]
        far[pl.ds(18 + 14 * high, 2)] = got[16:18]


def last_body(pos, far, near, it, fixed, weights, consts, inv, back, *rest):
    outs, (zed, fin, stage) = rest[:2], rest[2:]
    def put(x, j, c, v):
        fin[x * OWN + j, c] = v
    sweep_body(it, near, far, fixed, weights, consts, inv, zed, put)
    t = pos[0]
    matrix = back[...]
    for low in range(0, 2 * OWN, 4):
        done = transform(matrix, fin[low : low + 4].reshape(128, 128))
        for i in range(4):
            x, j = divmod(low + i, OWN)
            for c in range(4):
                stage[pl.ds((c * 2 + x) * OWN + j, 8, stride=8 * OWN), :] = done[(i * 4 + c) * 8 : (i * 4 + c + 1) * 8]
    for k in range(8):
        outs[k & 1][k >> 1] = stage[pl.ds(pl.multiple_of((t ^ k) * 8 * OWN, 8), 8 * OWN), :]


def merge_body(other, mine, *outs):
    for out, k in zip(outs, CHIPS):
        out[0] = mine[k]
        out[1] = other[k]


def unpack_body(pos, a, b, c, other, mine, state, adjoint, stage, held, sems):
    t = pos[0]
    flip = pos[1]
    for ref, k in zip((a, b, c), CHIPS):
        stage[t ^ (2 * k)] = ref[0]
        stage[t ^ (2 * k + 1)] = ref[1]
    stage[t] = mine[0]
    stage[t ^ 1] = other[0]
    copies = []
    for f, ref in enumerate((state, adjoint)):
        for n in range(2):
            for x in range(2):
                base = ((f * 2 + n) * 2 + x) * OWN
                for d in range(8):
                    held[f, n, x, OWN * d : OWN * (d + 1), :] = stage[d, base : base + OWN, :]
                copies.append(
                    pltpu.make_async_copy(held.at[f, n, x], ref.at[n, x ^ flip], sems.at[(f * 2 + n) * 2 + x])
                )
                copies[-1].start()
    for copy in copies:
        copy.wait()


def exchange(pieces):
    count = lax.axis_size("tm")
    return [lax.ppermute(pieces[k], "tm", [(i, i ^ k) for i in range(count)]) for k in ORDER] + [pieces[0]]


def swap_rows(block, start):
    count = lax.axis_size("tm")
    route = []
    for i in range(start, start + count, 2):
        low, high = i % count, (i + 1) % count
        route += [(low, high), (high, low)]
    return lax.ppermute(block, "tm", route)


def swap_planes(block, start):
    sections, slabs = lax.axis_size("tm"), lax.axis_size("space")
    route = []
    for t in range(sections):
        for s in range(slabs):
            pair = s + 1 if (s - start) % 2 == 0 else s - 1
            to = t * slabs + pair if 0 <= pair < slabs else (t ^ 1) * slabs + s
            route.append((t * slabs + s, to))
    return lax.ppermute(block, ("tm", "space"), route)


def on_device(state_guess, adjoint_guess, target, initial_state, diffusivity):
    t = lax.axis_index("tm").astype(jnp.int32)
    s = lax.axis_index("space").astype(jnp.int32)
    flip = s & 1
    pos = jnp.stack([t, flip, s])
    forward, back = (jnp.asarray(m) for m in transform_matrices())
    consts = jnp.asarray(mode_constants())

    arguments = (state_guess, adjoint_guess, target, diffusivity, initial_state, forward, back, consts)
    *pieces, near_c, far_c, here_c, forward, back, consts = call(
        pack_body,
        "pack",
        [whole(12 * WIN, 128)] * 8 + [whole(3, TALL, 128)] * 2 + [whole(4, TALL, 128)]
        + [whole(128, 128)] * 2 + [whole(10, 8, 128)],
        0,
        [pltpu.VMEM((8, 12 * WIN, 128), jnp.float32)]
        + [pltpu.VMEM((2, 2, 96, 128), jnp.float32)] * 3
        + [pltpu.VMEM((2, 96, 128), jnp.float32)] * 2
        + [pltpu.SemaphoreType.DMA((11,))],
        far_inputs=8,
    )(pos, *(pltpu.with_memory_space_constraint(a, pltpu.HBM) for a in arguments))
    got = exchange(pieces)
    own, wish, near, far = call(
        spread_body,
        "spread",
        [whole(2, WIN, 4, 8, 128), whole(2, 18, 2, 8, 128), whole(177, 8, 128), whole(177, 8, 128)],
        11,
        [pltpu.VMEM((8 * 12 * WIN, 128), jnp.float32)],
    )(pos, *got, near_c, far_c, forward)
    far = far_first = swap_planes(far, 0)
    near = near_first = swap_planes(near, 1)
    weights, inv = call(
        coefficient_body, "coefficients", [whole(4 * TALL * 8, 128), whole(68, 2, 8, 128)], 4
    )(pos, far, near, here_c, consts)
    weights = weights.reshape(4 * TALL, 8, 128)

    sweep_scratch = [pltpu.VMEM((52, 4, 8, 128), jnp.float32)]
    for outer in range(OUTER):
        fixed, it, near_z, far_z = call(
            front_body,
            "front",
            [whole(68, 4, 8, 128), whole(2, 16, 4, 8, 128), whole(26, 4, 8, 128), whole(26, 4, 8, 128)],
            9,
            [pltpu.VMEM((68, 4, 8, 128), jnp.float32)],
            scalars=0,
        )(far, near, own, wish, near_first, far_first, weights, consts, inv)
        far_z = swap_planes(far_z, 0)
        near_z = swap_planes(near_z, 1)
        if outer < OUTER - 1:
            new, near, far = call(
                middle_body,
                "middle",
                [whole(2, OWN, 4, 8, 128), whole(2 * OWN, 4, 8, 128), whole(2 * OWN, 4, 8, 128)],
                7,
                sweep_scratch,
                scalars=0,
            )(far_z, near_z, it, fixed, weights, consts, inv)
            far = swap_planes(far, 0)
            near = swap_planes(near, 1)
            send0, send1 = call(edges_body, "edges", [whole(18, 4, 8, 128)] * 2, 3)(pos, far, near, new)
            got1 = swap_rows(send1, 1)
            got0 = swap_rows(send0, 0)
            own, near, far = call(
                widen_body, "widen", [whole(2, WIN, 4, 8, 128), whole(34, 4, 8, 128), whole(34, 4, 8, 128)], 5
            )(pos, got1, got0, new, near, far)
            near = near.reshape(136, 8, 128)
            far = far.reshape(136, 8, 128)
    mine, other = call(
        last_body,
        "last",
        [whole(4, 8 * OWN, 128)] * 2,
        8,
        sweep_scratch + [pltpu.VMEM((2 * OWN, 4, 8, 128), jnp.float32), pltpu.VMEM((64 * OWN, 128), jnp.float32)],
    )(pos, far_z, near_z, it, fixed, weights, consts, inv, back)
    other = swap_rows(other, 0)
    pairs = call(merge_body, "merge", [whole(2, 8 * OWN, 128)] * 3, 2, scalars=0)(other, mine)
    count = lax.axis_size("tm")
    got = [
        lax.ppermute(pair, "tm", [(i, i ^ (2 * k)) for i in range(count)]) for pair, k in zip(pairs, CHIPS)
    ]
    return tuple(
        call(
            unpack_body,
            "unpack",
            [whole(2, 2, 96, 128)] * 2,
            5,
            [
                pltpu.VMEM((8, 8 * OWN, 128), jnp.float32),
                pltpu.VMEM((2, 2, 2, 96, 128), jnp.float32),
                pltpu.SemaphoreType.DMA((8,)),
            ],
            far_outputs=True,
        )(pos, *got, other, mine)
    )


def solution(mesh):
    in_specs = (
        P("tm", "space", None, None),
        P("tm", "space", None, None),
        P("tm", "space", None, None),
        P("space", None, None),
        P("space", None, None),
    )
    out_specs = (P("tm", "space", None, None), P("tm", "space", None, None))
    return jax.shard_map(
        on_device, mesh=mesh, in_specs=in_specs, out_specs=out_specs, check_vma=False
    )
```

```python
import math

import jax
import jax.numpy as jnp
import numpy as np
from jax import lax
from jax.experimental import pallas as pl
from jax.experimental.pallas import tpu as pltpu
from jax.sharding import PartitionSpec as P

TAU = 0.25
COUPLING = 5.0
DET_SHIFT = 1.25
OUTER = 2

OWN = 12
HALO = 4
WIN = OWN + 2 * HALO
ORDER = (4, 2, 6, 5, 3, 7, 1)
CHIPS = (2, 1, 3)
TALL = 24


def place():
    return lax.axis_index("tm"), lax.axis_index("space")


def transform_matrices():
    modes = np.arange(8)[:, None]
    steps = np.concatenate([np.arange(0, 16, 2), np.arange(1, 16, 2)])[None, :]
    angle = 2.0 * np.pi * ((modes * steps) % 16) / 16.0
    real, imag = np.cos(angle), -np.sin(angle)
    imag[0] = np.where(steps[0] % 2 == 0, 1.0, -1.0)
    forward = np.concatenate([real, imag], 0)
    back = forward.T.copy() / 8.0
    back[:, 0] /= 2.0
    back[:, 8] /= 2.0
    eye = np.eye(8)
    return np.kron(eye, forward).astype(np.float32), np.kron(eye, back).astype(np.float32)


def mode_constants():
    theta = 2.0 * np.pi * np.arange(8) / 16.0
    shift_a = 1.0 - np.cos(theta)
    shift_b = shift_a.copy()
    shift_b[0] = 2.0
    lag = np.sin(theta)
    phase_a, phase_b = np.cos(theta), np.sin(theta)
    phase_b[0] = -1.0
    share = np.where(np.arange(8) == 0, 1.0, 2.0) / 16.0
    last_a, last_b = share * np.cos(15.0 * theta), -share * np.sin(15.0 * theta)
    last_b[0] = -1.0 / 16.0
    first_a, first_b = share, np.where(np.arange(8) == 0, 1.0, 0.0) / 16.0
    slot = np.where(np.arange(8) == 0, 1.0, 0.0)
    kinds = [shift_a, shift_b, lag, phase_a, phase_b, last_a, last_b, first_a, first_b, slot]
    return (np.stack(kinds)[:, :, None] * np.ones((1, 1, 128))).astype(np.float32)


def whole(*shape):
    return jax.ShapeDtypeStruct(shape, jnp.float32)


def call(body, name, outs, n_in, scratch=(), far_inputs=0, far_outputs=False):
    vmem = pl.BlockSpec(memory_space=pltpu.VMEM)
    anywhere = pl.BlockSpec(memory_space=pltpu.HBM)
    return pl.pallas_call(
        body,
        name=name,
        out_shape=outs,
        in_specs=[anywhere] * far_inputs + [vmem] * n_in,
        out_specs=[anywhere if far_outputs else vmem] * len(outs),
        scratch_shapes=list(scratch),
        compiler_params=pltpu.CompilerParams(vmem_limit_bytes=16 * 1024 * 1024),
    )


def rows(lo, hi, body):
    lax.fori_loop(lo, hi, body, 0, unroll=True)


def pack_body(*rest):
    sources, outs, (near, far, here), tables = rest[:8], rest[8:16], rest[16:19], rest[19:22]
    stage, held, sems = rest[22], rest[23:28], rest[28]
    slabs = [
        pltpu.make_async_copy(sources[f].at[n], held[f].at[n], sems.at[2 * f + n]) for f in range(3) for n in range(2)
    ]
    copies = [pltpu.make_async_copy(sources[3 + i], ref, sems.at[6 + i]) for i, ref in enumerate(held[3:] + tables)]
    for copy in slabs + copies:
        copy.start()
    state, adjoint, target, kappa, begin = held
    t, s = place()
    flip = s & 1
    for f, ref in enumerate((state, adjoint, target)):
        for n in range(2):
            slabs[2 * f + n].wait()
            for x in range(2):
                base = ((f * 2 + n) * 2 + x) * WIN
                for d in range(8):
                    low = OWN * d - HALO
                    first, last = max(low, 0), min(low + WIN, 96)
                    stage[d, base + first - low : base + last - low, :] = ref[n, x ^ flip, first:last, :]
                    if first > low:
                        stage[d, base : base + first - low, :] = jnp.zeros((first - low, 128), jnp.float32)
                    if last < low + WIN:
                        stage[d, base + last - low : base + WIN, :] = jnp.zeros((low + WIN - last, 128), jnp.float32)
    for k in range(8):
        outs[k][...] = stage[t ^ k]
    for copy in copies:
        copy.wait()
    for d in range(8):
        @pl.when(t == d)
        def window(d=d):
            low = OWN * d - HALO
            first, last = max(low, 0), min(low + TALL, 96)
            parts = []
            for ref, x in ((kappa, 0), (kappa, 1), (begin, 0), (begin, 1)):
                v = ref[x ^ flip, first:last, :]
                if first > low:
                    v = jnp.concatenate([jnp.zeros((first - low, 128), jnp.float32), v], 0)
                if last < low + TALL:
                    v = jnp.concatenate([v, jnp.zeros((low + TALL - last, 128), jnp.float32)], 0)
                parts.append(v)
            for i, v in enumerate(parts):
                here[i] = v
            for i, q in enumerate((0, 1, 2)):
                near[i] = parts[q]
            for i, q in enumerate((1, 0, 3)):
                far[i] = parts[q]


def coefficient_body(far, near, here, consts, weights, inv):
    t, s = place()
    flip = s & 1
    near, far = ([side[168 + 3 * i : 171 + 3 * i].reshape(TALL, 128) for i in range(3)] for side in (near, far))
    kappa = [near[1], near[0], here[0], here[1], far[0], far[1]]
    for p in range(6):
        plane = jnp.where(flip == 1, 2 * s + 3 - p, 2 * s - 2 + p)
        kappa[p] = kappa[p] * jnp.where((plane >= 0) & (plane < 64), 1.0, 0.0)
    begin = [near[2], here[2], here[3], far[2]]
    lane = lax.broadcasted_iota(jnp.int32, (TALL, 128), 1)
    row = lax.broadcasted_iota(jnp.int32, (TALL, 128), 0) + (OWN * t - HALO)
    half = 0.5 * TAU
    for p in range(1, 5):
        plane = jnp.where(flip == 1, 2 * s + 3 - p, 2 * s - 2 + p)
        ahead = jnp.where(flip == 1, plane - 1, plane + 1)
        behind = jnp.where(flip == 1, plane + 1, plane - 1)
        real = jnp.where((plane >= 0) & (plane < 64), half, 0.0)
        to_ahead = jnp.where((ahead >= 0) & (ahead < 64), real, 0.0)
        to_behind = jnp.where((behind >= 0) & (behind < 64), real, 0.0)
        k = kappa[p]
        row_ok = (row >= 0) & (row < 96)
        xp = k + kappa[p + 1]
        xm = k + kappa[p - 1]
        yp = k + pltpu.roll(k, TALL - 1, 0)
        ym = k + pltpu.roll(k, 1, 0)
        zp = k + jnp.where(lane < 127, pltpu.roll(k, 127, 1), 0.0)
        zm = k + jnp.where(lane > 0, pltpu.roll(k, 1, 1), 0.0)
        kinds = [
            jnp.where(row_ok, xp * to_ahead, 0.0),
            jnp.where(row_ok, xm * to_behind, 0.0),
            jnp.where(row_ok & (row < 95), yp * real, 0.0),
            jnp.where(row_ok & (row > 0), ym * real, 0.0),
            jnp.where(row_ok & (lane < 127), zp * real, 0.0),
            jnp.where(row_ok & (lane > 0), zm * real, 0.0),
            half * (((xp + xm) + (yp + ym)) + (zp + zm)),
            begin[p - 1],
        ]
        for i, v in enumerate(kinds):
            weights[pl.ds((p - 1) * TALL * 8 + i, TALL, stride=8), :] = v
    ca, cb, lag = consts[0], consts[1], consts[2]
    base = lag * lag + DET_SHIFT
    for p, lo, hi in ((2, 1, 19), (3, 1, 19), (1, 2, 18), (4, 2, 18)):
        for j in range(lo, hi):
            td = jnp.broadcast_to(weights[pl.ds(((p - 1) * TALL + j) * 8 + 6, 1), :], (8, 128))
            a = ca + td
            b = cb + td
            at = region(p, j)
            inv[at, 0] = 1.0 / (a * a + base)
            inv[at, 1] = 1.0 / (b * b + base)


def spread_body(*rest):
    pieces, (near_c, far_c, forward), (own, wish, near, far), stage = rest[:8], rest[8:11], rest[11:15], rest[15]
    for i in range(3):
        near[168 + 3 * i : 171 + 3 * i] = near_c[i].reshape(3, 8, 128)
        far[168 + 3 * i : 171 + 3 * i] = far_c[i].reshape(3, 8, 128)
    t, _ = place()
    rows = 12 * WIN
    for k, piece in zip(ORDER + (0,), pieces):
        stage[pl.ds(pl.multiple_of((t ^ k) * rows, 8), rows), :] = piece[...]

    def steps(f, n, x, j):
        return stage[pl.ds(((f * 2 + n) * 2 + x) * WIN + j, 8, stride=rows), :]

    matrix = forward[...]
    for x in range(2):
        for low in range(0, WIN, 4):
            block = [steps(f, n, x, low + i) for i in range(4) for f in range(2) for n in range(2)]
            done = transform(matrix, jnp.concatenate(block, 0))
            for i in range(4):
                for c in range(4):
                    v = done[(i * 4 + c) * 8 : (i * 4 + c + 1) * 8]
                    own[x, low + i, c] = v
                    put_field(near, far, x, low + i, c, v)
    cells = [(x, j) for x in range(2) for j in range(WIN)]
    for low in range(0, len(cells), 8):
        block = [steps(2, n, x, j) for x, j in cells[low : low + 8] for n in range(2)]
        done = transform(matrix, jnp.concatenate(block, 0))
        for i, (x, j) in enumerate(cells[low : low + 8]):
            for n in range(2):
                v = done[(i * 2 + n) * 8 : (i * 2 + n + 1) * 8]
                if 1 <= j <= 18:
                    wish[x, j - 1, n] = v
                if 2 <= j <= 17:
                    out = far if x == 1 else near
                    out[136 + (j - 2) * 2 + n] = v


def transform(matrix, block):
    return jnp.dot(matrix, block, precision=lax.Precision.HIGHEST, preferred_element_type=jnp.float32)


def put_field(near, far, x, j, c, v):
    first, second = (near, far) if x == 0 else (far, near)
    if 1 <= j <= 18:
        first[(j - 1) * 4 + c] = v
    if 2 <= j <= 17:
        second[72 + (j - 2) * 4 + c] = v


def region(p, j):
    if p == 2 or p == 3:
        return (p - 2) * 18 + j - 1
    return (36 if p == 1 else 52) + j - 2


def spread_sum(v, around, w):
    px, mx, py, my = around
    up = pltpu.roll(v, 127, 1)
    down = pltpu.roll(v, 1, 1)
    return ((w[0] * px + w[1] * mx) + (w[2] * py + w[3] * my)) + (w[4] * up + w[5] * down)


def row_weights(weights, p, j, count):
    tile = weights[(p - 1) * TALL + j]
    return [jnp.broadcast_to(tile[k : k + 1, :], (8, 128)) for k in range(count)]


def solve(right, td, inv, consts):
    ur, ui, pr, pi = right
    shift_a, shift_b, lag = consts
    inv_a, inv_b = inv
    a = shift_a + td
    b = shift_b + td
    return (
        (a * ur + lag * ui - COUPLING * pr) * inv_a,
        (b * ui - lag * ur - COUPLING * pi) * inv_b,
        (TAU * ur + a * pr - lag * pi) * inv_a,
        (TAU * ui + b * pi + lag * pr) * inv_b,
    )


def over_sublanes(v):
    v = v + pltpu.roll(v, 4, 0)
    v = v + pltpu.roll(v, 2, 0)
    return v + pltpu.roll(v, 1, 0)


def front_body(far, near, own, wish, tnear, tfar, weights, consts, inv, fixed, it, out_near, out_far, zed):
    def field(p, j, c):
        if p == 2 or p == 3:
            return own[p - 2, j, c]
        side = near if p < 2 else far
        if p == 1 or p == 4:
            return side[(j - 1) * 4 + c]
        return side[72 + (j - 2) * 4 + c]

    def wanted(p, j, n):
        if p == 2 or p == 3:
            return wish[p - 2, j - 1, n]
        return (tnear if p == 1 else tfar)[136 + (j - 2) * 2 + n]

    cs = (consts[0], consts[1], consts[2])
    phase_a, phase_b, last_a, last_b, first_a, first_b, slot = (consts[i] for i in range(3, 10))
    for p, lo, hi in ((2, 1, 19), (3, 1, 19), (1, 2, 18), (4, 2, 18)):
        def row(j, carry, p=p):
            w = row_weights(weights, p, j, 8)
            v = [field(p, j, c) for c in range(4)]
            last = over_sublanes(last_a * v[0] + last_b * v[1])
            first = over_sublanes(first_a * v[2] + first_b * v[3])
            begin = w[7] - last
            kept = (
                begin,
                slot * begin,
                -TAU * wanted(p, j, 0) - phase_a * first,
                -TAU * wanted(p, j, 1) - phase_b * first,
            )
            at = region(p, j)
            pushed = []
            for c in range(4):
                fixed[at, c] = kept[c]
                around = (field(p + 1, j, c), field(p - 1, j, c), field(p, j + 1, c), field(p, j - 1, c))
                pushed.append(kept[c] + spread_sum(v[c], around, w))
            z = solve(pushed, w[6], (inv[at, 0], inv[at, 1]), cs)
            for c in range(4):
                zed[at, c] = z[c]
            return carry
        rows(lo, hi, row)

    for p in (2, 3):
        def row(j, carry, p=p):
            w = row_weights(weights, p, j, 8)
            at = region(p, j)
            pushed = []
            for c in range(4):
                around = (zed[region(p + 1, j), c], zed[region(p - 1, j), c], zed[at + 1, c], zed[at - 1, c])
                pushed.append(fixed[at, c] + spread_sum(zed[at, c], around, w))
            z = solve(pushed, w[6], (inv[at, 0], inv[at, 1]), cs)
            for c in range(4):
                it[p - 2, j - 2, c] = z[c]
            return carry
        rows(2, 18, row)
    out_near[0:14] = it[0, 1:15]
    out_near[14:26] = it[1, 2:14]
    out_far[0:14] = it[1, 1:15]
    out_far[14:26] = it[0, 2:14]


def sweep_body(it, near, far, fixed, weights, consts, inv, zed, put):
    def guess(p, j, c):
        if p == 2 or p == 3:
            return it[p - 2, j - 2, c]
        side = near if p < 2 else far
        if p == 1 or p == 4:
            return side[j - 3, c]
        return side[14 + j - 4, c]

    def at2(p, j):
        if p == 2 or p == 3:
            return (p - 2) * 14 + j - 3
        return (28 if p == 1 else 40) + j - 4

    cs = (consts[0], consts[1], consts[2])
    for p, lo, hi in ((2, 3, 17), (3, 3, 17), (1, 4, 16), (4, 4, 16)):
        def row(j, carry, p=p):
            w = row_weights(weights, p, j, 8)
            at = region(p, j)
            pushed = []
            for c in range(4):
                around = (guess(p + 1, j, c), guess(p - 1, j, c), guess(p, j + 1, c), guess(p, j - 1, c))
                pushed.append(fixed[at, c] + spread_sum(guess(p, j, c), around, w))
            z = solve(pushed, w[6], (inv[at, 0], inv[at, 1]), cs)
            for c in range(4):
                zed[at2(p, j), c] = z[c]
            return carry
        rows(lo, hi, row)
    for p in (2, 3):
        def row(j, carry, p=p):
            w = row_weights(weights, p, j, 8)
            at = region(p, j)
            here = at2(p, j)
            pushed = []
            for c in range(4):
                around = (zed[at2(p + 1, j), c], zed[at2(p - 1, j), c], zed[here + 1, c], zed[here - 1, c])
                pushed.append(fixed[at, c] + spread_sum(zed[here, c], around, w))
            z = solve(pushed, w[6], (inv[at, 0], inv[at, 1]), cs)
            for c in range(4):
                put(p - 2, j - 4, c, z[c])
            return carry
        rows(4, 16, row)


def middle_body(far, near, it, fixed, weights, consts, inv, new, out_near, out_far, zed):
    def put(x, j, c, v):
        new[x, j, c] = v
        first, second = (out_near, out_far) if x == 0 else (out_far, out_near)
        first[j, c] = v
        second[OWN + j, c] = v
    sweep_body(it, near, far, fixed, weights, consts, inv, zed, put)


EDGE = ((0, 4), (4, 4), (8, 3), (11, 3), (14, 2), (16, 2))


def edges_body(far, near, new, send0, send1):
    odd = place()[0] & 1
    planes = (
        lambda j, n: new[0, pl.ds(j, n)],
        lambda j, n: new[1, pl.ds(j, n)],
        lambda j, n: near[pl.ds(j, n)],
        lambda j, n: far[pl.ds(j, n)],
        lambda j, n: near[pl.ds(OWN + j, n)],
        lambda j, n: far[pl.ds(OWN + j, n)],
    )
    for take, (at, n) in zip(planes, EDGE):
        send0[at : at + n] = take((OWN - n) * (1 - odd), n)
        send1[at : at + n] = take((OWN - n) * odd, n)


def widen_body(got1, got0, new, near_x, far_x, own, near, far):
    odd = place()[0] & 1
    for x in range(2):
        own[x, HALO : HALO + OWN] = new[x]
    for out, got in ((near, near_x), (far, far_x)):
        out[3 : 3 + OWN] = got[0:OWN]
        out[20 : 20 + OWN] = got[OWN : 2 * OWN]
    for got, high in ((got0, 1 - odd), (got1, odd)):
        own[0, pl.ds(16 * high, 4)] = got[0:4]
        own[1, pl.ds(16 * high, 4)] = got[4:8]
        near[pl.ds(15 * high, 3)] = got[8:11]
        far[pl.ds(15 * high, 3)] = got[11:14]
        near[pl.ds(18 + 14 * high, 2)] = got[14:16]
        far[pl.ds(18 + 14 * high, 2)] = got[16:18]


def last_body(far, near, it, fixed, weights, consts, inv, back, *rest):
    outs, (zed, fin, stage) = rest[:2], rest[2:]
    def put(x, j, c, v):
        fin[x * OWN + j, c] = v
    sweep_body(it, near, far, fixed, weights, consts, inv, zed, put)
    t, _ = place()
    matrix = back[...]
    for low in range(0, 2 * OWN, 4):
        done = transform(matrix, fin[low : low + 4].reshape(128, 128))
        for i in range(4):
            x, j = divmod(low + i, OWN)
            for c in range(4):
                stage[pl.ds((c * 2 + x) * OWN + j, 8, stride=8 * OWN), :] = done[(i * 4 + c) * 8 : (i * 4 + c + 1) * 8]
    for k in range(8):
        outs[k & 1][k >> 1] = stage[pl.ds(pl.multiple_of((t ^ k) * 8 * OWN, 8), 8 * OWN), :]


def merge_body(other, mine, *outs):
    for out, k in zip(outs, CHIPS):
        out[0] = mine[k]
        out[1] = other[k]


def unpack_body(a, b, c, other, mine, state, adjoint, stage, held, sems):
    t, s = place()
    flip = s & 1
    for ref, k in zip((a, b, c), CHIPS):
        stage[t ^ (2 * k)] = ref[0]
        stage[t ^ (2 * k + 1)] = ref[1]
    stage[t] = mine[0]
    stage[t ^ 1] = other[0]
    copies = []
    for f, ref in enumerate((state, adjoint)):
        for n in range(2):
            for x in range(2):
                base = ((f * 2 + n) * 2 + x) * OWN
                for d in range(8):
                    held[f, n, x, OWN * d : OWN * (d + 1), :] = stage[d, base : base + OWN, :]
                copies.append(
                    pltpu.make_async_copy(held.at[f, n, x], ref.at[n, x ^ flip], sems.at[(f * 2 + n) * 2 + x])
                )
                copies[-1].start()
    for copy in copies:
        copy.wait()


def exchange(pieces):
    count = lax.axis_size("tm")
    return [lax.ppermute(pieces[k], "tm", [(i, i ^ k) for i in range(count)]) for k in ORDER] + [pieces[0]]


def swap_rows(block, start):
    count = lax.axis_size("tm")
    route = []
    for i in range(start, start + count, 2):
        low, high = i % count, (i + 1) % count
        route += [(low, high), (high, low)]
    return lax.ppermute(block, "tm", route)


def swap_planes(block, start):
    sections, slabs = lax.axis_size("tm"), lax.axis_size("space")
    route = []
    for t in range(sections):
        for s in range(slabs):
            pair = s + 1 if (s - start) % 2 == 0 else s - 1
            to = t * slabs + pair if 0 <= pair < slabs else (t ^ 1) * slabs + s
            route.append((t * slabs + s, to))
    return lax.ppermute(block, ("tm", "space"), route)


def on_device(state_guess, adjoint_guess, target, initial_state, diffusivity):
    forward, back = (jnp.asarray(m) for m in transform_matrices())
    consts = jnp.asarray(mode_constants())

    arguments = (state_guess, adjoint_guess, target, diffusivity, initial_state, forward, back, consts)
    *pieces, near_c, far_c, here_c, forward, back, consts = call(
        pack_body,
        "pack",
        [whole(12 * WIN, 128)] * 8 + [whole(3, TALL, 128)] * 2 + [whole(4, TALL, 128)]
        + [whole(128, 128)] * 2 + [whole(10, 8, 128)],
        0,
        [pltpu.VMEM((8, 12 * WIN, 128), jnp.float32)]
        + [pltpu.VMEM((2, 2, 96, 128), jnp.float32)] * 3
        + [pltpu.VMEM((2, 96, 128), jnp.float32)] * 2
        + [pltpu.SemaphoreType.DMA((11,))],
        far_inputs=8,
    )(*(pltpu.with_memory_space_constraint(a, pltpu.HBM) for a in arguments))
    got = exchange(pieces)
    own, wish, near, far = call(
        spread_body,
        "spread",
        [whole(2, WIN, 4, 8, 128), whole(2, 18, 2, 8, 128), whole(177, 8, 128), whole(177, 8, 128)],
        11,
        [pltpu.VMEM((8 * 12 * WIN, 128), jnp.float32)],
    )(*got, near_c, far_c, forward)
    far = far_first = swap_planes(far, 0)
    near = near_first = swap_planes(near, 1)
    weights, inv = call(
        coefficient_body, "coefficients", [whole(4 * TALL * 8, 128), whole(68, 2, 8, 128)], 4
    )(far, near, here_c, consts)
    weights = weights.reshape(4 * TALL, 8, 128)

    sweep_scratch = [pltpu.VMEM((52, 4, 8, 128), jnp.float32)]
    for outer in range(OUTER):
        fixed, it, near_z, far_z = call(
            front_body,
            "front",
            [whole(68, 4, 8, 128), whole(2, 16, 4, 8, 128), whole(26, 4, 8, 128), whole(26, 4, 8, 128)],
            9,
            [pltpu.VMEM((68, 4, 8, 128), jnp.float32)],
        )(far, near, own, wish, near_first, far_first, weights, consts, inv)
        far_z = swap_planes(far_z, 0)
        near_z = swap_planes(near_z, 1)
        if outer < OUTER - 1:
            new, near, far = call(
                middle_body,
                "middle",
                [whole(2, OWN, 4, 8, 128), whole(2 * OWN, 4, 8, 128), whole(2 * OWN, 4, 8, 128)],
                7,
                sweep_scratch,
            )(far_z, near_z, it, fixed, weights, consts, inv)
            far = swap_planes(far, 0)
            near = swap_planes(near, 1)
            send0, send1 = call(edges_body, "edges", [whole(18, 4, 8, 128)] * 2, 3)(far, near, new)
            got1 = swap_rows(send1, 1)
            got0 = swap_rows(send0, 0)
            own, near, far = call(
                widen_body, "widen", [whole(2, WIN, 4, 8, 128), whole(34, 4, 8, 128), whole(34, 4, 8, 128)], 5
            )(got1, got0, new, near, far)
            near = near.reshape(136, 8, 128)
            far = far.reshape(136, 8, 128)
    mine, other = call(
        last_body,
        "last",
        [whole(4, 8 * OWN, 128)] * 2,
        8,
        sweep_scratch + [pltpu.VMEM((2 * OWN, 4, 8, 128), jnp.float32), pltpu.VMEM((64 * OWN, 128), jnp.float32)],
    )(far_z, near_z, it, fixed, weights, consts, inv, back)
    other = swap_rows(other, 0)
    pairs = call(merge_body, "merge", [whole(2, 8 * OWN, 128)] * 3, 2)(other, mine)
    count = lax.axis_size("tm")
    got = [
        lax.ppermute(pair, "tm", [(i, i ^ (2 * k)) for i in range(count)]) for pair, k in zip(pairs, CHIPS)
    ]
    return tuple(
        call(
            unpack_body,
            "unpack",
            [whole(2, 2, 96, 128)] * 2,
            5,
            [
                pltpu.VMEM((8, 8 * OWN, 128), jnp.float32),
                pltpu.VMEM((2, 2, 2, 96, 128), jnp.float32),
                pltpu.SemaphoreType.DMA((8,)),
            ],
            far_outputs=True,
        )(*got, other, mine)
    )


def solution(mesh):
    in_specs = (
        P("tm", "space", None, None),
        P("tm", "space", None, None),
        P("tm", "space", None, None),
        P("space", None, None),
        P("space", None, None),
    )
    out_specs = (P("tm", "space", None, None), P("tm", "space", None, None))
    return jax.shard_map(
        on_device, mesh=mesh, in_specs=in_specs, out_specs=out_specs, check_vma=False
    )
```

```python
import math

import jax
import jax.numpy as jnp
import numpy as np
from jax import lax
from jax.experimental import pallas as pl
from jax.experimental.pallas import tpu as pltpu
from jax.sharding import PartitionSpec as P

TAU = 0.25
COUPLING = 5.0
DET_SHIFT = 1.25
OUTER = 2

OWN = 12
HALO = 4
WIN = OWN + 2 * HALO
ORDER = (4, 2, 6, 5, 3, 7, 1)
PIECE = 8 * WIN + 4 * (WIN - 2)
CHIPS = (2, 1, 3)
TALL = 24


def place():
    return lax.axis_index("tm"), lax.axis_index("space")


def transform_matrices():
    modes = np.arange(8)[:, None]
    steps = np.concatenate([np.arange(0, 16, 2), np.arange(1, 16, 2)])[None, :]
    angle = 2.0 * np.pi * ((modes * steps) % 16) / 16.0
    real, imag = np.cos(angle), -np.sin(angle)
    imag[0] = np.where(steps[0] % 2 == 0, 1.0, -1.0)
    forward = np.concatenate([real, imag], 0)
    back = forward.T.copy() / 8.0
    back[:, 0] /= 2.0
    back[:, 8] /= 2.0
    eye = np.eye(8)
    return np.kron(eye, forward).astype(np.float32), np.kron(eye, back).astype(np.float32)


def mode_constants():
    theta = 2.0 * np.pi * np.arange(8) / 16.0
    shift_a = 1.0 - np.cos(theta)
    shift_b = shift_a.copy()
    shift_b[0] = 2.0
    lag = np.sin(theta)
    phase_a, phase_b = np.cos(theta), np.sin(theta)
    phase_b[0] = -1.0
    share = np.where(np.arange(8) == 0, 1.0, 2.0) / 16.0
    last_a, last_b = share * np.cos(15.0 * theta), -share * np.sin(15.0 * theta)
    last_b[0] = -1.0 / 16.0
    first_a, first_b = share, np.where(np.arange(8) == 0, 1.0, 0.0) / 16.0
    slot = np.where(np.arange(8) == 0, 1.0, 0.0)
    kinds = [shift_a, shift_b, lag, phase_a, phase_b, last_a, last_b, first_a, first_b, slot]
    return (np.stack(kinds)[:, :, None] * np.ones((1, 1, 128))).astype(np.float32)


def whole(*shape):
    return jax.ShapeDtypeStruct(shape, jnp.float32)


def call(body, name, outs, n_in, scratch=(), far_inputs=0, far_outputs=False):
    vmem = pl.BlockSpec(memory_space=pltpu.VMEM)
    anywhere = pl.BlockSpec(memory_space=pltpu.HBM)
    return pl.pallas_call(
        body,
        name=name,
        out_shape=outs,
        in_specs=[anywhere] * far_inputs + [vmem] * n_in,
        out_specs=[anywhere if far_outputs else vmem] * len(outs),
        scratch_shapes=list(scratch),
        compiler_params=pltpu.CompilerParams(vmem_limit_bytes=16 * 1024 * 1024),
    )


def rows(lo, hi, body):
    lax.fori_loop(lo, hi, body, 0, unroll=True)


def piece_row(f, n, x):
    return ((f * 2 + n) * 2 + x) * WIN if f < 2 else 8 * WIN + (n * 2 + x) * (WIN - 2)


def pack_body(*rest):
    sources, outs, (near, far, here), tables = rest[:8], rest[8:16], rest[16:19], rest[19:22]
    stage, held, sems = rest[22], rest[23:28], rest[28]
    slabs = [
        pltpu.make_async_copy(sources[f].at[n], held[f].at[n], sems.at[2 * f + n]) for f in range(3) for n in range(2)
    ]
    copies = [pltpu.make_async_copy(sources[3 + i], ref, sems.at[6 + i]) for i, ref in enumerate(held[3:] + tables)]
    for copy in slabs + copies:
        copy.start()
    state, adjoint, target, kappa, begin = held
    t, s = place()
    flip = s & 1
    for f, ref in enumerate((state, adjoint, target)):
        for n in range(2):
            slabs[2 * f + n].wait()
            for x in range(2):
                base = piece_row(f, n, x)
                size = WIN if f < 2 else WIN - 2
                for d in range(8):
                    low = OWN * d - (HALO if f < 2 else HALO - 1)
                    first, last = max(low, 0), min(low + size, 96)
                    stage[d, base + first - low : base + last - low, :] = ref[n, x ^ flip, first:last, :]
                    if first > low:
                        stage[d, base : base + first - low, :] = jnp.zeros((first - low, 128), jnp.float32)
                    if last < low + size:
                        stage[d, base + last - low : base + size, :] = jnp.zeros((low + size - last, 128), jnp.float32)
    for k in range(8):
        outs[k][...] = stage[t ^ k]
    for copy in copies:
        copy.wait()
    for d in range(8):
        @pl.when(t == d)
        def window(d=d):
            low = OWN * d - HALO
            first, last = max(low, 0), min(low + TALL, 96)
            parts = []
            for ref, x in ((kappa, 0), (kappa, 1), (begin, 0), (begin, 1)):
                v = ref[x ^ flip, first:last, :]
                if first > low:
                    v = jnp.concatenate([jnp.zeros((first - low, 128), jnp.float32), v], 0)
                if last < low + TALL:
                    v = jnp.concatenate([v, jnp.zeros((low + TALL - last, 128), jnp.float32)], 0)
                parts.append(v)
            for i, v in enumerate(parts):
                here[i] = v
            for i, q in enumerate((0, 1, 2)):
                near[i] = parts[q]
            for i, q in enumerate((1, 0, 3)):
                far[i] = parts[q]


def coefficient_body(far, near, here, consts, weights, inv):
    t, s = place()
    flip = s & 1
    near, far = ([side[168 + 3 * i : 171 + 3 * i].reshape(TALL, 128) for i in range(3)] for side in (near, far))
    kappa = [near[1], near[0], here[0], here[1], far[0], far[1]]
    for p in range(6):
        plane = jnp.where(flip == 1, 2 * s + 3 - p, 2 * s - 2 + p)
        kappa[p] = kappa[p] * jnp.where((plane >= 0) & (plane < 64), 1.0, 0.0)
    begin = [near[2], here[2], here[3], far[2]]
    lane = lax.broadcasted_iota(jnp.int32, (TALL, 128), 1)
    row = lax.broadcasted_iota(jnp.int32, (TALL, 128), 0) + (OWN * t - HALO)
    half = 0.5 * TAU
    for p in range(1, 5):
        plane = jnp.where(flip == 1, 2 * s + 3 - p, 2 * s - 2 + p)
        ahead = jnp.where(flip == 1, plane - 1, plane + 1)
        behind = jnp.where(flip == 1, plane + 1, plane - 1)
        real = jnp.where((plane >= 0) & (plane < 64), half, 0.0)
        to_ahead = jnp.where((ahead >= 0) & (ahead < 64), real, 0.0)
        to_behind = jnp.where((behind >= 0) & (behind < 64), real, 0.0)
        k = kappa[p]
        row_ok = (row >= 0) & (row < 96)
        xp = k + kappa[p + 1]
        xm = k + kappa[p - 1]
        yp = k + pltpu.roll(k, TALL - 1, 0)
        ym = k + pltpu.roll(k, 1, 0)
        zp = k + jnp.where(lane < 127, pltpu.roll(k, 127, 1), 0.0)
        zm = k + jnp.where(lane > 0, pltpu.roll(k, 1, 1), 0.0)
        kinds = [
            jnp.where(row_ok, xp * to_ahead, 0.0),
            jnp.where(row_ok, xm * to_behind, 0.0),
            jnp.where(row_ok & (row < 95), yp * real, 0.0),
            jnp.where(row_ok & (row > 0), ym * real, 0.0),
            jnp.where(row_ok & (lane < 127), zp * real, 0.0),
            jnp.where(row_ok & (lane > 0), zm * real, 0.0),
            half * (((xp + xm) + (yp + ym)) + (zp + zm)),
            begin[p - 1],
        ]
        for i, v in enumerate(kinds):
            weights[pl.ds((p - 1) * TALL * 8 + i, TALL, stride=8), :] = v
    ca, cb, lag = consts[0], consts[1], consts[2]
    base = lag * lag + DET_SHIFT
    for p, lo, hi in ((2, 1, 19), (3, 1, 19), (1, 2, 18), (4, 2, 18)):
        for j in range(lo, hi):
            td = jnp.broadcast_to(weights[pl.ds(((p - 1) * TALL + j) * 8 + 6, 1), :], (8, 128))
            a = ca + td
            b = cb + td
            at = region(p, j)
            inv[at, 0] = 1.0 / (a * a + base)
            inv[at, 1] = 1.0 / (b * b + base)


def spread_body(*rest):
    pieces, (near_c, far_c, forward), (own, wish, near, far), stage = rest[:8], rest[8:11], rest[11:15], rest[15]
    for i in range(3):
        near[168 + 3 * i : 171 + 3 * i] = near_c[i].reshape(3, 8, 128)
        far[168 + 3 * i : 171 + 3 * i] = far_c[i].reshape(3, 8, 128)
    t, _ = place()
    rows = PIECE
    for k, piece in zip(ORDER + (0,), pieces):
        stage[pl.ds(pl.multiple_of((t ^ k) * rows, 8), rows), :] = piece[...]

    def steps(f, n, x, j):
        return stage[pl.ds(piece_row(f, n, x) + j - (0 if f < 2 else 1), 8, stride=rows), :]

    matrix = forward[...]
    for x in range(2):
        for low in range(0, WIN, 4):
            block = [steps(f, n, x, low + i) for i in range(4) for f in range(2) for n in range(2)]
            done = transform(matrix, jnp.concatenate(block, 0))
            for i in range(4):
                for c in range(4):
                    v = done[(i * 4 + c) * 8 : (i * 4 + c + 1) * 8]
                    own[x, low + i, c] = v
                    put_field(near, far, x, low + i, c, v)
    cells = [(x, j) for x in range(2) for j in range(1, WIN - 1)]
    for low in range(0, len(cells), 8):
        block = jnp.concatenate([steps(2, n, x, j) for x, j in cells[low : low + 8] for n in range(2)], 0)
        done = transform(matrix[: len(block), : len(block)], block)
        for i, (x, j) in enumerate(cells[low : low + 8]):
            for n in range(2):
                v = done[(i * 2 + n) * 8 : (i * 2 + n + 1) * 8]
                wish[x, j - 1, n] = v
                if 2 <= j <= 17:
                    out = far if x == 1 else near
                    out[136 + (j - 2) * 2 + n] = v


def transform(matrix, block):
    return jnp.dot(matrix, block, precision=lax.Precision.HIGHEST, preferred_element_type=jnp.float32)


def put_field(near, far, x, j, c, v):
    first, second = (near, far) if x == 0 else (far, near)
    if 1 <= j <= 18:
        first[(j - 1) * 4 + c] = v
    if 2 <= j <= 17:
        second[72 + (j - 2) * 4 + c] = v


def region(p, j):
    if p == 2 or p == 3:
        return (p - 2) * 18 + j - 1
    return (36 if p == 1 else 52) + j - 2


def spread_sum(v, around, w):
    px, mx, py, my = around
    up = pltpu.roll(v, 127, 1)
    down = pltpu.roll(v, 1, 1)
    return ((w[0] * px + w[1] * mx) + (w[2] * py + w[3] * my)) + (w[4] * up + w[5] * down)


def row_weights(weights, p, j, count):
    tile = weights[(p - 1) * TALL + j]
    return [jnp.broadcast_to(tile[k : k + 1, :], (8, 128)) for k in range(count)]


def solve(right, td, inv, consts):
    ur, ui, pr, pi = right
    shift_a, shift_b, lag = consts
    inv_a, inv_b = inv
    a = shift_a + td
    b = shift_b + td
    return (
        (a * ur + lag * ui - COUPLING * pr) * inv_a,
        (b * ui - lag * ur - COUPLING * pi) * inv_b,
        (TAU * ur + a * pr - lag * pi) * inv_a,
        (TAU * ui + b * pi + lag * pr) * inv_b,
    )


def over_sublanes(v):
    v = v + pltpu.roll(v, 4, 0)
    v = v + pltpu.roll(v, 2, 0)
    return v + pltpu.roll(v, 1, 0)


def front_body(far, near, own, wish, tnear, tfar, weights, consts, inv, fixed, it, out_near, out_far, zed):
    def field(p, j, c):
        if p == 2 or p == 3:
            return own[p - 2, j, c]
        side = near if p < 2 else far
        if p == 1 or p == 4:
            return side[(j - 1) * 4 + c]
        return side[72 + (j - 2) * 4 + c]

    def wanted(p, j, n):
        if p == 2 or p == 3:
            return wish[p - 2, j - 1, n]
        return (tnear if p == 1 else tfar)[136 + (j - 2) * 2 + n]

    cs = (consts[0], consts[1], consts[2])
    phase_a, phase_b, last_a, last_b, first_a, first_b, slot = (consts[i] for i in range(3, 10))
    for p, lo, hi in ((2, 1, 19), (3, 1, 19), (1, 2, 18), (4, 2, 18)):
        def row(j, carry, p=p):
            w = row_weights(weights, p, j, 8)
            v = [field(p, j, c) for c in range(4)]
            last = over_sublanes(last_a * v[0] + last_b * v[1])
            first = over_sublanes(first_a * v[2] + first_b * v[3])
            begin = w[7] - last
            kept = (
                begin,
                slot * begin,
                -TAU * wanted(p, j, 0) - phase_a * first,
                -TAU * wanted(p, j, 1) - phase_b * first,
            )
            at = region(p, j)
            pushed = []
            for c in range(4):
                fixed[at, c] = kept[c]
                around = (field(p + 1, j, c), field(p - 1, j, c), field(p, j + 1, c), field(p, j - 1, c))
                pushed.append(kept[c] + spread_sum(v[c], around, w))
            z = solve(pushed, w[6], (inv[at, 0], inv[at, 1]), cs)
            for c in range(4):
                zed[at, c] = z[c]
            return carry
        rows(lo, hi, row)

    for p in (2, 3):
        def row(j, carry, p=p):
            w = row_weights(weights, p, j, 8)
            at = region(p, j)
            pushed = []
            for c in range(4):
                around = (zed[region(p + 1, j), c], zed[region(p - 1, j), c], zed[at + 1, c], zed[at - 1, c])
                pushed.append(fixed[at, c] + spread_sum(zed[at, c], around, w))
            z = solve(pushed, w[6], (inv[at, 0], inv[at, 1]), cs)
            for c in range(4):
                it[p - 2, j - 2, c] = z[c]
            return carry
        rows(2, 18, row)
    out_near[0:14] = it[0, 1:15]
    out_near[14:26] = it[1, 2:14]
    out_far[0:14] = it[1, 1:15]
    out_far[14:26] = it[0, 2:14]


def sweep_body(it, near, far, fixed, weights, consts, inv, zed, put):
    def guess(p, j, c):
        if p == 2 or p == 3:
            return it[p - 2, j - 2, c]
        side = near if p < 2 else far
        if p == 1 or p == 4:
            return side[j - 3, c]
        return side[14 + j - 4, c]

    def at2(p, j):
        if p == 2 or p == 3:
            return (p - 2) * 14 + j - 3
        return (28 if p == 1 else 40) + j - 4

    cs = (consts[0], consts[1], consts[2])
    for p, lo, hi in ((2, 3, 17), (3, 3, 17), (1, 4, 16), (4, 4, 16)):
        def row(j, carry, p=p):
            w = row_weights(weights, p, j, 8)
            at = region(p, j)
            pushed = []
            for c in range(4):
                around = (guess(p + 1, j, c), guess(p - 1, j, c), guess(p, j + 1, c), guess(p, j - 1, c))
                pushed.append(fixed[at, c] + spread_sum(guess(p, j, c), around, w))
            z = solve(pushed, w[6], (inv[at, 0], inv[at, 1]), cs)
            for c in range(4):
                zed[at2(p, j), c] = z[c]
            return carry
        rows(lo, hi, row)
    for p in (2, 3):
        def row(j, carry, p=p):
            w = row_weights(weights, p, j, 8)
            at = region(p, j)
            here = at2(p, j)
            pushed = []
            for c in range(4):
                around = (zed[at2(p + 1, j), c], zed[at2(p - 1, j), c], zed[here + 1, c], zed[here - 1, c])
                pushed.append(fixed[at, c] + spread_sum(zed[here, c], around, w))
            z = solve(pushed, w[6], (inv[at, 0], inv[at, 1]), cs)
            for c in range(4):
                put(p - 2, j - 4, c, z[c])
            return carry
        rows(4, 16, row)


def middle_body(far, near, it, fixed, weights, consts, inv, new, out_near, out_far, send0, send1, zed):
    def put(x, j, c, v):
        new[x, j, c] = v
        first, second = (out_near, out_far) if x == 0 else (out_far, out_near)
        first[j, c] = v
        second[OWN + j, c] = v
    sweep_body(far=far, near=near, it=it, fixed=fixed, weights=weights, consts=consts, inv=inv, zed=zed, put=put)
    odd = place()[0] & 1
    for x in range(2):
        send0[x] = new[x, pl.ds((OWN - HALO) * (1 - odd), HALO)]
        send1[x] = new[x, pl.ds((OWN - HALO) * odd, HALO)]


def edges_body(far, near, row1, row0, new, own, send0, send1):
    odd = place()[0] & 1
    for x in range(2):
        own[x, HALO : HALO + OWN] = new[x]
    for row, send, high in ((row0, send0, 1 - odd), (row1, send1, odd)):
        for x in range(2):
            own[x, pl.ds(16 * high, HALO)] = row[x]
        for i, side in enumerate((near, far)):
            send[3 * i : 3 * i + 3] = side[pl.ds((OWN - 3) * high, 3)]
            send[6 + 2 * i : 8 + 2 * i] = side[pl.ds(OWN + (OWN - 2) * high, 2)]


def widen_body(edge1, edge0, near_x, far_x, near, far):
    odd = place()[0] & 1
    for out, got in ((near, near_x), (far, far_x)):
        out[3 : 3 + OWN] = got[0:OWN]
        out[20 : 20 + OWN] = got[OWN : 2 * OWN]
    for edge, high in ((edge0, 1 - odd), (edge1, odd)):
        for i, side in enumerate((near, far)):
            side[pl.ds(15 * high, 3)] = edge[3 * i : 3 * i + 3]
            side[pl.ds(18 + 14 * high, 2)] = edge[6 + 2 * i : 8 + 2 * i]


def last_body(far, near, it, fixed, weights, consts, inv, back, *rest):
    outs, (zed, fin, stage) = rest[:2], rest[2:]
    def put(x, j, c, v):
        fin[x * OWN + j, c] = v
    sweep_body(far=far, near=near, it=it, fixed=fixed, weights=weights, consts=consts, inv=inv, zed=zed, put=put)
    t, _ = place()
    matrix = back[...]
    for low in range(0, 2 * OWN, 4):
        done = transform(matrix, fin[low : low + 4].reshape(128, 128))
        for i in range(4):
            x, j = divmod(low + i, OWN)
            for c in range(4):
                stage[pl.ds((c * 2 + x) * OWN + j, 8, stride=8 * OWN), :] = done[(i * 4 + c) * 8 : (i * 4 + c + 1) * 8]
    for k in range(8):
        outs[k & 1][k >> 1] = stage[pl.ds(pl.multiple_of((t ^ k) * 8 * OWN, 8), 8 * OWN), :]


def merge_body(other, mine, *outs):
    for out, k in zip(outs, CHIPS):
        out[0] = mine[k]
        out[1] = other[k]


def unpack_body(a, b, c, other, mine, state, adjoint, stage, held, sems):
    t, s = place()
    flip = s & 1
    for ref, k in zip((a, b, c), CHIPS):
        stage[t ^ (2 * k)] = ref[0]
        stage[t ^ (2 * k + 1)] = ref[1]
    stage[t] = mine[0]
    stage[t ^ 1] = other[0]
    copies = []
    for f, ref in enumerate((state, adjoint)):
        for n in range(2):
            for x in range(2):
                base = ((f * 2 + n) * 2 + x) * OWN
                for d in range(8):
                    held[f, n, x, OWN * d : OWN * (d + 1), :] = stage[d, base : base + OWN, :]
                copies.append(
                    pltpu.make_async_copy(held.at[f, n, x], ref.at[n, x ^ flip], sems.at[(f * 2 + n) * 2 + x])
                )
                copies[-1].start()
    for copy in copies:
        copy.wait()


def exchange(pieces):
    count = lax.axis_size("tm")
    return [lax.ppermute(pieces[k], "tm", [(i, i ^ k) for i in range(count)]) for k in ORDER] + [pieces[0]]


def swap_rows(block, start):
    count = lax.axis_size("tm")
    route = []
    for i in range(start, start + count, 2):
        low, high = i % count, (i + 1) % count
        route += [(low, high), (high, low)]
    return lax.ppermute(block, "tm", route)


def swap_planes(block, start):
    sections, slabs = lax.axis_size("tm"), lax.axis_size("space")
    route = []
    for t in range(sections):
        for s in range(slabs):
            pair = s + 1 if (s - start) % 2 == 0 else s - 1
            to = t * slabs + pair if 0 <= pair < slabs else (t ^ 1) * slabs + s
            route.append((t * slabs + s, to))
    return lax.ppermute(block, ("tm", "space"), route)


def on_device(state_guess, adjoint_guess, target, initial_state, diffusivity):
    forward, back = (jnp.asarray(m) for m in transform_matrices())
    consts = jnp.asarray(mode_constants())

    arguments = (state_guess, adjoint_guess, target, diffusivity, initial_state, forward, back, consts)
    *pieces, near_c, far_c, here_c, forward, back, consts = call(
        pack_body,
        "pack",
        [whole(PIECE, 128)] * 8 + [whole(3, TALL, 128)] * 2 + [whole(4, TALL, 128)]
        + [whole(128, 128)] * 2 + [whole(10, 8, 128)],
        0,
        [pltpu.VMEM((8, PIECE, 128), jnp.float32)]
        + [pltpu.VMEM((2, 2, 96, 128), jnp.float32)] * 3
        + [pltpu.VMEM((2, 96, 128), jnp.float32)] * 2
        + [pltpu.SemaphoreType.DMA((11,))],
        far_inputs=8,
    )(*(pltpu.with_memory_space_constraint(a, pltpu.HBM) for a in arguments))
    got = exchange(pieces)
    own, wish, near, far = call(
        spread_body,
        "spread",
        [whole(2, WIN, 4, 8, 128), whole(2, 18, 2, 8, 128), whole(177, 8, 128), whole(177, 8, 128)],
        11,
        [pltpu.VMEM((8 * PIECE, 128), jnp.float32)],
    )(*got, near_c, far_c, forward)
    far = far_first = swap_planes(far, 0)
    near = near_first = swap_planes(near, 1)
    weights, inv = call(
        coefficient_body, "coefficients", [whole(4 * TALL * 8, 128), whole(68, 2, 8, 128)], 4
    )(far, near, here_c, consts)
    weights = weights.reshape(4 * TALL, 8, 128)

    sweep_scratch = [pltpu.VMEM((52, 4, 8, 128), jnp.float32)]
    for outer in range(OUTER):
        fixed, it, near_z, far_z = call(
            front_body,
            "front",
            [whole(68, 4, 8, 128), whole(2, 16, 4, 8, 128), whole(26, 4, 8, 128), whole(26, 4, 8, 128)],
            9,
            [pltpu.VMEM((68, 4, 8, 128), jnp.float32)],
        )(far, near, own, wish, near_first, far_first, weights, consts, inv)
        far_z = swap_planes(far_z, 0)
        near_z = swap_planes(near_z, 1)
        if outer < OUTER - 1:
            new, near, far, row0, row1 = call(
                middle_body,
                "middle",
                [whole(2, OWN, 4, 8, 128)] + [whole(2 * OWN, 4, 8, 128)] * 2 + [whole(2, HALO, 4, 8, 128)] * 2,
                7,
                sweep_scratch,
            )(far_z, near_z, it, fixed, weights, consts, inv)
            far = swap_planes(far, 0)
            near = swap_planes(near, 1)
            row1 = swap_rows(row1, 1)
            row0 = swap_rows(row0, 0)
            own, edge0, edge1 = call(
                edges_body, "edges", [whole(2, WIN, 4, 8, 128)] + [whole(10, 4, 8, 128)] * 2, 5
            )(far, near, row1, row0, new)
            edge1 = swap_rows(edge1, 1)
            edge0 = swap_rows(edge0, 0)
            near, far = call(widen_body, "widen", [whole(34, 4, 8, 128)] * 2, 4)(edge1, edge0, near, far)
            near = near.reshape(136, 8, 128)
            far = far.reshape(136, 8, 128)
    mine, other = call(
        last_body,
        "last",
        [whole(4, 8 * OWN, 128)] * 2,
        8,
        sweep_scratch + [pltpu.VMEM((2 * OWN, 4, 8, 128), jnp.float32), pltpu.VMEM((64 * OWN, 128), jnp.float32)],
    )(far_z, near_z, it, fixed, weights, consts, inv, back)
    other = swap_rows(other, 0)
    pairs = call(merge_body, "merge", [whole(2, 8 * OWN, 128)] * 3, 2)(other, mine)
    count = lax.axis_size("tm")
    got = [
        lax.ppermute(pair, "tm", [(i, i ^ (2 * k)) for i in range(count)]) for pair, k in zip(pairs, CHIPS)
    ]
    return tuple(
        call(
            unpack_body,
            "unpack",
            [whole(2, 2, 96, 128)] * 2,
            5,
            [
                pltpu.VMEM((8, 8 * OWN, 128), jnp.float32),
                pltpu.VMEM((2, 2, 2, 96, 128), jnp.float32),
                pltpu.SemaphoreType.DMA((8,)),
            ],
            far_outputs=True,
        )(*got, other, mine)
    )


def solution(mesh):
    in_specs = (
        P("tm", "space", None, None),
        P("tm", "space", None, None),
        P("tm", "space", None, None),
        P("space", None, None),
        P("space", None, None),
    )
    out_specs = (P("tm", "space", None, None), P("tm", "space", None, None))
    return jax.shard_map(
        on_device, mesh=mesh, in_specs=in_specs, out_specs=out_specs, check_vma=False
    )
```

```python
import math

import jax
import jax.numpy as jnp
import numpy as np
from jax import lax
from jax.experimental import pallas as pl
from jax.experimental.pallas import tpu as pltpu
from jax.sharding import PartitionSpec as P

TAU = 0.25
COUPLING = 5.0
DET_SHIFT = 1.25
OUTER = 2

OWN = 12
HALO = 4
WIN = OWN + 2 * HALO
ORDER = (4, 2, 6, 5, 3, 7, 1)
PIECE = 8 * WIN + 4 * (WIN - 2)
CHIPS = (2, 1, 3)
TALL = 24


def place():
    return lax.axis_index("tm"), lax.axis_index("space")


def transform_matrices():
    modes = np.arange(8)[:, None]
    steps = np.concatenate([np.arange(0, 16, 2), np.arange(1, 16, 2)])[None, :]
    angle = 2.0 * np.pi * ((modes * steps) % 16) / 16.0
    real, imag = np.cos(angle), -np.sin(angle)
    imag[0] = np.where(steps[0] % 2 == 0, 1.0, -1.0)
    forward = np.concatenate([real, imag], 0)
    back = forward.T.copy() / 8.0
    back[:, 0] /= 2.0
    back[:, 8] /= 2.0
    eye = np.eye(8)
    return np.kron(eye, forward).astype(np.float32), np.kron(eye, back).astype(np.float32)


def mode_constants():
    theta = 2.0 * np.pi * np.arange(8) / 16.0
    shift_a = 1.0 - np.cos(theta)
    shift_b = shift_a.copy()
    shift_b[0] = 2.0
    lag = np.sin(theta)
    phase_a, phase_b = np.cos(theta), np.sin(theta)
    phase_b[0] = -1.0
    share = np.where(np.arange(8) == 0, 1.0, 2.0) / 16.0
    last_a, last_b = share * np.cos(15.0 * theta), -share * np.sin(15.0 * theta)
    last_b[0] = -1.0 / 16.0
    first_a, first_b = share, np.where(np.arange(8) == 0, 1.0, 0.0) / 16.0
    slot = np.where(np.arange(8) == 0, 1.0, 0.0)
    kinds = [shift_a, shift_b, lag, phase_a, phase_b, last_a, last_b, first_a, first_b, slot]
    return (np.stack(kinds)[:, :, None] * np.ones((1, 1, 128))).astype(np.float32)


def whole(*shape):
    return jax.ShapeDtypeStruct(shape, jnp.float32)


def call(body, name, outs, n_in, scratch=(), far_inputs=0, far_outputs=False):
    vmem = pl.BlockSpec(memory_space=pltpu.VMEM)
    anywhere = pl.BlockSpec(memory_space=pltpu.HBM)
    return pl.pallas_call(
        body,
        name=name,
        out_shape=outs,
        in_specs=[anywhere] * far_inputs + [vmem] * n_in,
        out_specs=[anywhere if far_outputs else vmem] * len(outs),
        scratch_shapes=list(scratch),
        compiler_params=pltpu.CompilerParams(vmem_limit_bytes=16 * 1024 * 1024),
    )


def rows(lo, hi, body):
    lax.fori_loop(lo, hi, body, 0, unroll=True)


def piece_row(f, n, x):
    return ((f * 2 + n) * 2 + x) * WIN if f < 2 else 8 * WIN + (n * 2 + x) * (WIN - 2)


def pack_body(*rest):
    sources, outs, (near, far, here), tables = rest[:8], rest[8:16], rest[16:19], rest[19:22]
    stage, held, sems = rest[22], rest[23:28], rest[28]
    slabs = [
        pltpu.make_async_copy(sources[f].at[n], held[f].at[n], sems.at[2 * f + n]) for f in range(3) for n in range(2)
    ]
    copies = [pltpu.make_async_copy(sources[3 + i], ref, sems.at[6 + i]) for i, ref in enumerate(held[3:] + tables)]
    for copy in slabs + copies:
        copy.start()
    state, adjoint, target, kappa, begin = held
    t, s = place()
    flip = s & 1
    for f, ref in enumerate((state, adjoint, target)):
        for n in range(2):
            slabs[2 * f + n].wait()
            for x in range(2):
                base = piece_row(f, n, x)
                size = WIN if f < 2 else WIN - 2
                for d in range(8):
                    low = OWN * d - (HALO if f < 2 else HALO - 1)
                    first, last = max(low, 0), min(low + size, 96)
                    stage[d, base + first - low : base + last - low, :] = ref[n, x ^ flip, first:last, :]
                    if first > low:
                        stage[d, base : base + first - low, :] = jnp.zeros((first - low, 128), jnp.float32)
                    if last < low + size:
                        stage[d, base + last - low : base + size, :] = jnp.zeros((low + size - last, 128), jnp.float32)
    for k in range(8):
        outs[k][...] = stage[t ^ k]
    for copy in copies:
        copy.wait()
    for d in range(8):
        @pl.when(t == d)
        def window(d=d):
            low = OWN * d - HALO
            first, last = max(low, 0), min(low + TALL, 96)
            parts = []
            for ref, x in ((kappa, 0), (kappa, 1), (begin, 0), (begin, 1)):
                v = ref[x ^ flip, first:last, :]
                if first > low:
                    v = jnp.concatenate([jnp.zeros((first - low, 128), jnp.float32), v], 0)
                if last < low + TALL:
                    v = jnp.concatenate([v, jnp.zeros((low + TALL - last, 128), jnp.float32)], 0)
                parts.append(v)
            for i, v in enumerate(parts):
                here[i] = v
            for i, q in enumerate((0, 1, 2)):
                near[i] = parts[q]
            for i, q in enumerate((1, 0, 3)):
                far[i] = parts[q]


def coefficient_body(far, near, here, consts, weights, inv):
    t, s = place()
    flip = s & 1
    kappa = [near[1], near[0], here[0], here[1], far[0], far[1]]
    for p in range(6):
        plane = jnp.where(flip == 1, 2 * s + 3 - p, 2 * s - 2 + p)
        kappa[p] = kappa[p] * jnp.where((plane >= 0) & (plane < 64), 1.0, 0.0)
    begin = [near[2], here[2], here[3], far[2]]
    lane = lax.broadcasted_iota(jnp.int32, (TALL, 128), 1)
    row = lax.broadcasted_iota(jnp.int32, (TALL, 128), 0) + (OWN * t - HALO)
    half = 0.5 * TAU
    for p in range(1, 5):
        plane = jnp.where(flip == 1, 2 * s + 3 - p, 2 * s - 2 + p)
        ahead = jnp.where(flip == 1, plane - 1, plane + 1)
        behind = jnp.where(flip == 1, plane + 1, plane - 1)
        real = jnp.where((plane >= 0) & (plane < 64), half, 0.0)
        to_ahead = jnp.where((ahead >= 0) & (ahead < 64), real, 0.0)
        to_behind = jnp.where((behind >= 0) & (behind < 64), real, 0.0)
        k = kappa[p]
        row_ok = (row >= 0) & (row < 96)
        xp = k + kappa[p + 1]
        xm = k + kappa[p - 1]
        yp = k + pltpu.roll(k, TALL - 1, 0)
        ym = k + pltpu.roll(k, 1, 0)
        zp = k + jnp.where(lane < 127, pltpu.roll(k, 127, 1), 0.0)
        zm = k + jnp.where(lane > 0, pltpu.roll(k, 1, 1), 0.0)
        kinds = [
            jnp.where(row_ok, xp * to_ahead, 0.0),
            jnp.where(row_ok, xm * to_behind, 0.0),
            jnp.where(row_ok & (row < 95), yp * real, 0.0),
            jnp.where(row_ok & (row > 0), ym * real, 0.0),
            jnp.where(row_ok & (lane < 127), zp * real, 0.0),
            jnp.where(row_ok & (lane > 0), zm * real, 0.0),
            half * (((xp + xm) + (yp + ym)) + (zp + zm)),
            begin[p - 1],
        ]
        for i, v in enumerate(kinds):
            weights[pl.ds((p - 1) * TALL * 8 + i, TALL, stride=8), :] = v
    ca, cb, lag = consts[0], consts[1], consts[2]
    base = lag * lag + DET_SHIFT
    for p, lo, hi in ((2, 1, 19), (3, 1, 19), (1, 2, 18), (4, 2, 18)):
        for j in range(lo, hi):
            td = jnp.broadcast_to(weights[pl.ds(((p - 1) * TALL + j) * 8 + 6, 1), :], (8, 128))
            a = ca + td
            b = cb + td
            at = region(p, j)
            inv[at, 0] = 1.0 / (a * a + base)
            inv[at, 1] = 1.0 / (b * b + base)


def spread_body(*rest):
    pieces, forward, (own, wish, near, far), stage = rest[:8], rest[10], rest[11:15], rest[15]
    t, _ = place()
    rows = PIECE
    for k, piece in zip(ORDER + (0,), pieces):
        stage[pl.ds(pl.multiple_of((t ^ k) * rows, 8), rows), :] = piece[...]

    def steps(f, n, x, j):
        return stage[pl.ds(piece_row(f, n, x) + j - (0 if f < 2 else 1), 8, stride=rows), :]

    matrix = forward[...]
    for x in range(2):
        for low in range(0, WIN, 4):
            block = [steps(f, n, x, low + i) for i in range(4) for f in range(2) for n in range(2)]
            done = transform(matrix, jnp.concatenate(block, 0))
            for i in range(4):
                for c in range(4):
                    v = done[(i * 4 + c) * 8 : (i * 4 + c + 1) * 8]
                    own[x, low + i, c] = v
                    put_field(near, far, x, low + i, c, v)
    cells = [(x, j) for x in range(2) for j in range(1, WIN - 1)]
    for low in range(0, len(cells), 8):
        block = jnp.concatenate([steps(2, n, x, j) for x, j in cells[low : low + 8] for n in range(2)], 0)
        done = transform(matrix[: len(block), : len(block)], block)
        for i, (x, j) in enumerate(cells[low : low + 8]):
            for n in range(2):
                v = done[(i * 2 + n) * 8 : (i * 2 + n + 1) * 8]
                wish[x, j - 1, n] = v
                if 2 <= j <= 17:
                    out = far if x == 1 else near
                    out[136 + (j - 2) * 2 + n] = v


def transform(matrix, block):
    return jnp.dot(matrix, block, precision=lax.Precision.HIGHEST, preferred_element_type=jnp.float32)


def put_field(near, far, x, j, c, v):
    first, second = (near, far) if x == 0 else (far, near)
    if 1 <= j <= 18:
        first[(j - 1) * 4 + c] = v
    if 2 <= j <= 17:
        second[72 + (j - 2) * 4 + c] = v


def region(p, j):
    if p == 2 or p == 3:
        return (p - 2) * 18 + j - 1
    return (36 if p == 1 else 52) + j - 2


def spread_sum(v, around, w):
    px, mx, py, my = around
    up = pltpu.roll(v, 127, 1)
    down = pltpu.roll(v, 1, 1)
    return ((w[0] * px + w[1] * mx) + (w[2] * py + w[3] * my)) + (w[4] * up + w[5] * down)


def row_weights(weights, p, j, count):
    tile = weights[(p - 1) * TALL + j]
    return [jnp.broadcast_to(tile[k : k + 1, :], (8, 128)) for k in range(count)]


def solve(right, td, inv, consts):
    ur, ui, pr, pi = right
    shift_a, shift_b, lag = consts
    inv_a, inv_b = inv
    a = shift_a + td
    b = shift_b + td
    return (
        (a * ur + lag * ui - COUPLING * pr) * inv_a,
        (b * ui - lag * ur - COUPLING * pi) * inv_b,
        (TAU * ur + a * pr - lag * pi) * inv_a,
        (TAU * ui + b * pi + lag * pr) * inv_b,
    )


def over_sublanes(v):
    v = v + pltpu.roll(v, 4, 0)
    v = v + pltpu.roll(v, 2, 0)
    return v + pltpu.roll(v, 1, 0)


def own_sum(v, other, py, my, w, p):
    up = pltpu.roll(v, 127, 1)
    down = pltpu.roll(v, 1, 1)
    return ((w[0] if p == 2 else w[1]) * other + (w[2] * py + w[3] * my)) + (w[4] * up + w[5] * down)


def kept_parts(v, wanted, begin, consts):
    phase_a, phase_b, last_a, last_b, first_a, first_b, slot = (consts[i] for i in range(3, 10))
    begin = begin - over_sublanes(last_a * v[0] + last_b * v[1])
    first = over_sublanes(first_a * v[2] + first_b * v[3])
    return begin, slot * begin, -TAU * wanted[0] - phase_a * first, -TAU * wanted[1] - phase_b * first


def prepare_body(own, wish, weights, consts, kept, part):
    for p in (2, 3):
        def row(j, carry, p=p):
            x = p - 2
            w = row_weights(weights, p, j, 8)
            v = [own[x, j, c] for c in range(4)]
            at = region(p, j)
            for c, k in enumerate(kept_parts(v, (wish[x, j - 1, 0], wish[x, j - 1, 1]), w[7], consts)):
                kept[at, c] = k
                part[at, c] = k + own_sum(v[c], own[1 - x, j, c], own[x, j + 1, c], own[x, j - 1, c], w, p)
            return carry
        rows(1, 19, row)


def ahead_body(it, kept, weights, part):
    for p in (2, 3):
        def row(j, carry, p=p):
            x = p - 2
            w = row_weights(weights, p, j, 6)
            for c in range(4):
                around = own_sum(it[x, j - 2, c], it[1 - x, j - 2, c], it[x, j - 1, c], it[x, j - 3, c], w, p)
                part[x * 14 + j - 3, c] = kept[region(p, j), c] + around
            return carry
        rows(3, 17, row)


def front_body(far, near, own, tnear, tfar, weights, consts, inv, kept, part, side, it, out_near, out_far, zed):
    def field(p, j, c):
        if p == 2 or p == 3:
            return own[p - 2, j, c]
        got = near if p < 2 else far
        if p == 1 or p == 4:
            return got[(j - 1) * 4 + c]
        return got[72 + (j - 2) * 4 + c]

    cs = (consts[0], consts[1], consts[2])
    for p in (2, 3):
        def row(j, carry, p=p):
            w = row_weights(weights, p, j, 8)
            at = region(p, j)
            pushed = []
            for c in range(4):
                pushed.append(part[at, c] + (w[1] * field(1, j, c) if p == 2 else w[0] * field(4, j, c)))
            z = solve(pushed, w[6], (inv[at, 0], inv[at, 1]), cs)
            for c in range(4):
                zed[at, c] = z[c]
            return carry
        rows(1, 19, row)
    for p in (1, 4):
        def row(j, carry, p=p):
            w = row_weights(weights, p, j, 8)
            v = [field(p, j, c) for c in range(4)]
            wanted = [(tnear if p == 1 else tfar)[136 + (j - 2) * 2 + n] for n in range(2)]
            at = region(p, j)
            pushed = []
            for c, k in enumerate(kept_parts(v, wanted, w[7], consts)):
                side[at - 36, c] = k
                around = (field(p + 1, j, c), field(p - 1, j, c), field(p, j + 1, c), field(p, j - 1, c))
                pushed.append(k + spread_sum(v[c], around, w))
            z = solve(pushed, w[6], (inv[at, 0], inv[at, 1]), cs)
            for c in range(4):
                zed[at, c] = z[c]
            return carry
        rows(2, 18, row)

    for p in (2, 3):
        def row(j, carry, p=p):
            w = row_weights(weights, p, j, 8)
            at = region(p, j)
            pushed = []
            for c in range(4):
                around = (zed[region(p + 1, j), c], zed[region(p - 1, j), c], zed[at + 1, c], zed[at - 1, c])
                pushed.append(kept[at, c] + spread_sum(zed[at, c], around, w))
            z = solve(pushed, w[6], (inv[at, 0], inv[at, 1]), cs)
            for c in range(4):
                it[p - 2, j - 2, c] = z[c]
            return carry
        rows(2, 18, row)
    out_near[0:14] = it[0, 1:15]
    out_near[14:26] = it[1, 2:14]
    out_far[0:14] = it[1, 1:15]
    out_far[14:26] = it[0, 2:14]


def sweep_body(it, near, far, kept, side, part, weights, consts, inv, zed, put):
    def guess(p, j, c):
        if p == 2 or p == 3:
            return it[p - 2, j - 2, c]
        side = near if p < 2 else far
        if p == 1 or p == 4:
            return side[j - 3, c]
        return side[14 + j - 4, c]

    def at2(p, j):
        if p == 2 or p == 3:
            return (p - 2) * 14 + j - 3
        return (28 if p == 1 else 40) + j - 4

    cs = (consts[0], consts[1], consts[2])
    for p, lo, hi in ((2, 3, 17), (3, 3, 17), (1, 4, 16), (4, 4, 16)):
        def row(j, carry, p=p):
            w = row_weights(weights, p, j, 8)
            at = region(p, j)
            pushed = []
            for c in range(4):
                if p == 2 or p == 3:
                    beside = w[1] * guess(1, j, c) if p == 2 else w[0] * guess(4, j, c)
                    pushed.append(part[at2(p, j), c] + beside)
                    continue
                around = (guess(p + 1, j, c), guess(p - 1, j, c), guess(p, j + 1, c), guess(p, j - 1, c))
                pushed.append(side[at - 36, c] + spread_sum(guess(p, j, c), around, w))
            z = solve(pushed, w[6], (inv[at, 0], inv[at, 1]), cs)
            for c in range(4):
                zed[at2(p, j), c] = z[c]
            return carry
        rows(lo, hi, row)
    for p in (2, 3):
        def row(j, carry, p=p):
            w = row_weights(weights, p, j, 8)
            at = region(p, j)
            here = at2(p, j)
            pushed = []
            for c in range(4):
                around = (zed[at2(p + 1, j), c], zed[at2(p - 1, j), c], zed[here + 1, c], zed[here - 1, c])
                pushed.append(kept[at, c] + spread_sum(zed[here, c], around, w))
            z = solve(pushed, w[6], (inv[at, 0], inv[at, 1]), cs)
            for c in range(4):
                put(p - 2, j - 4, c, z[c])
            return carry
        rows(4, 16, row)


def middle_body(far, near, it, kept, side, part, weights, consts, inv, new, out_near, out_far, send0, send1, zed):
    def put(x, j, c, v):
        new[x, j, c] = v
        first, second = (out_near, out_far) if x == 0 else (out_far, out_near)
        first[j, c] = v
        second[OWN + j, c] = v
    sweep_body(far=far, near=near, it=it, kept=kept, side=side, part=part, weights=weights, consts=consts, inv=inv, zed=zed, put=put)
    odd = place()[0] & 1
    for x in range(2):
        send0[x] = new[x, pl.ds((OWN - HALO) * (1 - odd), HALO)]
        send1[x] = new[x, pl.ds((OWN - HALO) * odd, HALO)]


def edges_body(far, near, row1, row0, new, own, send0, send1):
    odd = place()[0] & 1
    for x in range(2):
        own[x, HALO : HALO + OWN] = new[x]
    for row, send, high in ((row0, send0, 1 - odd), (row1, send1, odd)):
        for x in range(2):
            own[x, pl.ds(16 * high, HALO)] = row[x]
        for i, side in enumerate((near, far)):
            send[3 * i : 3 * i + 3] = side[pl.ds((OWN - 3) * high, 3)]
            send[6 + 2 * i : 8 + 2 * i] = side[pl.ds(OWN + (OWN - 2) * high, 2)]


def widen_body(edge1, edge0, near_x, far_x, near, far):
    odd = place()[0] & 1
    for out, got in ((near, near_x), (far, far_x)):
        out[3 : 3 + OWN] = got[0:OWN]
        out[20 : 20 + OWN] = got[OWN : 2 * OWN]
    for edge, high in ((edge0, 1 - odd), (edge1, odd)):
        for i, side in enumerate((near, far)):
            side[pl.ds(15 * high, 3)] = edge[3 * i : 3 * i + 3]
            side[pl.ds(18 + 14 * high, 2)] = edge[6 + 2 * i : 8 + 2 * i]


def last_body(far, near, it, kept, side, part, weights, consts, inv, back, *rest):
    outs, (zed, fin, stage) = rest[:2], rest[2:]
    def put(x, j, c, v):
        fin[x * OWN + j, c] = v
    sweep_body(far=far, near=near, it=it, kept=kept, side=side, part=part, weights=weights, consts=consts, inv=inv, zed=zed, put=put)
    t, _ = place()
    matrix = back[...]
    for low in range(0, 2 * OWN, 4):
        done = transform(matrix, fin[low : low + 4].reshape(128, 128))
        for i in range(4):
            x, j = divmod(low + i, OWN)
            for c in range(4):
                stage[pl.ds((c * 2 + x) * OWN + j, 8, stride=8 * OWN), :] = done[(i * 4 + c) * 8 : (i * 4 + c + 1) * 8]
    for k in range(8):
        outs[k & 1][k >> 1] = stage[pl.ds(pl.multiple_of((t ^ k) * 8 * OWN, 8), 8 * OWN), :]


def merge_body(other, mine, *outs):
    for out, k in zip(outs, CHIPS):
        out[0] = mine[k]
        out[1] = other[k]


def unpack_body(a, b, c, other, mine, state, adjoint, stage, held, sems):
    t, s = place()
    flip = s & 1
    for ref, k in zip((a, b, c), CHIPS):
        stage[t ^ (2 * k)] = ref[0]
        stage[t ^ (2 * k + 1)] = ref[1]
    stage[t] = mine[0]
    stage[t ^ 1] = other[0]
    copies = []
    for f, ref in enumerate((state, adjoint)):
        for n in range(2):
            for x in range(2):
                base = ((f * 2 + n) * 2 + x) * OWN
                for d in range(8):
                    held[f, n, x, OWN * d : OWN * (d + 1), :] = stage[d, base : base + OWN, :]
                copies.append(
                    pltpu.make_async_copy(held.at[f, n, x], ref.at[n, x ^ flip], sems.at[(f * 2 + n) * 2 + x])
                )
                copies[-1].start()
    for copy in copies:
        copy.wait()


def exchange(pieces):
    count = lax.axis_size("tm")
    return [lax.ppermute(pieces[k], "tm", [(i, i ^ k) for i in range(count)]) for k in ORDER] + [pieces[0]]


def swap_rows(block, start):
    count = lax.axis_size("tm")
    route = []
    for i in range(start, start + count, 2):
        low, high = i % count, (i + 1) % count
        route += [(low, high), (high, low)]
    return lax.ppermute(block, "tm", route)


def swap_planes(block, start):
    sections, slabs = lax.axis_size("tm"), lax.axis_size("space")
    route = []
    for t in range(sections):
        for s in range(slabs):
            pair = s + 1 if (s - start) % 2 == 0 else s - 1
            to = t * slabs + pair if 0 <= pair < slabs else (t ^ 1) * slabs + s
            route.append((t * slabs + s, to))
    return lax.ppermute(block, ("tm", "space"), route)


def on_device(state_guess, adjoint_guess, target, initial_state, diffusivity):
    forward, back = (jnp.asarray(m) for m in transform_matrices())
    consts = jnp.asarray(mode_constants())

    arguments = (state_guess, adjoint_guess, target, diffusivity, initial_state, forward, back, consts)
    *pieces, near_c, far_c, here_c, forward, back, consts = call(
        pack_body,
        "pack",
        [whole(PIECE, 128)] * 8 + [whole(3, TALL, 128)] * 2 + [whole(4, TALL, 128)]
        + [whole(128, 128)] * 2 + [whole(10, 8, 128)],
        0,
        [pltpu.VMEM((8, PIECE, 128), jnp.float32)]
        + [pltpu.VMEM((2, 2, 96, 128), jnp.float32)] * 3
        + [pltpu.VMEM((2, 96, 128), jnp.float32)] * 2
        + [pltpu.SemaphoreType.DMA((11,))],
        far_inputs=8,
    )(*(pltpu.with_memory_space_constraint(a, pltpu.HBM) for a in arguments))
    got = exchange(pieces)
    far_c = swap_planes(far_c, 0)
    near_c = swap_planes(near_c, 1)
    own, wish, near, far = call(
        spread_body,
        "spread",
        [whole(2, WIN, 4, 8, 128), whole(2, 18, 2, 8, 128), whole(168, 8, 128), whole(168, 8, 128)],
        11,
        [pltpu.VMEM((8 * PIECE, 128), jnp.float32)],
    )(*got, far_c, near_c, forward)
    far = far_first = swap_planes(far, 0)
    near = near_first = swap_planes(near, 1)
    weights, inv = call(
        coefficient_body, "coefficients", [whole(4 * TALL * 8, 128), whole(68, 2, 8, 128)], 4
    )(far_c, near_c, here_c, consts)
    weights = weights.reshape(4 * TALL, 8, 128)

    sweep_scratch = [pltpu.VMEM((52, 4, 8, 128), jnp.float32)]
    for outer in range(OUTER):
        kept, part = call(prepare_body, "prepare", [whole(36, 4, 8, 128)] * 2, 4)(own, wish, weights, consts)
        side, it, near_z, far_z = call(
            front_body,
            "front",
            [whole(32, 4, 8, 128), whole(2, 16, 4, 8, 128), whole(26, 4, 8, 128), whole(26, 4, 8, 128)],
            10,
            [pltpu.VMEM((68, 4, 8, 128), jnp.float32)],
        )(far, near, own, near_first, far_first, weights, consts, inv, kept, part)
        ahead = call(ahead_body, "ahead", [whole(28, 4, 8, 128)], 3)(it, kept, weights)[0]
        far_z = swap_planes(far_z, 0)
        near_z = swap_planes(near_z, 1)
        if outer < OUTER - 1:
            new, near, far, row0, row1 = call(
                middle_body,
                "middle",
                [whole(2, OWN, 4, 8, 128)] + [whole(2 * OWN, 4, 8, 128)] * 2 + [whole(2, HALO, 4, 8, 128)] * 2,
                9,
                sweep_scratch,
            )(far_z, near_z, it, kept, side, ahead, weights, consts, inv)
            far = swap_planes(far, 0)
            near = swap_planes(near, 1)
            row1 = swap_rows(row1, 1)
            row0 = swap_rows(row0, 0)
            own, edge0, edge1 = call(
                edges_body, "edges", [whole(2, WIN, 4, 8, 128)] + [whole(10, 4, 8, 128)] * 2, 5
            )(far, near, row1, row0, new)
            edge1 = swap_rows(edge1, 1)
            edge0 = swap_rows(edge0, 0)
            near, far = call(widen_body, "widen", [whole(34, 4, 8, 128)] * 2, 4)(edge1, edge0, near, far)
            near = near.reshape(136, 8, 128)
            far = far.reshape(136, 8, 128)
    mine, other = call(
        last_body,
        "last",
        [whole(4, 8 * OWN, 128)] * 2,
        10,
        sweep_scratch + [pltpu.VMEM((2 * OWN, 4, 8, 128), jnp.float32), pltpu.VMEM((64 * OWN, 128), jnp.float32)],
    )(far_z, near_z, it, kept, side, ahead, weights, consts, inv, back)
    other = swap_rows(other, 0)
    pairs = call(merge_body, "merge", [whole(2, 8 * OWN, 128)] * 3, 2)(other, mine)
    count = lax.axis_size("tm")
    got = [
        lax.ppermute(pair, "tm", [(i, i ^ (2 * k)) for i in range(count)]) for pair, k in zip(pairs, CHIPS)
    ]
    return tuple(
        call(
            unpack_body,
            "unpack",
            [whole(2, 2, 96, 128)] * 2,
            5,
            [
                pltpu.VMEM((8, 8 * OWN, 128), jnp.float32),
                pltpu.VMEM((2, 2, 2, 96, 128), jnp.float32),
                pltpu.SemaphoreType.DMA((8,)),
            ],
            far_outputs=True,
        )(*got, other, mine)
    )


def solution(mesh):
    in_specs = (
        P("tm", "space", None, None),
        P("tm", "space", None, None),
        P("tm", "space", None, None),
        P("space", None, None),
        P("space", None, None),
    )
    out_specs = (P("tm", "space", None, None), P("tm", "space", None, None))
    return jax.shard_map(
        on_device, mesh=mesh, in_specs=in_specs, out_specs=out_specs, check_vma=False
    )
```

```python
import math

import jax
import jax.numpy as jnp
import numpy as np
from jax import lax
from jax.experimental import pallas as pl
from jax.experimental.pallas import tpu as pltpu
from jax.sharding import PartitionSpec as P

TAU = 0.25
COUPLING = 5.0
DET_SHIFT = 1.25
OUTER = 2

OWN = 12
HALO = 4
WIN = OWN + 2 * HALO
ORDER = (4, 2, 6, 5, 3, 7, 1)
PIECE = 8 * WIN + 4 * (WIN - 2)
CHIPS = (2, 1, 3)
TALL = 24


def place():
    return lax.axis_index("tm"), lax.axis_index("space")


def transform_matrices():
    modes = np.arange(8)[:, None]
    steps = np.concatenate([np.arange(0, 16, 2), np.arange(1, 16, 2)])[None, :]
    angle = 2.0 * np.pi * ((modes * steps) % 16) / 16.0
    real, imag = np.cos(angle), -np.sin(angle)
    imag[0] = np.where(steps[0] % 2 == 0, 1.0, -1.0)
    forward = np.concatenate([real, imag], 0)
    back = forward.T.copy() / 8.0
    back[:, 0] /= 2.0
    back[:, 8] /= 2.0
    eye = np.eye(8)
    return np.kron(eye, forward).astype(np.float32), np.kron(eye, back).astype(np.float32)


def mode_constants():
    theta = 2.0 * np.pi * np.arange(8) / 16.0
    shift_a = 1.0 - np.cos(theta)
    shift_b = shift_a.copy()
    shift_b[0] = 2.0
    lag = np.sin(theta)
    phase_a, phase_b = np.cos(theta), np.sin(theta)
    phase_b[0] = -1.0
    share = np.where(np.arange(8) == 0, 1.0, 2.0) / 16.0
    last_a, last_b = share * np.cos(15.0 * theta), -share * np.sin(15.0 * theta)
    last_b[0] = -1.0 / 16.0
    first_a, first_b = share, np.where(np.arange(8) == 0, 1.0, 0.0) / 16.0
    slot = np.where(np.arange(8) == 0, 1.0, 0.0)
    kinds = [shift_a, shift_b, lag, phase_a, phase_b, last_a, last_b, first_a, first_b, slot]
    return (np.stack(kinds)[:, :, None] * np.ones((1, 1, 128))).astype(np.float32)


def whole(*shape):
    return jax.ShapeDtypeStruct(shape, jnp.float32)


def call(body, name, outs, n_in, scratch=(), far_inputs=0, far_outputs=False):
    vmem = pl.BlockSpec(memory_space=pltpu.VMEM)
    anywhere = pl.BlockSpec(memory_space=pltpu.HBM)
    return pl.pallas_call(
        body,
        name=name,
        out_shape=outs,
        in_specs=[anywhere] * far_inputs + [vmem] * n_in,
        out_specs=[anywhere if far_outputs else vmem] * len(outs),
        scratch_shapes=list(scratch),
        compiler_params=pltpu.CompilerParams(vmem_limit_bytes=16 * 1024 * 1024),
    )


def rows(lo, hi, body):
    lax.fori_loop(lo, hi, body, 0, unroll=True)


def piece_row(f, n, x):
    return ((f * 2 + n) * 2 + x) * WIN if f < 2 else 8 * WIN + (n * 2 + x) * (WIN - 2)


def pack_body(*rest):
    sources, outs, (near, far, here), tables = rest[:8], rest[8:16], rest[16:19], rest[19:22]
    stage, held, sems = rest[22], rest[23:28], rest[28]
    slabs = [
        pltpu.make_async_copy(sources[f].at[n], held[f].at[n], sems.at[2 * f + n]) for f in range(3) for n in range(2)
    ]
    copies = [pltpu.make_async_copy(sources[3 + i], ref, sems.at[6 + i]) for i, ref in enumerate(held[3:] + tables)]
    for copy in slabs + copies:
        copy.start()
    state, adjoint, target, kappa, begin = held
    t, s = place()
    flip = s & 1
    for f, ref in enumerate((state, adjoint, target)):
        for n in range(2):
            slabs[2 * f + n].wait()
            for x in range(2):
                base = piece_row(f, n, x)
                size = WIN if f < 2 else WIN - 2
                for d in range(8):
                    low = OWN * d - (HALO if f < 2 else HALO - 1)
                    first, last = max(low, 0), min(low + size, 96)
                    stage[d, base + first - low : base + last - low, :] = ref[n, x ^ flip, first:last, :]
                    if first > low:
                        stage[d, base : base + first - low, :] = jnp.zeros((first - low, 128), jnp.float32)
                    if last < low + size:
                        stage[d, base + last - low : base + size, :] = jnp.zeros((low + size - last, 128), jnp.float32)
    for k in range(8):
        outs[k][...] = stage[t ^ k]
    for copy in copies:
        copy.wait()
    for d in range(8):
        @pl.when(t == d)
        def window(d=d):
            low = OWN * d - HALO
            first, last = max(low, 0), min(low + TALL, 96)
            parts = []
            for ref, x in ((kappa, 0), (kappa, 1), (begin, 0), (begin, 1)):
                v = ref[x ^ flip, first:last, :]
                if first > low:
                    v = jnp.concatenate([jnp.zeros((first - low, 128), jnp.float32), v], 0)
                if last < low + TALL:
                    v = jnp.concatenate([v, jnp.zeros((low + TALL - last, 128), jnp.float32)], 0)
                parts.append(v)
            for i, v in enumerate(parts):
                here[i] = v
            for i, q in enumerate((0, 1, 2)):
                near[i] = parts[q]
            for i, q in enumerate((1, 0, 3)):
                far[i] = parts[q]


def coefficient_body(far, near, here, consts, weights, inv):
    t, s = place()
    flip = s & 1
    near, far = ([side[168 + 3 * i : 171 + 3 * i].reshape(TALL, 128) for i in range(3)] for side in (near, far))
    kappa = [near[1], near[0], here[0], here[1], far[0], far[1]]
    for p in range(6):
        plane = jnp.where(flip == 1, 2 * s + 3 - p, 2 * s - 2 + p)
        kappa[p] = kappa[p] * jnp.where((plane >= 0) & (plane < 64), 1.0, 0.0)
    begin = [near[2], here[2], here[3], far[2]]
    lane = lax.broadcasted_iota(jnp.int32, (TALL, 128), 1)
    row = lax.broadcasted_iota(jnp.int32, (TALL, 128), 0) + (OWN * t - HALO)
    half = 0.5 * TAU
    for p in range(1, 5):
        plane = jnp.where(flip == 1, 2 * s + 3 - p, 2 * s - 2 + p)
        ahead = jnp.where(flip == 1, plane - 1, plane + 1)
        behind = jnp.where(flip == 1, plane + 1, plane - 1)
        real = jnp.where((plane >= 0) & (plane < 64), half, 0.0)
        to_ahead = jnp.where((ahead >= 0) & (ahead < 64), real, 0.0)
        to_behind = jnp.where((behind >= 0) & (behind < 64), real, 0.0)
        k = kappa[p]
        row_ok = (row >= 0) & (row < 96)
        xp = k + kappa[p + 1]
        xm = k + kappa[p - 1]
        yp = k + pltpu.roll(k, TALL - 1, 0)
        ym = k + pltpu.roll(k, 1, 0)
        zp = k + jnp.where(lane < 127, pltpu.roll(k, 127, 1), 0.0)
        zm = k + jnp.where(lane > 0, pltpu.roll(k, 1, 1), 0.0)
        kinds = [
            jnp.where(row_ok, xp * to_ahead, 0.0),
            jnp.where(row_ok, xm * to_behind, 0.0),
            jnp.where(row_ok & (row < 95), yp * real, 0.0),
            jnp.where(row_ok & (row > 0), ym * real, 0.0),
            jnp.where(row_ok & (lane < 127), zp * real, 0.0),
            jnp.where(row_ok & (lane > 0), zm * real, 0.0),
            half * (((xp + xm) + (yp + ym)) + (zp + zm)),
            begin[p - 1],
        ]
        for i, v in enumerate(kinds):
            weights[pl.ds((p - 1) * TALL * 8 + i, TALL, stride=8), :] = v
    ca, cb, lag = consts[0], consts[1], consts[2]
    base = lag * lag + DET_SHIFT
    for p, lo, hi in ((2, 1, 19), (3, 1, 19), (1, 2, 18), (4, 2, 18)):
        for j in range(lo, hi):
            td = jnp.broadcast_to(weights[pl.ds(((p - 1) * TALL + j) * 8 + 6, 1), :], (8, 128))
            a = ca + td
            b = cb + td
            at = region(p, j)
            inv[at, 0] = 1.0 / (a * a + base)
            inv[at, 1] = 1.0 / (b * b + base)


def spread_body(*rest):
    pieces, (near_c, far_c, forward), (own, wish, near, far), stage = rest[:8], rest[8:11], rest[11:15], rest[15]
    for i in range(3):
        near[168 + 3 * i : 171 + 3 * i] = near_c[i].reshape(3, 8, 128)
        far[168 + 3 * i : 171 + 3 * i] = far_c[i].reshape(3, 8, 128)
    t, _ = place()
    rows = PIECE
    for k, piece in zip(ORDER + (0,), pieces):
        stage[pl.ds(pl.multiple_of((t ^ k) * rows, 8), rows), :] = piece[...]

    def steps(f, n, x, j):
        return stage[pl.ds(piece_row(f, n, x) + j - (0 if f < 2 else 1), 8, stride=rows), :]

    matrix = forward[...]
    for x in range(2):
        for low in range(0, WIN, 4):
            block = [steps(f, n, x, low + i) for i in range(4) for f in range(2) for n in range(2)]
            done = transform(matrix, jnp.concatenate(block, 0))
            for i in range(4):
                for c in range(4):
                    v = done[(i * 4 + c) * 8 : (i * 4 + c + 1) * 8]
                    own[x, low + i, c] = v
                    put_field(near, far, x, low + i, c, v)
    cells = [(x, j) for x in range(2) for j in range(1, WIN - 1)]
    for low in range(0, len(cells), 8):
        block = jnp.concatenate([steps(2, n, x, j) for x, j in cells[low : low + 8] for n in range(2)], 0)
        done = transform(matrix[: len(block), : len(block)], block)
        for i, (x, j) in enumerate(cells[low : low + 8]):
            for n in range(2):
                v = done[(i * 2 + n) * 8 : (i * 2 + n + 1) * 8]
                wish[x, j - 1, n] = v
                if 2 <= j <= 17:
                    out = far if x == 1 else near
                    out[136 + (j - 2) * 2 + n] = v


def transform(matrix, block):
    return jnp.dot(matrix, block, precision=lax.Precision.HIGHEST, preferred_element_type=jnp.float32)


def put_field(near, far, x, j, c, v):
    first, second = (near, far) if x == 0 else (far, near)
    if 1 <= j <= 18:
        first[(j - 1) * 4 + c] = v
    if 2 <= j <= 17:
        second[72 + (j - 2) * 4 + c] = v


def region(p, j):
    if p == 2 or p == 3:
        return (p - 2) * 18 + j - 1
    return (36 if p == 1 else 52) + j - 2


def spread_sum(v, around, w):
    px, mx, py, my = around
    up = pltpu.roll(v, 127, 1)
    down = pltpu.roll(v, 1, 1)
    return ((w[0] * px + w[1] * mx) + (w[2] * py + w[3] * my)) + (w[4] * up + w[5] * down)


def row_weights(weights, p, j, count):
    tile = weights[(p - 1) * TALL + j]
    return [jnp.broadcast_to(tile[k : k + 1, :], (8, 128)) for k in range(count)]


def solve(right, td, inv, consts):
    ur, ui, pr, pi = right
    shift_a, shift_b, lag = consts
    inv_a, inv_b = inv
    a = shift_a + td
    b = shift_b + td
    return (
        (a * ur + lag * ui - COUPLING * pr) * inv_a,
        (b * ui - lag * ur - COUPLING * pi) * inv_b,
        (TAU * ur + a * pr - lag * pi) * inv_a,
        (TAU * ui + b * pi + lag * pr) * inv_b,
    )


def over_sublanes(v):
    v = v + pltpu.roll(v, 4, 0)
    v = v + pltpu.roll(v, 2, 0)
    return v + pltpu.roll(v, 1, 0)


def own_sum(v, other, py, my, w, p):
    up = pltpu.roll(v, 127, 1)
    down = pltpu.roll(v, 1, 1)
    return ((w[0] if p == 2 else w[1]) * other + (w[2] * py + w[3] * my)) + (w[4] * up + w[5] * down)


def kept_parts(v, wanted, begin, consts):
    phase_a, phase_b, last_a, last_b, first_a, first_b, slot = (consts[i] for i in range(3, 10))
    begin = begin - over_sublanes(last_a * v[0] + last_b * v[1])
    first = over_sublanes(first_a * v[2] + first_b * v[3])
    return begin, slot * begin, -TAU * wanted[0] - phase_a * first, -TAU * wanted[1] - phase_b * first


def prepare_body(own, wish, weights, consts, kept, part):
    for p in (2, 3):
        def row(j, carry, p=p):
            x = p - 2
            w = row_weights(weights, p, j, 8)
            v = [own[x, j, c] for c in range(4)]
            at = region(p, j)
            for c, k in enumerate(kept_parts(v, (wish[x, j - 1, 0], wish[x, j - 1, 1]), w[7], consts)):
                kept[at, c] = k
                part[at, c] = k + own_sum(v[c], own[1 - x, j, c], own[x, j + 1, c], own[x, j - 1, c], w, p)
            return carry
        rows(1, 19, row)


def ahead_body(it, kept, weights, part):
    for p in (2, 3):
        def row(j, carry, p=p):
            x = p - 2
            w = row_weights(weights, p, j, 6)
            for c in range(4):
                around = own_sum(it[x, j - 2, c], it[1 - x, j - 2, c], it[x, j - 1, c], it[x, j - 3, c], w, p)
                part[x * 14 + j - 3, c] = kept[region(p, j), c] + around
            return carry
        rows(3, 17, row)


def front_body(far, near, own, tnear, tfar, weights, consts, inv, kept, part, side, it, out_near, out_far, zed):
    def field(p, j, c):
        if p == 2 or p == 3:
            return own[p - 2, j, c]
        got = near if p < 2 else far
        if p == 1 or p == 4:
            return got[(j - 1) * 4 + c]
        return got[72 + (j - 2) * 4 + c]

    cs = (consts[0], consts[1], consts[2])
    for p in (2, 3):
        def row(j, carry, p=p):
            w = row_weights(weights, p, j, 8)
            at = region(p, j)
            pushed = []
            for c in range(4):
                pushed.append(part[at, c] + (w[1] * field(1, j, c) if p == 2 else w[0] * field(4, j, c)))
            z = solve(pushed, w[6], (inv[at, 0], inv[at, 1]), cs)
            for c in range(4):
                zed[at, c] = z[c]
            return carry
        rows(1, 19, row)
    for p in (1, 4):
        def row(j, carry, p=p):
            w = row_weights(weights, p, j, 8)
            v = [field(p, j, c) for c in range(4)]
            wanted = [(tnear if p == 1 else tfar)[136 + (j - 2) * 2 + n] for n in range(2)]
            at = region(p, j)
            pushed = []
            for c, k in enumerate(kept_parts(v, wanted, w[7], consts)):
                side[at - 36, c] = k
                around = (field(p + 1, j, c), field(p - 1, j, c), field(p, j + 1, c), field(p, j - 1, c))
                pushed.append(k + spread_sum(v[c], around, w))
            z = solve(pushed, w[6], (inv[at, 0], inv[at, 1]), cs)
            for c in range(4):
                zed[at, c] = z[c]
            return carry
        rows(2, 18, row)

    for p in (2, 3):
        def row(j, carry, p=p):
            w = row_weights(weights, p, j, 8)
            at = region(p, j)
            pushed = []
            for c in range(4):
                around = (zed[region(p + 1, j), c], zed[region(p - 1, j), c], zed[at + 1, c], zed[at - 1, c])
                pushed.append(kept[at, c] + spread_sum(zed[at, c], around, w))
            z = solve(pushed, w[6], (inv[at, 0], inv[at, 1]), cs)
            for c in range(4):
                it[p - 2, j - 2, c] = z[c]
            return carry
        rows(2, 18, row)
    out_near[0:14] = it[0, 1:15]
    out_near[14:26] = it[1, 2:14]
    out_far[0:14] = it[1, 1:15]
    out_far[14:26] = it[0, 2:14]


def sweep_body(it, near, far, kept, side, part, weights, consts, inv, zed, put):
    def guess(p, j, c):
        if p == 2 or p == 3:
            return it[p - 2, j - 2, c]
        side = near if p < 2 else far
        if p == 1 or p == 4:
            return side[j - 3, c]
        return side[14 + j - 4, c]

    def at2(p, j):
        if p == 2 or p == 3:
            return (p - 2) * 14 + j - 3
        return (28 if p == 1 else 40) + j - 4

    cs = (consts[0], consts[1], consts[2])
    for p, lo, hi in ((2, 3, 17), (3, 3, 17), (1, 4, 16), (4, 4, 16)):
        def row(j, carry, p=p):
            w = row_weights(weights, p, j, 8)
            at = region(p, j)
            pushed = []
            for c in range(4):
                if p == 2 or p == 3:
                    beside = w[1] * guess(1, j, c) if p == 2 else w[0] * guess(4, j, c)
                    pushed.append(part[at2(p, j), c] + beside)
                    continue
                around = (guess(p + 1, j, c), guess(p - 1, j, c), guess(p, j + 1, c), guess(p, j - 1, c))
                pushed.append(side[at - 36, c] + spread_sum(guess(p, j, c), around, w))
            z = solve(pushed, w[6], (inv[at, 0], inv[at, 1]), cs)
            for c in range(4):
                zed[at2(p, j), c] = z[c]
            return carry
        rows(lo, hi, row)
    for p in (2, 3):
        def row(j, carry, p=p):
            w = row_weights(weights, p, j, 8)
            at = region(p, j)
            here = at2(p, j)
            pushed = []
            for c in range(4):
                around = (zed[at2(p + 1, j), c], zed[at2(p - 1, j), c], zed[here + 1, c], zed[here - 1, c])
                pushed.append(kept[at, c] + spread_sum(zed[here, c], around, w))
            z = solve(pushed, w[6], (inv[at, 0], inv[at, 1]), cs)
            for c in range(4):
                put(p - 2, j - 4, c, z[c])
            return carry
        rows(4, 16, row)


def middle_body(far, near, it, kept, side, part, weights, consts, inv, new, out_near, out_far, send0, send1, zed):
    def put(x, j, c, v):
        new[x, j, c] = v
        first, second = (out_near, out_far) if x == 0 else (out_far, out_near)
        first[j, c] = v
        second[OWN + j, c] = v
    sweep_body(far=far, near=near, it=it, kept=kept, side=side, part=part, weights=weights, consts=consts, inv=inv, zed=zed, put=put)
    odd = place()[0] & 1
    for x in range(2):
        send0[x] = new[x, pl.ds((OWN - HALO) * (1 - odd), HALO)]
        send1[x] = new[x, pl.ds((OWN - HALO) * odd, HALO)]


def edges_body(far, near, row1, row0, new, own, send0, send1):
    odd = place()[0] & 1
    for x in range(2):
        own[x, HALO : HALO + OWN] = new[x]
    for row, send, high in ((row0, send0, 1 - odd), (row1, send1, odd)):
        for x in range(2):
            own[x, pl.ds(16 * high, HALO)] = row[x]
        for i, side in enumerate((near, far)):
            send[3 * i : 3 * i + 3] = side[pl.ds((OWN - 3) * high, 3)]
            send[6 + 2 * i : 8 + 2 * i] = side[pl.ds(OWN + (OWN - 2) * high, 2)]


def widen_body(edge1, edge0, near_x, far_x, near, far):
    odd = place()[0] & 1
    for out, got in ((near, near_x), (far, far_x)):
        out[3 : 3 + OWN] = got[0:OWN]
        out[20 : 20 + OWN] = got[OWN : 2 * OWN]
    for edge, high in ((edge0, 1 - odd), (edge1, odd)):
        for i, side in enumerate((near, far)):
            side[pl.ds(15 * high, 3)] = edge[3 * i : 3 * i + 3]
            side[pl.ds(18 + 14 * high, 2)] = edge[6 + 2 * i : 8 + 2 * i]


def last_body(far, near, it, kept, side, part, weights, consts, inv, back, *rest):
    outs, (zed, fin, stage) = rest[:2], rest[2:]
    def put(x, j, c, v):
        fin[x * OWN + j, c] = v
    sweep_body(far=far, near=near, it=it, kept=kept, side=side, part=part, weights=weights, consts=consts, inv=inv, zed=zed, put=put)
    t, _ = place()
    matrix = back[...]
    for low in range(0, 2 * OWN, 4):
        done = transform(matrix, fin[low : low + 4].reshape(128, 128))
        for i in range(4):
            x, j = divmod(low + i, OWN)
            for c in range(4):
                stage[pl.ds((c * 2 + x) * OWN + j, 8, stride=8 * OWN), :] = done[(i * 4 + c) * 8 : (i * 4 + c + 1) * 8]
    for k in range(8):
        outs[k & 1][k >> 1] = stage[pl.ds(pl.multiple_of((t ^ k) * 8 * OWN, 8), 8 * OWN), :]


def merge_body(other, mine, *outs):
    for out, k in zip(outs, CHIPS):
        out[0] = mine[k]
        out[1] = other[k]


def unpack_body(a, b, c, other, mine, state, adjoint, stage, held, sems):
    t, s = place()
    flip = s & 1
    for ref, k in zip((a, b, c), CHIPS):
        stage[t ^ (2 * k)] = ref[0]
        stage[t ^ (2 * k + 1)] = ref[1]
    stage[t] = mine[0]
    stage[t ^ 1] = other[0]
    copies = []
    for f, ref in enumerate((state, adjoint)):
        for n in range(2):
            for x in range(2):
                base = ((f * 2 + n) * 2 + x) * OWN
                for d in range(8):
                    held[f, n, x, OWN * d : OWN * (d + 1), :] = stage[d, base : base + OWN, :]
                copies.append(
                    pltpu.make_async_copy(held.at[f, n, x], ref.at[n, x ^ flip], sems.at[(f * 2 + n) * 2 + x])
                )
                copies[-1].start()
    for copy in copies:
        copy.wait()


def exchange(pieces):
    count = lax.axis_size("tm")
    return [lax.ppermute(pieces[k], "tm", [(i, i ^ k) for i in range(count)]) for k in ORDER] + [pieces[0]]


def swap_rows(block, start):
    count = lax.axis_size("tm")
    route = []
    for i in range(start, start + count, 2):
        low, high = i % count, (i + 1) % count
        route += [(low, high), (high, low)]
    return lax.ppermute(block, "tm", route)


def swap_planes(block, start):
    sections, slabs = lax.axis_size("tm"), lax.axis_size("space")
    route = []
    for t in range(sections):
        for s in range(slabs):
            pair = s + 1 if (s - start) % 2 == 0 else s - 1
            to = t * slabs + pair if 0 <= pair < slabs else (t ^ 1) * slabs + s
            route.append((t * slabs + s, to))
    return lax.ppermute(block, ("tm", "space"), route)


def on_device(state_guess, adjoint_guess, target, initial_state, diffusivity):
    forward, back = (jnp.asarray(m) for m in transform_matrices())
    consts = jnp.asarray(mode_constants())

    arguments = (state_guess, adjoint_guess, target, diffusivity, initial_state, forward, back, consts)
    *pieces, near_c, far_c, here_c, forward, back, consts = call(
        pack_body,
        "pack",
        [whole(PIECE, 128)] * 8 + [whole(3, TALL, 128)] * 2 + [whole(4, TALL, 128)]
        + [whole(128, 128)] * 2 + [whole(10, 8, 128)],
        0,
        [pltpu.VMEM((8, PIECE, 128), jnp.float32)]
        + [pltpu.VMEM((2, 2, 96, 128), jnp.float32)] * 3
        + [pltpu.VMEM((2, 96, 128), jnp.float32)] * 2
        + [pltpu.SemaphoreType.DMA((11,))],
        far_inputs=8,
    )(*(pltpu.with_memory_space_constraint(a, pltpu.HBM) for a in arguments))
    got = exchange(pieces)
    own, wish, near, far = call(
        spread_body,
        "spread",
        [whole(2, WIN, 4, 8, 128), whole(2, 18, 2, 8, 128), whole(177, 8, 128), whole(177, 8, 128)],
        11,
        [pltpu.VMEM((8 * PIECE, 128), jnp.float32)],
    )(*got, near_c, far_c, forward)
    coefficients = call(
        coefficient_body, "coefficients", [whole(4 * TALL * 8, 128), whole(68, 2, 8, 128)], 4
    )
    slab_weights = coefficients(far, near, here_c, consts)[0].reshape(4 * TALL, 8, 128)
    far = far_first = swap_planes(far, 0)
    near = near_first = swap_planes(near, 1)
    weights, inv = coefficients(far, near, here_c, consts)
    weights = weights.reshape(4 * TALL, 8, 128)

    sweep_scratch = [pltpu.VMEM((52, 4, 8, 128), jnp.float32)]
    for outer in range(OUTER):
        kept, part = call(prepare_body, "prepare", [whole(36, 4, 8, 128)] * 2, 4)(own, wish, slab_weights, consts)
        side, it, near_z, far_z = call(
            front_body,
            "front",
            [whole(32, 4, 8, 128), whole(2, 16, 4, 8, 128), whole(26, 4, 8, 128), whole(26, 4, 8, 128)],
            10,
            [pltpu.VMEM((68, 4, 8, 128), jnp.float32)],
        )(far, near, own, near_first, far_first, weights, consts, inv, kept, part)
        ahead = call(ahead_body, "ahead", [whole(28, 4, 8, 128)], 3)(it, kept, weights)[0]
        far_z = swap_planes(far_z, 0)
        near_z = swap_planes(near_z, 1)
        if outer < OUTER - 1:
            new, near, far, row0, row1 = call(
                middle_body,
                "middle",
                [whole(2, OWN, 4, 8, 128)] + [whole(2 * OWN, 4, 8, 128)] * 2 + [whole(2, HALO, 4, 8, 128)] * 2,
                9,
                sweep_scratch,
            )(far_z, near_z, it, kept, side, ahead, weights, consts, inv)
            far = swap_planes(far, 0)
            near = swap_planes(near, 1)
            row1 = swap_rows(row1, 1)
            row0 = swap_rows(row0, 0)
            own, edge0, edge1 = call(
                edges_body, "edges", [whole(2, WIN, 4, 8, 128)] + [whole(10, 4, 8, 128)] * 2, 5
            )(far, near, row1, row0, new)
            edge1 = swap_rows(edge1, 1)
            edge0 = swap_rows(edge0, 0)
            near, far = call(widen_body, "widen", [whole(34, 4, 8, 128)] * 2, 4)(edge1, edge0, near, far)
            near = near.reshape(136, 8, 128)
            far = far.reshape(136, 8, 128)
    mine, other = call(
        last_body,
        "last",
        [whole(4, 8 * OWN, 128)] * 2,
        10,
        sweep_scratch + [pltpu.VMEM((2 * OWN, 4, 8, 128), jnp.float32), pltpu.VMEM((64 * OWN, 128), jnp.float32)],
    )(far_z, near_z, it, kept, side, ahead, weights, consts, inv, back)
    other = swap_rows(other, 0)
    pairs = call(merge_body, "merge", [whole(2, 8 * OWN, 128)] * 3, 2)(other, mine)
    count = lax.axis_size("tm")
    got = [
        lax.ppermute(pair, "tm", [(i, i ^ (2 * k)) for i in range(count)]) for pair, k in zip(pairs, CHIPS)
    ]
    return tuple(
        call(
            unpack_body,
            "unpack",
            [whole(2, 2, 96, 128)] * 2,
            5,
            [
                pltpu.VMEM((8, 8 * OWN, 128), jnp.float32),
                pltpu.VMEM((2, 2, 2, 96, 128), jnp.float32),
                pltpu.SemaphoreType.DMA((8,)),
            ],
            far_outputs=True,
        )(*got, other, mine)
    )


def solution(mesh):
    in_specs = (
        P("tm", "space", None, None),
        P("tm", "space", None, None),
        P("tm", "space", None, None),
        P("space", None, None),
        P("space", None, None),
    )
    out_specs = (P("tm", "space", None, None), P("tm", "space", None, None))
    return jax.shard_map(
        on_device, mesh=mesh, in_specs=in_specs, out_specs=out_specs, check_vma=False
    )
```

```python
import math

import jax
import jax.numpy as jnp
import numpy as np
from jax import lax
from jax.experimental import pallas as pl
from jax.experimental.pallas import tpu as pltpu
from jax.sharding import PartitionSpec as P

TAU = 0.25
COUPLING = 5.0
DET_SHIFT = 1.25
OUTER = 2

OWN = 12
HALO = 4
WIN = OWN + 2 * HALO
ORDER = (4, 2, 6, 5, 3, 7, 1)
PIECE = 8 * WIN + 4 * (WIN - 2)
CHIPS = (2, 1, 3)
TALL = 24


def place():
    return lax.axis_index("tm"), lax.axis_index("space")


def transform_matrices():
    modes = np.arange(8)[:, None]
    steps = np.concatenate([np.arange(0, 16, 2), np.arange(1, 16, 2)])[None, :]
    angle = 2.0 * np.pi * ((modes * steps) % 16) / 16.0
    real, imag = np.cos(angle), -np.sin(angle)
    imag[0] = np.where(steps[0] % 2 == 0, 1.0, -1.0)
    forward = np.concatenate([real, imag], 0)
    back = forward.T.copy() / 8.0
    back[:, 0] /= 2.0
    back[:, 8] /= 2.0
    eye = np.eye(8)
    return np.kron(eye, forward).astype(np.float32), np.kron(eye, back).astype(np.float32)


def mode_constants():
    theta = 2.0 * np.pi * np.arange(8) / 16.0
    shift_a = 1.0 - np.cos(theta)
    shift_b = shift_a.copy()
    shift_b[0] = 2.0
    lag = np.sin(theta)
    phase_a, phase_b = np.cos(theta), np.sin(theta)
    phase_b[0] = -1.0
    share = np.where(np.arange(8) == 0, 1.0, 2.0) / 16.0
    last_a, last_b = share * np.cos(15.0 * theta), -share * np.sin(15.0 * theta)
    last_b[0] = -1.0 / 16.0
    first_a, first_b = share, np.where(np.arange(8) == 0, 1.0, 0.0) / 16.0
    slot = np.where(np.arange(8) == 0, 1.0, 0.0)
    kinds = [shift_a, shift_b, lag, phase_a, phase_b, last_a, last_b, first_a, first_b, slot]
    return (np.stack(kinds)[:, :, None] * np.ones((1, 1, 128))).astype(np.float32)


def whole(*shape):
    return jax.ShapeDtypeStruct(shape, jnp.float32)


def call(body, name, outs, n_in, scratch=(), far_inputs=0, far_outputs=False):
    vmem = pl.BlockSpec(memory_space=pltpu.VMEM)
    anywhere = pl.BlockSpec(memory_space=pltpu.HBM)
    return pl.pallas_call(
        body,
        name=name,
        out_shape=outs,
        in_specs=[anywhere] * far_inputs + [vmem] * n_in,
        out_specs=[anywhere if far_outputs else vmem] * len(outs),
        scratch_shapes=list(scratch),
        compiler_params=pltpu.CompilerParams(vmem_limit_bytes=16 * 1024 * 1024),
    )


def rows(lo, hi, body):
    lax.fori_loop(lo, hi, body, 0, unroll=True)


def piece_row(f, n, x):
    return ((f * 2 + n) * 2 + x) * WIN if f < 2 else 8 * WIN + (n * 2 + x) * (WIN - 2)


def pack_body(*rest):
    sources, outs, (near, far, here), tables = rest[:8], rest[8:16], rest[16:19], rest[19:22]
    stage, held, sems = rest[22], rest[23:28], rest[28]
    slabs = [
        pltpu.make_async_copy(sources[f].at[n], held[f].at[n], sems.at[2 * f + n]) for f in range(3) for n in range(2)
    ]
    copies = [pltpu.make_async_copy(sources[3 + i], ref, sems.at[6 + i]) for i, ref in enumerate(held[3:] + tables)]
    for copy in slabs + copies:
        copy.start()
    state, adjoint, target, kappa, begin = held
    t, s = place()
    flip = s & 1
    for f, ref in enumerate((state, adjoint, target)):
        for n in range(2):
            slabs[2 * f + n].wait()
            for x in range(2):
                base = piece_row(f, n, x)
                size = WIN if f < 2 else WIN - 2
                for d in range(8):
                    low = OWN * d - (HALO if f < 2 else HALO - 1)
                    first, last = max(low, 0), min(low + size, 96)
                    stage[d, base + first - low : base + last - low, :] = ref[n, x ^ flip, first:last, :]
                    if first > low:
                        stage[d, base : base + first - low, :] = jnp.zeros((first - low, 128), jnp.float32)
                    if last < low + size:
                        stage[d, base + last - low : base + size, :] = jnp.zeros((low + size - last, 128), jnp.float32)
    for k in range(8):
        outs[k][...] = stage[t ^ k]
    for copy in copies:
        copy.wait()
    for d in range(8):
        @pl.when(t == d)
        def window(d=d):
            low = OWN * d - HALO
            first, last = max(low, 0), min(low + TALL, 96)
            parts = []
            for ref, x in ((kappa, 0), (kappa, 1), (begin, 0), (begin, 1)):
                v = ref[x ^ flip, first:last, :]
                if first > low:
                    v = jnp.concatenate([jnp.zeros((first - low, 128), jnp.float32), v], 0)
                if last < low + TALL:
                    v = jnp.concatenate([v, jnp.zeros((low + TALL - last, 128), jnp.float32)], 0)
                parts.append(v)
            for i, v in enumerate(parts):
                here[i] = v
            for i, q in enumerate((0, 1, 2)):
                near[i] = parts[q]
            for i, q in enumerate((1, 0, 3)):
                far[i] = parts[q]


def coefficient_body(far, near, here, consts, weights, inv):
    t, s = place()
    flip = s & 1
    kappa = [near[1], near[0], here[0], here[1], far[0], far[1]]
    for p in range(6):
        plane = jnp.where(flip == 1, 2 * s + 3 - p, 2 * s - 2 + p)
        kappa[p] = kappa[p] * jnp.where((plane >= 0) & (plane < 64), 1.0, 0.0)
    begin = [near[2], here[2], here[3], far[2]]
    lane = lax.broadcasted_iota(jnp.int32, (TALL, 128), 1)
    row = lax.broadcasted_iota(jnp.int32, (TALL, 128), 0) + (OWN * t - HALO)
    half = 0.5 * TAU
    for p in range(1, 5):
        plane = jnp.where(flip == 1, 2 * s + 3 - p, 2 * s - 2 + p)
        ahead = jnp.where(flip == 1, plane - 1, plane + 1)
        behind = jnp.where(flip == 1, plane + 1, plane - 1)
        real = jnp.where((plane >= 0) & (plane < 64), half, 0.0)
        to_ahead = jnp.where((ahead >= 0) & (ahead < 64), real, 0.0)
        to_behind = jnp.where((behind >= 0) & (behind < 64), real, 0.0)
        k = kappa[p]
        row_ok = (row >= 0) & (row < 96)
        xp = k + kappa[p + 1]
        xm = k + kappa[p - 1]
        yp = k + pltpu.roll(k, TALL - 1, 0)
        ym = k + pltpu.roll(k, 1, 0)
        zp = k + jnp.where(lane < 127, pltpu.roll(k, 127, 1), 0.0)
        zm = k + jnp.where(lane > 0, pltpu.roll(k, 1, 1), 0.0)
        kinds = [
            jnp.where(row_ok, xp * to_ahead, 0.0),
            jnp.where(row_ok, xm * to_behind, 0.0),
            jnp.where(row_ok & (row < 95), yp * real, 0.0),
            jnp.where(row_ok & (row > 0), ym * real, 0.0),
            jnp.where(row_ok & (lane < 127), zp * real, 0.0),
            jnp.where(row_ok & (lane > 0), zm * real, 0.0),
            half * (((xp + xm) + (yp + ym)) + (zp + zm)),
            begin[p - 1],
        ]
        for i, v in enumerate(kinds):
            weights[pl.ds((p - 1) * TALL * 8 + i, TALL, stride=8), :] = v
    ca, cb, lag = consts[0], consts[1], consts[2]
    base = lag * lag + DET_SHIFT
    for p, lo, hi in ((2, 1, 19), (3, 1, 19), (1, 2, 18), (4, 2, 18)):
        for j in range(lo, hi):
            td = jnp.broadcast_to(weights[pl.ds(((p - 1) * TALL + j) * 8 + 6, 1), :], (8, 128))
            a = ca + td
            b = cb + td
            at = region(p, j)
            inv[at, 0] = 1.0 / (a * a + base)
            inv[at, 1] = 1.0 / (b * b + base)


def spread_body(*rest):
    pieces, forward, (own, wish, near, far), stage = rest[:8], rest[10], rest[11:15], rest[15]
    t, _ = place()
    rows = PIECE
    for k, piece in zip(ORDER + (0,), pieces):
        stage[pl.ds(pl.multiple_of((t ^ k) * rows, 8), rows), :] = piece[...]

    def steps(f, n, x, j):
        return stage[pl.ds(piece_row(f, n, x) + j - (0 if f < 2 else 1), 8, stride=rows), :]

    matrix = forward[...]
    for x in range(2):
        for low in range(0, WIN, 4):
            block = [steps(f, n, x, low + i) for i in range(4) for f in range(2) for n in range(2)]
            done = transform(matrix, jnp.concatenate(block, 0))
            for i in range(4):
                for c in range(4):
                    v = done[(i * 4 + c) * 8 : (i * 4 + c + 1) * 8]
                    own[x, low + i, c] = v
                    put_field(near, far, x, low + i, c, v)
    cells = [(x, j) for x in range(2) for j in range(1, WIN - 1)]
    for low in range(0, len(cells), 8):
        block = jnp.concatenate([steps(2, n, x, j) for x, j in cells[low : low + 8] for n in range(2)], 0)
        done = transform(matrix[: len(block), : len(block)], block)
        for i, (x, j) in enumerate(cells[low : low + 8]):
            for n in range(2):
                v = done[(i * 2 + n) * 8 : (i * 2 + n + 1) * 8]
                wish[x, j - 1, n] = v
                if 2 <= j <= 17:
                    out = far if x == 1 else near
                    out[136 + (j - 2) * 2 + n] = v


def transform(matrix, block):
    return jnp.dot(matrix, block, precision=lax.Precision.HIGHEST, preferred_element_type=jnp.float32)


def put_field(near, far, x, j, c, v):
    first, second = (near, far) if x == 0 else (far, near)
    if 1 <= j <= 18:
        first[(j - 1) * 4 + c] = v
    if 2 <= j <= 17:
        second[72 + (j - 2) * 4 + c] = v


def region(p, j):
    if p == 2 or p == 3:
        return (p - 2) * 18 + j - 1
    return (36 if p == 1 else 52) + j - 2


def spread_sum(v, around, w):
    px, mx, py, my = around
    up = pltpu.roll(v, 127, 1)
    down = pltpu.roll(v, 1, 1)
    return ((w[0] * px + w[1] * mx) + (w[2] * py + w[3] * my)) + (w[4] * up + w[5] * down)


def row_weights(weights, p, j, count):
    tile = weights[(p - 1) * TALL + j]
    return [jnp.broadcast_to(tile[k : k + 1, :], (8, 128)) for k in range(count)]


def solve(right, td, inv, consts):
    ur, ui, pr, pi = right
    shift_a, shift_b, lag = consts
    inv_a, inv_b = inv
    a = shift_a + td
    b = shift_b + td
    return (
        (a * ur + lag * ui - COUPLING * pr) * inv_a,
        (b * ui - lag * ur - COUPLING * pi) * inv_b,
        (TAU * ur + a * pr - lag * pi) * inv_a,
        (TAU * ui + b * pi + lag * pr) * inv_b,
    )


def over_sublanes(v):
    v = v + pltpu.roll(v, 4, 0)
    v = v + pltpu.roll(v, 2, 0)
    return v + pltpu.roll(v, 1, 0)


def own_sum(v, other, py, my, w, p):
    up = pltpu.roll(v, 127, 1)
    down = pltpu.roll(v, 1, 1)
    return ((w[0] if p == 2 else w[1]) * other + (w[2] * py + w[3] * my)) + (w[4] * up + w[5] * down)


def kept_parts(v, wanted, begin, consts):
    phase_a, phase_b, last_a, last_b, first_a, first_b, slot = (consts[i] for i in range(3, 10))
    begin = begin - over_sublanes(last_a * v[0] + last_b * v[1])
    first = over_sublanes(first_a * v[2] + first_b * v[3])
    return begin, slot * begin, -TAU * wanted[0] - phase_a * first, -TAU * wanted[1] - phase_b * first


def prepare_body(own, wish, weights, consts, kept, part):
    for p in (2, 3):
        def row(j, carry, p=p):
            x = p - 2
            w = row_weights(weights, p, j, 8)
            v = [own[x, j, c] for c in range(4)]
            at = region(p, j)
            for c, k in enumerate(kept_parts(v, (wish[x, j - 1, 0], wish[x, j - 1, 1]), w[7], consts)):
                kept[at, c] = k
                part[at, c] = k + own_sum(v[c], own[1 - x, j, c], own[x, j + 1, c], own[x, j - 1, c], w, p)
            return carry
        rows(1, 19, row)


def ahead_body(it, kept, weights, part):
    for p in (2, 3):
        def row(j, carry, p=p):
            x = p - 2
            w = row_weights(weights, p, j, 6)
            for c in range(4):
                around = own_sum(it[x, j - 2, c], it[1 - x, j - 2, c], it[x, j - 1, c], it[x, j - 3, c], w, p)
                part[x * 14 + j - 3, c] = kept[region(p, j), c] + around
            return carry
        rows(3, 17, row)


def front_body(far, near, own, tnear, tfar, weights, consts, inv, kept, part, side, it, out_near, out_far, zed):
    def field(p, j, c):
        if p == 2 or p == 3:
            return own[p - 2, j, c]
        got = near if p < 2 else far
        if p == 1 or p == 4:
            return got[(j - 1) * 4 + c]
        return got[72 + (j - 2) * 4 + c]

    cs = (consts[0], consts[1], consts[2])
    for p in (2, 3):
        def row(j, carry, p=p):
            w = row_weights(weights, p, j, 8)
            at = region(p, j)
            pushed = []
            for c in range(4):
                pushed.append(part[at, c] + (w[1] * field(1, j, c) if p == 2 else w[0] * field(4, j, c)))
            z = solve(pushed, w[6], (inv[at, 0], inv[at, 1]), cs)
            for c in range(4):
                zed[at, c] = z[c]
            return carry
        rows(1, 19, row)
    for p in (1, 4):
        def row(j, carry, p=p):
            w = row_weights(weights, p, j, 8)
            v = [field(p, j, c) for c in range(4)]
            wanted = [(tnear if p == 1 else tfar)[136 + (j - 2) * 2 + n] for n in range(2)]
            at = region(p, j)
            pushed = []
            for c, k in enumerate(kept_parts(v, wanted, w[7], consts)):
                side[at - 36, c] = k
                around = (field(p + 1, j, c), field(p - 1, j, c), field(p, j + 1, c), field(p, j - 1, c))
                pushed.append(k + spread_sum(v[c], around, w))
            z = solve(pushed, w[6], (inv[at, 0], inv[at, 1]), cs)
            for c in range(4):
                zed[at, c] = z[c]
            return carry
        rows(2, 18, row)

    for p in (2, 3):
        def row(j, carry, p=p):
            w = row_weights(weights, p, j, 8)
            at = region(p, j)
            pushed = []
            for c in range(4):
                around = (zed[region(p + 1, j), c], zed[region(p - 1, j), c], zed[at + 1, c], zed[at - 1, c])
                pushed.append(kept[at, c] + spread_sum(zed[at, c], around, w))
            z = solve(pushed, w[6], (inv[at, 0], inv[at, 1]), cs)
            for c in range(4):
                it[p - 2, j - 2, c] = z[c]
            return carry
        rows(2, 18, row)
    out_near[0:14] = it[0, 1:15]
    out_near[14:26] = it[1, 2:14]
    out_far[0:14] = it[1, 1:15]
    out_far[14:26] = it[0, 2:14]


def sweep_body(it, near, far, kept, side, part, weights, consts, inv, zed, put):
    def guess(p, j, c):
        if p == 2 or p == 3:
            return it[p - 2, j - 2, c]
        side = near if p < 2 else far
        if p == 1 or p == 4:
            return side[j - 3, c]
        return side[14 + j - 4, c]

    def at2(p, j):
        if p == 2 or p == 3:
            return (p - 2) * 14 + j - 3
        return (28 if p == 1 else 40) + j - 4

    cs = (consts[0], consts[1], consts[2])
    for p, lo, hi in ((2, 3, 17), (3, 3, 17), (1, 4, 16), (4, 4, 16)):
        def row(j, carry, p=p):
            w = row_weights(weights, p, j, 8)
            at = region(p, j)
            pushed = []
            for c in range(4):
                if p == 2 or p == 3:
                    beside = w[1] * guess(1, j, c) if p == 2 else w[0] * guess(4, j, c)
                    pushed.append(part[at2(p, j), c] + beside)
                    continue
                around = (guess(p + 1, j, c), guess(p - 1, j, c), guess(p, j + 1, c), guess(p, j - 1, c))
                pushed.append(side[at - 36, c] + spread_sum(guess(p, j, c), around, w))
            z = solve(pushed, w[6], (inv[at, 0], inv[at, 1]), cs)
            for c in range(4):
                zed[at2(p, j), c] = z[c]
            return carry
        rows(lo, hi, row)
    for p in (2, 3):
        def row(j, carry, p=p):
            w = row_weights(weights, p, j, 8)
            at = region(p, j)
            here = at2(p, j)
            pushed = []
            for c in range(4):
                around = (zed[at2(p + 1, j), c], zed[at2(p - 1, j), c], zed[here + 1, c], zed[here - 1, c])
                pushed.append(kept[at, c] + spread_sum(zed[here, c], around, w))
            z = solve(pushed, w[6], (inv[at, 0], inv[at, 1]), cs)
            for c in range(4):
                put(p - 2, j - 4, c, z[c])
            return carry
        rows(4, 16, row)


def middle_body(far, near, it, kept, side, part, weights, consts, inv, new, out_near, out_far, send0, send1, zed):
    def put(x, j, c, v):
        new[x, j, c] = v
        first, second = (out_near, out_far) if x == 0 else (out_far, out_near)
        first[j, c] = v
        second[OWN + j, c] = v
    sweep_body(far=far, near=near, it=it, kept=kept, side=side, part=part, weights=weights, consts=consts, inv=inv, zed=zed, put=put)
    odd = place()[0] & 1
    for x in range(2):
        send0[x] = new[x, pl.ds((OWN - HALO) * (1 - odd), HALO)]
        send1[x] = new[x, pl.ds((OWN - HALO) * odd, HALO)]


def edges_body(far, near, row1, row0, new, own, send0, send1):
    odd = place()[0] & 1
    for x in range(2):
        own[x, HALO : HALO + OWN] = new[x]
    for row, send, high in ((row0, send0, 1 - odd), (row1, send1, odd)):
        for x in range(2):
            own[x, pl.ds(16 * high, HALO)] = row[x]
        for i, side in enumerate((near, far)):
            send[3 * i : 3 * i + 3] = side[pl.ds((OWN - 3) * high, 3)]
            send[6 + 2 * i : 8 + 2 * i] = side[pl.ds(OWN + (OWN - 2) * high, 2)]


def widen_body(edge1, edge0, near_x, far_x, near, far):
    odd = place()[0] & 1
    for out, got in ((near, near_x), (far, far_x)):
        out[3 : 3 + OWN] = got[0:OWN]
        out[20 : 20 + OWN] = got[OWN : 2 * OWN]
    for edge, high in ((edge0, 1 - odd), (edge1, odd)):
        for i, side in enumerate((near, far)):
            side[pl.ds(15 * high, 3)] = edge[3 * i : 3 * i + 3]
            side[pl.ds(18 + 14 * high, 2)] = edge[6 + 2 * i : 8 + 2 * i]


def last_body(far, near, it, kept, side, part, weights, consts, inv, back, *rest):
    outs, (zed, fin, stage) = rest[:2], rest[2:]
    def put(x, j, c, v):
        fin[x * OWN + j, c] = v
    sweep_body(far=far, near=near, it=it, kept=kept, side=side, part=part, weights=weights, consts=consts, inv=inv, zed=zed, put=put)
    t, _ = place()
    matrix = back[...]
    for low in range(0, 2 * OWN, 4):
        done = transform(matrix, fin[low : low + 4].reshape(128, 128))
        for i in range(4):
            x, j = divmod(low + i, OWN)
            for c in range(4):
                stage[pl.ds((c * 2 + x) * OWN + j, 8, stride=8 * OWN), :] = done[(i * 4 + c) * 8 : (i * 4 + c + 1) * 8]
    for k in range(8):
        outs[k & 1][k >> 1] = stage[pl.ds(pl.multiple_of((t ^ k) * 8 * OWN, 8), 8 * OWN), :]


def merge_body(other, mine, *outs):
    for out, k in zip(outs, CHIPS):
        out[0] = mine[k]
        out[1] = other[k]


def unpack_body(a, b, c, other, mine, state, adjoint, stage, held, sems):
    t, s = place()
    flip = s & 1
    for ref, k in zip((a, b, c), CHIPS):
        stage[t ^ (2 * k)] = ref[0]
        stage[t ^ (2 * k + 1)] = ref[1]
    stage[t] = mine[0]
    stage[t ^ 1] = other[0]
    copies = []
    for f, ref in enumerate((state, adjoint)):
        for n in range(2):
            for x in range(2):
                base = ((f * 2 + n) * 2 + x) * OWN
                for d in range(8):
                    held[f, n, x, OWN * d : OWN * (d + 1), :] = stage[d, base : base + OWN, :]
                copies.append(
                    pltpu.make_async_copy(held.at[f, n, x], ref.at[n, x ^ flip], sems.at[(f * 2 + n) * 2 + x])
                )
                copies[-1].start()
    for copy in copies:
        copy.wait()


def exchange(pieces):
    count = lax.axis_size("tm")
    return [lax.ppermute(pieces[k], "tm", [(i, i ^ k) for i in range(count)]) for k in ORDER] + [pieces[0]]


def swap_rows(block, start):
    count = lax.axis_size("tm")
    route = []
    for i in range(start, start + count, 2):
        low, high = i % count, (i + 1) % count
        route += [(low, high), (high, low)]
    return lax.ppermute(block, "tm", route)


def swap_planes(block, start):
    sections, slabs = lax.axis_size("tm"), lax.axis_size("space")
    route = []
    for t in range(sections):
        for s in range(slabs):
            pair = s + 1 if (s - start) % 2 == 0 else s - 1
            to = t * slabs + pair if 0 <= pair < slabs else (t ^ 1) * slabs + s
            route.append((t * slabs + s, to))
    return lax.ppermute(block, ("tm", "space"), route)


def on_device(state_guess, adjoint_guess, target, initial_state, diffusivity):
    forward, back = (jnp.asarray(m) for m in transform_matrices())
    consts = jnp.asarray(mode_constants())

    arguments = (state_guess, adjoint_guess, target, diffusivity, initial_state, forward, back, consts)
    *pieces, near_c, far_c, here_c, forward, back, consts = call(
        pack_body,
        "pack",
        [whole(PIECE, 128)] * 8 + [whole(3, TALL, 128)] * 2 + [whole(4, TALL, 128)]
        + [whole(128, 128)] * 2 + [whole(10, 8, 128)],
        0,
        [pltpu.VMEM((8, PIECE, 128), jnp.float32)]
        + [pltpu.VMEM((2, 2, 96, 128), jnp.float32)] * 3
        + [pltpu.VMEM((2, 96, 128), jnp.float32)] * 2
        + [pltpu.SemaphoreType.DMA((11,))],
        far_inputs=8,
    )(*(pltpu.with_memory_space_constraint(a, pltpu.HBM) for a in arguments))
    got = exchange(pieces)
    got[1], far_c, near_c = lax.optimization_barrier((got[1], far_c, near_c))
    far_c = swap_planes(far_c, 0)
    near_c = swap_planes(near_c, 1)
    own, wish, near, far = call(
        spread_body,
        "spread",
        [whole(2, WIN, 4, 8, 128), whole(2, 18, 2, 8, 128), whole(168, 8, 128), whole(168, 8, 128)],
        11,
        [pltpu.VMEM((8 * PIECE, 128), jnp.float32)],
    )(*got, far_c, near_c, forward)
    far = far_first = swap_planes(far, 0)
    near = near_first = swap_planes(near, 1)
    weights, inv = call(
        coefficient_body, "coefficients", [whole(4 * TALL * 8, 128), whole(68, 2, 8, 128)], 4
    )(far_c, near_c, here_c, consts)
    weights = weights.reshape(4 * TALL, 8, 128)

    sweep_scratch = [pltpu.VMEM((52, 4, 8, 128), jnp.float32)]
    for outer in range(OUTER):
        kept, part = call(prepare_body, "prepare", [whole(36, 4, 8, 128)] * 2, 4)(own, wish, weights, consts)
        side, it, near_z, far_z = call(
            front_body,
            "front",
            [whole(32, 4, 8, 128), whole(2, 16, 4, 8, 128), whole(26, 4, 8, 128), whole(26, 4, 8, 128)],
            10,
            [pltpu.VMEM((68, 4, 8, 128), jnp.float32)],
        )(far, near, own, near_first, far_first, weights, consts, inv, kept, part)
        ahead = call(ahead_body, "ahead", [whole(28, 4, 8, 128)], 3)(it, kept, weights)[0]
        far_z = swap_planes(far_z, 0)
        near_z = swap_planes(near_z, 1)
        if outer < OUTER - 1:
            new, near, far, row0, row1 = call(
                middle_body,
                "middle",
                [whole(2, OWN, 4, 8, 128)] + [whole(2 * OWN, 4, 8, 128)] * 2 + [whole(2, HALO, 4, 8, 128)] * 2,
                9,
                sweep_scratch,
            )(far_z, near_z, it, kept, side, ahead, weights, consts, inv)
            far = swap_planes(far, 0)
            near = swap_planes(near, 1)
            row1 = swap_rows(row1, 1)
            row0 = swap_rows(row0, 0)
            own, edge0, edge1 = call(
                edges_body, "edges", [whole(2, WIN, 4, 8, 128)] + [whole(10, 4, 8, 128)] * 2, 5
            )(far, near, row1, row0, new)
            edge1 = swap_rows(edge1, 1)
            edge0 = swap_rows(edge0, 0)
            near, far = call(widen_body, "widen", [whole(34, 4, 8, 128)] * 2, 4)(edge1, edge0, near, far)
            near = near.reshape(136, 8, 128)
            far = far.reshape(136, 8, 128)
    mine, other = call(
        last_body,
        "last",
        [whole(4, 8 * OWN, 128)] * 2,
        10,
        sweep_scratch + [pltpu.VMEM((2 * OWN, 4, 8, 128), jnp.float32), pltpu.VMEM((64 * OWN, 128), jnp.float32)],
    )(far_z, near_z, it, kept, side, ahead, weights, consts, inv, back)
    other = swap_rows(other, 0)
    pairs = call(merge_body, "merge", [whole(2, 8 * OWN, 128)] * 3, 2)(other, mine)
    count = lax.axis_size("tm")
    got = [
        lax.ppermute(pair, "tm", [(i, i ^ (2 * k)) for i in range(count)]) for pair, k in zip(pairs, CHIPS)
    ]
    return tuple(
        call(
            unpack_body,
            "unpack",
            [whole(2, 2, 96, 128)] * 2,
            5,
            [
                pltpu.VMEM((8, 8 * OWN, 128), jnp.float32),
                pltpu.VMEM((2, 2, 2, 96, 128), jnp.float32),
                pltpu.SemaphoreType.DMA((8,)),
            ],
            far_outputs=True,
        )(*got, other, mine)
    )


def solution(mesh):
    in_specs = (
        P("tm", "space", None, None),
        P("tm", "space", None, None),
        P("tm", "space", None, None),
        P("space", None, None),
        P("space", None, None),
    )
    out_specs = (P("tm", "space", None, None), P("tm", "space", None, None))
    return jax.shard_map(
        on_device, mesh=mesh, in_specs=in_specs, out_specs=out_specs, check_vma=False
    )
```

```python
import math

import jax
import jax.numpy as jnp
import numpy as np
from jax import lax
from jax.experimental import pallas as pl
from jax.experimental.pallas import tpu as pltpu
from jax.sharding import PartitionSpec as P

TAU = 0.25
COUPLING = 5.0
DET_SHIFT = 1.25
OUTER = 2

OWN = 12
HALO = 4
WIN = OWN + 2 * HALO
ORDER = (4, 2, 6, 5, 3, 7, 1)
PIECE = 8 * WIN + 4 * (WIN - 2)
CHIPS = (2, 1, 3)
TALL = 24


def place():
    return lax.axis_index("tm"), lax.axis_index("space")


def transform_matrices():
    modes = np.arange(8)[:, None]
    steps = np.concatenate([np.arange(0, 16, 2), np.arange(1, 16, 2)])[None, :]
    angle = 2.0 * np.pi * ((modes * steps) % 16) / 16.0
    real, imag = np.cos(angle), -np.sin(angle)
    imag[0] = np.where(steps[0] % 2 == 0, 1.0, -1.0)
    forward = np.concatenate([real, imag], 0)
    back = forward.T.copy() / 8.0
    back[:, 0] /= 2.0
    back[:, 8] /= 2.0
    eye = np.eye(8)
    return np.kron(eye, forward).astype(np.float32), np.kron(eye, back).astype(np.float32)


def mode_constants():
    theta = 2.0 * np.pi * np.arange(8) / 16.0
    shift_a = 1.0 - np.cos(theta)
    shift_b = shift_a.copy()
    shift_b[0] = 2.0
    lag = np.sin(theta)
    phase_a, phase_b = np.cos(theta), np.sin(theta)
    phase_b[0] = -1.0
    share = np.where(np.arange(8) == 0, 1.0, 2.0) / 16.0
    last_a, last_b = share * np.cos(15.0 * theta), -share * np.sin(15.0 * theta)
    last_b[0] = -1.0 / 16.0
    first_a, first_b = share, np.where(np.arange(8) == 0, 1.0, 0.0) / 16.0
    slot = np.where(np.arange(8) == 0, 1.0, 0.0)
    kinds = [shift_a, shift_b, lag, phase_a, phase_b, last_a, last_b, first_a, first_b, slot]
    return (np.stack(kinds)[:, :, None] * np.ones((1, 1, 128))).astype(np.float32)


def whole(*shape):
    return jax.ShapeDtypeStruct(shape, jnp.float32)


def call(body, name, outs, n_in, scratch=(), far_inputs=0, far_outputs=False):
    vmem = pl.BlockSpec(memory_space=pltpu.VMEM)
    anywhere = pl.BlockSpec(memory_space=pltpu.HBM)
    return pl.pallas_call(
        body,
        name=name,
        out_shape=outs,
        in_specs=[anywhere] * far_inputs + [vmem] * n_in,
        out_specs=[anywhere if far_outputs else vmem] * len(outs),
        scratch_shapes=list(scratch),
        compiler_params=pltpu.CompilerParams(vmem_limit_bytes=16 * 1024 * 1024),
    )


def rows(lo, hi, body):
    lax.fori_loop(lo, hi, body, 0, unroll=True)


def piece_row(f, n, x):
    return ((f * 2 + n) * 2 + x) * WIN if f < 2 else 8 * WIN + (n * 2 + x) * (WIN - 2)


def pack_body(*rest):
    sources, outs, (near, far, here), tables = rest[:8], rest[8:16], rest[16:19], rest[19:22]
    stage, held, sems = rest[22], rest[23:28], rest[28]
    slabs = [
        pltpu.make_async_copy(sources[f].at[n], held[f].at[n], sems.at[2 * f + n]) for f in range(3) for n in range(2)
    ]
    copies = [pltpu.make_async_copy(sources[3 + i], ref, sems.at[6 + i]) for i, ref in enumerate(held[3:] + tables)]
    for copy in slabs + copies:
        copy.start()
    state, adjoint, target, kappa, begin = held
    t, s = place()
    flip = s & 1
    for f, ref in enumerate((state, adjoint, target)):
        for n in range(2):
            slabs[2 * f + n].wait()
            for x in range(2):
                base = piece_row(f, n, x)
                size = WIN if f < 2 else WIN - 2
                for d in range(8):
                    low = OWN * d - (HALO if f < 2 else HALO - 1)
                    first, last = max(low, 0), min(low + size, 96)
                    stage[d, base + first - low : base + last - low, :] = ref[n, x ^ flip, first:last, :]
                    if first > low:
                        stage[d, base : base + first - low, :] = jnp.zeros((first - low, 128), jnp.float32)
                    if last < low + size:
                        stage[d, base + last - low : base + size, :] = jnp.zeros((low + size - last, 128), jnp.float32)
    for k in range(8):
        outs[k][...] = stage[t ^ k]
    for copy in copies:
        copy.wait()
    for d in range(8):
        @pl.when(t == d)
        def window(d=d):
            low = OWN * d - HALO
            first, last = max(low, 0), min(low + TALL, 96)
            parts = []
            for ref, x in ((kappa, 0), (kappa, 1), (begin, 0), (begin, 1)):
                v = ref[x ^ flip, first:last, :]
                if first > low:
                    v = jnp.concatenate([jnp.zeros((first - low, 128), jnp.float32), v], 0)
                if last < low + TALL:
                    v = jnp.concatenate([v, jnp.zeros((low + TALL - last, 128), jnp.float32)], 0)
                parts.append(v)
            for i, v in enumerate(parts):
                here[i] = v
            for i, q in enumerate((0, 1, 2)):
                near[i] = parts[q]
            for i, q in enumerate((1, 0, 3)):
                far[i] = parts[q]


def coefficient_body(far, near, here, consts, weights, inv):
    t, s = place()
    flip = s & 1
    near, far = ([side[168 + 3 * i : 171 + 3 * i].reshape(TALL, 128) for i in range(3)] for side in (near, far))
    kappa = [near[1], near[0], here[0], here[1], far[0], far[1]]
    for p in range(6):
        plane = jnp.where(flip == 1, 2 * s + 3 - p, 2 * s - 2 + p)
        kappa[p] = kappa[p] * jnp.where((plane >= 0) & (plane < 64), 1.0, 0.0)
    begin = [near[2], here[2], here[3], far[2]]
    lane = lax.broadcasted_iota(jnp.int32, (TALL, 128), 1)
    row = lax.broadcasted_iota(jnp.int32, (TALL, 128), 0) + (OWN * t - HALO)
    half = 0.5 * TAU
    for p in range(1, 5):
        plane = jnp.where(flip == 1, 2 * s + 3 - p, 2 * s - 2 + p)
        ahead = jnp.where(flip == 1, plane - 1, plane + 1)
        behind = jnp.where(flip == 1, plane + 1, plane - 1)
        real = jnp.where((plane >= 0) & (plane < 64), half, 0.0)
        to_ahead = jnp.where((ahead >= 0) & (ahead < 64), real, 0.0)
        to_behind = jnp.where((behind >= 0) & (behind < 64), real, 0.0)
        k = kappa[p]
        row_ok = (row >= 0) & (row < 96)
        xp = k + kappa[p + 1]
        xm = k + kappa[p - 1]
        yp = k + pltpu.roll(k, TALL - 1, 0)
        ym = k + pltpu.roll(k, 1, 0)
        zp = k + jnp.where(lane < 127, pltpu.roll(k, 127, 1), 0.0)
        zm = k + jnp.where(lane > 0, pltpu.roll(k, 1, 1), 0.0)
        kinds = [
            jnp.where(row_ok, xp * to_ahead, 0.0),
            jnp.where(row_ok, xm * to_behind, 0.0),
            jnp.where(row_ok & (row < 95), yp * real, 0.0),
            jnp.where(row_ok & (row > 0), ym * real, 0.0),
            jnp.where(row_ok & (lane < 127), zp * real, 0.0),
            jnp.where(row_ok & (lane > 0), zm * real, 0.0),
            half * (((xp + xm) + (yp + ym)) + (zp + zm)),
            begin[p - 1],
        ]
        for i, v in enumerate(kinds):
            weights[pl.ds((p - 1) * TALL * 8 + i, TALL, stride=8), :] = v
    ca, cb, lag = consts[0], consts[1], consts[2]
    base = lag * lag + DET_SHIFT
    for p, lo, hi in ((2, 1, 19), (3, 1, 19), (1, 2, 18), (4, 2, 18)):
        for j in range(lo, hi):
            td = jnp.broadcast_to(weights[pl.ds(((p - 1) * TALL + j) * 8 + 6, 1), :], (8, 128))
            a = ca + td
            b = cb + td
            at = region(p, j)
            inv[at, 0] = 1.0 / (a * a + base)
            inv[at, 1] = 1.0 / (b * b + base)


def spread_body(*rest):
    pieces, (near_c, far_c, forward), (own, wish, near, far), stage = rest[:8], rest[8:11], rest[11:15], rest[15]
    for i in range(3):
        near[168 + 3 * i : 171 + 3 * i] = near_c[i].reshape(3, 8, 128)
        far[168 + 3 * i : 171 + 3 * i] = far_c[i].reshape(3, 8, 128)
    t, _ = place()
    rows = PIECE
    for k, piece in zip(ORDER + (0,), pieces):
        stage[pl.ds(pl.multiple_of((t ^ k) * rows, 8), rows), :] = piece[...]

    def steps(f, n, x, j):
        return stage[pl.ds(piece_row(f, n, x) + j - (0 if f < 2 else 1), 8, stride=rows), :]

    matrix = forward[...]
    for x in range(2):
        for low in range(0, WIN, 4):
            block = [steps(f, n, x, low + i) for i in range(4) for f in range(2) for n in range(2)]
            done = transform(matrix, jnp.concatenate(block, 0))
            for i in range(4):
                for c in range(4):
                    v = done[(i * 4 + c) * 8 : (i * 4 + c + 1) * 8]
                    own[x, low + i, c] = v
                    put_field(near, far, x, low + i, c, v)
    cells = [(x, j) for x in range(2) for j in range(1, WIN - 1)]
    for low in range(0, len(cells), 8):
        block = jnp.concatenate([steps(2, n, x, j) for x, j in cells[low : low + 8] for n in range(2)], 0)
        done = transform(matrix[: len(block), : len(block)], block)
        for i, (x, j) in enumerate(cells[low : low + 8]):
            for n in range(2):
                v = done[(i * 2 + n) * 8 : (i * 2 + n + 1) * 8]
                wish[x, j - 1, n] = v
                if 2 <= j <= 17:
                    out = far if x == 1 else near
                    out[136 + (j - 2) * 2 + n] = v


def halves(v):
    high = v.astype(jnp.bfloat16)
    return high, (v - high.astype(jnp.float32)).astype(jnp.bfloat16)


def transform(matrix, block):
    (mh, ml), (bh, bl) = halves(matrix), halves(block)
    dot = lambda p, q: jnp.dot(p, q, preferred_element_type=jnp.float32)
    return dot(mh, bh) + (dot(mh, bl) + dot(ml, bh))


def put_field(near, far, x, j, c, v):
    first, second = (near, far) if x == 0 else (far, near)
    if 1 <= j <= 18:
        first[(j - 1) * 4 + c] = v
    if 2 <= j <= 17:
        second[72 + (j - 2) * 4 + c] = v


def region(p, j):
    if p == 2 or p == 3:
        return (p - 2) * 18 + j - 1
    return (36 if p == 1 else 52) + j - 2


def spread_sum(v, around, w):
    px, mx, py, my = around
    up = pltpu.roll(v, 127, 1)
    down = pltpu.roll(v, 1, 1)
    return ((w[0] * px + w[1] * mx) + (w[2] * py + w[3] * my)) + (w[4] * up + w[5] * down)


def row_weights(weights, p, j, count):
    tile = weights[(p - 1) * TALL + j]
    return [jnp.broadcast_to(tile[k : k + 1, :], (8, 128)) for k in range(count)]


def solve(right, td, inv, consts):
    ur, ui, pr, pi = right
    shift_a, shift_b, lag = consts
    inv_a, inv_b = inv
    a = shift_a + td
    b = shift_b + td
    return (
        (a * ur + lag * ui - COUPLING * pr) * inv_a,
        (b * ui - lag * ur - COUPLING * pi) * inv_b,
        (TAU * ur + a * pr - lag * pi) * inv_a,
        (TAU * ui + b * pi + lag * pr) * inv_b,
    )


def over_sublanes(v):
    v = v + pltpu.roll(v, 4, 0)
    v = v + pltpu.roll(v, 2, 0)
    return v + pltpu.roll(v, 1, 0)


def own_sum(v, other, py, my, w, p):
    up = pltpu.roll(v, 127, 1)
    down = pltpu.roll(v, 1, 1)
    return ((w[0] if p == 2 else w[1]) * other + (w[2] * py + w[3] * my)) + (w[4] * up + w[5] * down)


def kept_parts(v, wanted, begin, consts):
    phase_a, phase_b, last_a, last_b, first_a, first_b, slot = (consts[i] for i in range(3, 10))
    begin = begin - over_sublanes(last_a * v[0] + last_b * v[1])
    first = over_sublanes(first_a * v[2] + first_b * v[3])
    return begin, slot * begin, -TAU * wanted[0] - phase_a * first, -TAU * wanted[1] - phase_b * first


def prepare_body(own, wish, weights, consts, kept, part):
    for p in (2, 3):
        def row(j, carry, p=p):
            x = p - 2
            w = row_weights(weights, p, j, 8)
            v = [own[x, j, c] for c in range(4)]
            at = region(p, j)
            for c, k in enumerate(kept_parts(v, (wish[x, j - 1, 0], wish[x, j - 1, 1]), w[7], consts)):
                kept[at, c] = k
                part[at, c] = k + own_sum(v[c], own[1 - x, j, c], own[x, j + 1, c], own[x, j - 1, c], w, p)
            return carry
        rows(1, 19, row)


def ahead_body(it, kept, weights, part):
    for p in (2, 3):
        def row(j, carry, p=p):
            x = p - 2
            w = row_weights(weights, p, j, 6)
            for c in range(4):
                around = own_sum(it[x, j - 2, c], it[1 - x, j - 2, c], it[x, j - 1, c], it[x, j - 3, c], w, p)
                part[x * 14 + j - 3, c] = kept[region(p, j), c] + around
            return carry
        rows(3, 17, row)


def front_body(far, near, own, tnear, tfar, weights, consts, inv, kept, part, side, it, out_near, out_far, zed):
    def field(p, j, c):
        if p == 2 or p == 3:
            return own[p - 2, j, c]
        got = near if p < 2 else far
        if p == 1 or p == 4:
            return got[(j - 1) * 4 + c]
        return got[72 + (j - 2) * 4 + c]

    cs = (consts[0], consts[1], consts[2])
    for p in (2, 3):
        def row(j, carry, p=p):
            w = row_weights(weights, p, j, 8)
            at = region(p, j)
            pushed = []
            for c in range(4):
                pushed.append(part[at, c] + (w[1] * field(1, j, c) if p == 2 else w[0] * field(4, j, c)))
            z = solve(pushed, w[6], (inv[at, 0], inv[at, 1]), cs)
            for c in range(4):
                zed[at, c] = z[c]
            return carry
        rows(1, 19, row)
    for p in (1, 4):
        def row(j, carry, p=p):
            w = row_weights(weights, p, j, 8)
            v = [field(p, j, c) for c in range(4)]
            wanted = [(tnear if p == 1 else tfar)[136 + (j - 2) * 2 + n] for n in range(2)]
            at = region(p, j)
            pushed = []
            for c, k in enumerate(kept_parts(v, wanted, w[7], consts)):
                side[at - 36, c] = k
                around = (field(p + 1, j, c), field(p - 1, j, c), field(p, j + 1, c), field(p, j - 1, c))
                pushed.append(k + spread_sum(v[c], around, w))
            z = solve(pushed, w[6], (inv[at, 0], inv[at, 1]), cs)
            for c in range(4):
                zed[at, c] = z[c]
            return carry
        rows(2, 18, row)

    for p in (2, 3):
        def row(j, carry, p=p):
            w = row_weights(weights, p, j, 8)
            at = region(p, j)
            pushed = []
            for c in range(4):
                around = (zed[region(p + 1, j), c], zed[region(p - 1, j), c], zed[at + 1, c], zed[at - 1, c])
                pushed.append(kept[at, c] + spread_sum(zed[at, c], around, w))
            z = solve(pushed, w[6], (inv[at, 0], inv[at, 1]), cs)
            for c in range(4):
                it[p - 2, j - 2, c] = z[c]
            return carry
        rows(2, 18, row)
    out_near[0:14] = it[0, 1:15]
    out_near[14:26] = it[1, 2:14]
    out_far[0:14] = it[1, 1:15]
    out_far[14:26] = it[0, 2:14]


def sweep_body(it, near, far, kept, side, part, weights, consts, inv, zed, put):
    def guess(p, j, c):
        if p == 2 or p == 3:
            return it[p - 2, j - 2, c]
        side = near if p < 2 else far
        if p == 1 or p == 4:
            return side[j - 3, c]
        return side[14 + j - 4, c]

    def at2(p, j):
        if p == 2 or p == 3:
            return (p - 2) * 14 + j - 3
        return (28 if p == 1 else 40) + j - 4

    cs = (consts[0], consts[1], consts[2])
    for p, lo, hi in ((2, 3, 17), (3, 3, 17), (1, 4, 16), (4, 4, 16)):
        def row(j, carry, p=p):
            w = row_weights(weights, p, j, 8)
            at = region(p, j)
            pushed = []
            for c in range(4):
                if p == 2 or p == 3:
                    beside = w[1] * guess(1, j, c) if p == 2 else w[0] * guess(4, j, c)
                    pushed.append(part[at2(p, j), c] + beside)
                    continue
                around = (guess(p + 1, j, c), guess(p - 1, j, c), guess(p, j + 1, c), guess(p, j - 1, c))
                pushed.append(side[at - 36, c] + spread_sum(guess(p, j, c), around, w))
            z = solve(pushed, w[6], (inv[at, 0], inv[at, 1]), cs)
            for c in range(4):
                zed[at2(p, j), c] = z[c]
            return carry
        rows(lo, hi, row)
    for p in (2, 3):
        def row(j, carry, p=p):
            w = row_weights(weights, p, j, 8)
            at = region(p, j)
            here = at2(p, j)
            pushed = []
            for c in range(4):
                around = (zed[at2(p + 1, j), c], zed[at2(p - 1, j), c], zed[here + 1, c], zed[here - 1, c])
                pushed.append(kept[at, c] + spread_sum(zed[here, c], around, w))
            z = solve(pushed, w[6], (inv[at, 0], inv[at, 1]), cs)
            for c in range(4):
                put(p - 2, j - 4, c, z[c])
            return carry
        rows(4, 16, row)


def middle_body(far, near, it, kept, side, part, weights, consts, inv, new, out_near, out_far, send0, send1, zed):
    def put(x, j, c, v):
        new[x, j, c] = v
        first, second = (out_near, out_far) if x == 0 else (out_far, out_near)
        first[j, c] = v
        second[OWN + j, c] = v
    sweep_body(far=far, near=near, it=it, kept=kept, side=side, part=part, weights=weights, consts=consts, inv=inv, zed=zed, put=put)
    odd = place()[0] & 1
    for x in range(2):
        send0[x] = new[x, pl.ds((OWN - HALO) * (1 - odd), HALO)]
        send1[x] = new[x, pl.ds((OWN - HALO) * odd, HALO)]


def edges_body(far, near, row1, row0, new, own, send0, send1):
    odd = place()[0] & 1
    for x in range(2):
        own[x, HALO : HALO + OWN] = new[x]
    for row, send, high in ((row0, send0, 1 - odd), (row1, send1, odd)):
        for x in range(2):
            own[x, pl.ds(16 * high, HALO)] = row[x]
        for i, side in enumerate((near, far)):
            send[3 * i : 3 * i + 3] = side[pl.ds((OWN - 3) * high, 3)]
            send[6 + 2 * i : 8 + 2 * i] = side[pl.ds(OWN + (OWN - 2) * high, 2)]


def widen_body(edge1, edge0, near_x, far_x, near, far):
    odd = place()[0] & 1
    for out, got in ((near, near_x), (far, far_x)):
        out[3 : 3 + OWN] = got[0:OWN]
        out[20 : 20 + OWN] = got[OWN : 2 * OWN]
    for edge, high in ((edge0, 1 - odd), (edge1, odd)):
        for i, side in enumerate((near, far)):
            side[pl.ds(15 * high, 3)] = edge[3 * i : 3 * i + 3]
            side[pl.ds(18 + 14 * high, 2)] = edge[6 + 2 * i : 8 + 2 * i]


def last_body(far, near, it, kept, side, part, weights, consts, inv, back, *rest):
    outs, (zed, fin, stage) = rest[:2], rest[2:]
    def put(x, j, c, v):
        fin[x * OWN + j, c] = v
    sweep_body(far=far, near=near, it=it, kept=kept, side=side, part=part, weights=weights, consts=consts, inv=inv, zed=zed, put=put)
    t, _ = place()
    matrix = back[...]
    for low in range(0, 2 * OWN, 4):
        done = transform(matrix, fin[low : low + 4].reshape(128, 128))
        for i in range(4):
            x, j = divmod(low + i, OWN)
            for c in range(4):
                stage[pl.ds((c * 2 + x) * OWN + j, 8, stride=8 * OWN), :] = done[(i * 4 + c) * 8 : (i * 4 + c + 1) * 8]
    for k in range(8):
        outs[k & 1][k >> 1] = stage[pl.ds(pl.multiple_of((t ^ k) * 8 * OWN, 8), 8 * OWN), :]


def merge_body(other, mine, *outs):
    for out, k in zip(outs, CHIPS):
        out[0] = mine[k]
        out[1] = other[k]


def unpack_body(a, b, c, other, mine, state, adjoint, stage, held, sems):
    t, s = place()
    flip = s & 1
    for ref, k in zip((a, b, c), CHIPS):
        stage[t ^ (2 * k)] = ref[0]
        stage[t ^ (2 * k + 1)] = ref[1]
    stage[t] = mine[0]
    stage[t ^ 1] = other[0]
    copies = []
    for f, ref in enumerate((state, adjoint)):
        for n in range(2):
            for x in range(2):
                base = ((f * 2 + n) * 2 + x) * OWN
                for d in range(8):
                    held[f, n, x, OWN * d : OWN * (d + 1), :] = stage[d, base : base + OWN, :]
                copies.append(
                    pltpu.make_async_copy(held.at[f, n, x], ref.at[n, x ^ flip], sems.at[(f * 2 + n) * 2 + x])
                )
                copies[-1].start()
    for copy in copies:
        copy.wait()


def exchange(pieces):
    count = lax.axis_size("tm")
    return [lax.ppermute(pieces[k], "tm", [(i, i ^ k) for i in range(count)]) for k in ORDER] + [pieces[0]]


def swap_rows(block, start):
    count = lax.axis_size("tm")
    route = []
    for i in range(start, start + count, 2):
        low, high = i % count, (i + 1) % count
        route += [(low, high), (high, low)]
    return lax.ppermute(block, "tm", route)


def swap_planes(block, start):
    sections, slabs = lax.axis_size("tm"), lax.axis_size("space")
    route = []
    for t in range(sections):
        for s in range(slabs):
            pair = s + 1 if (s - start) % 2 == 0 else s - 1
            to = t * slabs + pair if 0 <= pair < slabs else (t ^ 1) * slabs + s
            route.append((t * slabs + s, to))
    return lax.ppermute(block, ("tm", "space"), route)


def on_device(state_guess, adjoint_guess, target, initial_state, diffusivity):
    forward, back = (jnp.asarray(m) for m in transform_matrices())
    consts = jnp.asarray(mode_constants())

    arguments = (state_guess, adjoint_guess, target, diffusivity, initial_state, forward, back, consts)
    *pieces, near_c, far_c, here_c, forward, back, consts = call(
        pack_body,
        "pack",
        [whole(PIECE, 128)] * 8 + [whole(3, TALL, 128)] * 2 + [whole(4, TALL, 128)]
        + [whole(128, 128)] * 2 + [whole(10, 8, 128)],
        0,
        [pltpu.VMEM((8, PIECE, 128), jnp.float32)]
        + [pltpu.VMEM((2, 2, 96, 128), jnp.float32)] * 3
        + [pltpu.VMEM((2, 96, 128), jnp.float32)] * 2
        + [pltpu.SemaphoreType.DMA((11,))],
        far_inputs=8,
    )(*(pltpu.with_memory_space_constraint(a, pltpu.HBM) for a in arguments))
    got = exchange(pieces)
    own, wish, near, far = call(
        spread_body,
        "spread",
        [whole(2, WIN, 4, 8, 128), whole(2, 18, 2, 8, 128), whole(177, 8, 128), whole(177, 8, 128)],
        11,
        [pltpu.VMEM((8 * PIECE, 128), jnp.float32)],
    )(*got, near_c, far_c, forward)
    coefficients = call(
        coefficient_body, "coefficients", [whole(4 * TALL * 8, 128), whole(68, 2, 8, 128)], 4
    )
    slab_weights = coefficients(far, near, here_c, consts)[0].reshape(4 * TALL, 8, 128)
    far = far_first = swap_planes(far, 0)
    near = near_first = swap_planes(near, 1)
    weights, inv = coefficients(far, near, here_c, consts)
    weights = weights.reshape(4 * TALL, 8, 128)

    sweep_scratch = [pltpu.VMEM((52, 4, 8, 128), jnp.float32)]
    for outer in range(OUTER):
        kept, part = call(prepare_body, "prepare", [whole(36, 4, 8, 128)] * 2, 4)(own, wish, slab_weights, consts)
        side, it, near_z, far_z = call(
            front_body,
            "front",
            [whole(32, 4, 8, 128), whole(2, 16, 4, 8, 128), whole(26, 4, 8, 128), whole(26, 4, 8, 128)],
            10,
            [pltpu.VMEM((68, 4, 8, 128), jnp.float32)],
        )(far, near, own, near_first, far_first, weights, consts, inv, kept, part)
        ahead = call(ahead_body, "ahead", [whole(28, 4, 8, 128)], 3)(it, kept, weights)[0]
        far_z = swap_planes(far_z, 0)
        near_z = swap_planes(near_z, 1)
        if outer < OUTER - 1:
            new, near, far, row0, row1 = call(
                middle_body,
                "middle",
                [whole(2, OWN, 4, 8, 128)] + [whole(2 * OWN, 4, 8, 128)] * 2 + [whole(2, HALO, 4, 8, 128)] * 2,
                9,
                sweep_scratch,
            )(far_z, near_z, it, kept, side, ahead, weights, consts, inv)
            far = swap_planes(far, 0)
            near = swap_planes(near, 1)
            row1 = swap_rows(row1, 1)
            row0 = swap_rows(row0, 0)
            own, edge0, edge1 = call(
                edges_body, "edges", [whole(2, WIN, 4, 8, 128)] + [whole(10, 4, 8, 128)] * 2, 5
            )(far, near, row1, row0, new)
            edge1 = swap_rows(edge1, 1)
            edge0 = swap_rows(edge0, 0)
            near, far = call(widen_body, "widen", [whole(34, 4, 8, 128)] * 2, 4)(edge1, edge0, near, far)
            near = near.reshape(136, 8, 128)
            far = far.reshape(136, 8, 128)
    mine, other = call(
        last_body,
        "last",
        [whole(4, 8 * OWN, 128)] * 2,
        10,
        sweep_scratch + [pltpu.VMEM((2 * OWN, 4, 8, 128), jnp.float32), pltpu.VMEM((64 * OWN, 128), jnp.float32)],
    )(far_z, near_z, it, kept, side, ahead, weights, consts, inv, back)
    other = swap_rows(other, 0)
    pairs = call(merge_body, "merge", [whole(2, 8 * OWN, 128)] * 3, 2)(other, mine)
    count = lax.axis_size("tm")
    got = [
        lax.ppermute(pair, "tm", [(i, i ^ (2 * k)) for i in range(count)]) for pair, k in zip(pairs, CHIPS)
    ]
    return tuple(
        call(
            unpack_body,
            "unpack",
            [whole(2, 2, 96, 128)] * 2,
            5,
            [
                pltpu.VMEM((8, 8 * OWN, 128), jnp.float32),
                pltpu.VMEM((2, 2, 2, 96, 128), jnp.float32),
                pltpu.SemaphoreType.DMA((8,)),
            ],
            far_outputs=True,
        )(*got, other, mine)
    )


def solution(mesh):
    in_specs = (
        P("tm", "space", None, None),
        P("tm", "space", None, None),
        P("tm", "space", None, None),
        P("space", None, None),
        P("space", None, None),
    )
    out_specs = (P("tm", "space", None, None), P("tm", "space", None, None))
    return jax.shard_map(
        on_device, mesh=mesh, in_specs=in_specs, out_specs=out_specs, check_vma=False
    )
```
